512 devices in a mesh: grp: 8 (over z), mem: 64 (over y, x, core).
Axes of the slice: x: 4, y: 8, z: 8, core: 2. Of those that a mesh axis runs over, the one named last changes fastest.
Arguments:
- phi_owned: float32 [8, 8, 8, 65536], P(None, None, None, ('grp', 'mem')), may hold values from -6 to 6
- band_counts: int32 [8, 64], P('grp'), may hold values from 1 to 128, 2048 in all within a row
- neighbours: int32 [8, 6, 2048], P('grp'), may hold values from -1 to 16383, as said below
Outputs:
- phi_new: float32 [8, 8, 8, 65536], P(None, None, None, ('grp', 'mem'))
The draws below stay inside these ranges and needn't reach their ends.
Inputs may be any that keep to these rules, and one draw needn't show every extreme that they name: `band_counts`: in every group the counts sum to 2048, each is at least 1, and the largest is exactly 128. `neighbours`: tile k of a group lies at column k mod 64 and row k // 64 of the group's tile sheet. An entry is -1 (no neighbour) or the id of the tile across that face: tile k - 1, k + 1, k - 64, k + 64 of the same group for faces 0 to 3 (never across an edge of the sheet), tile k of group g - 1 or g + 1 for faces 4 and 5. Links are mutual.
All inputs are finite; a program needn't handle non-finite values.
Results may differ from the reference program's by a relative error of at most 0.0003.
Values sent between devices are 32-bit elements; how exact they have to be, the bound alone decides.
No kernel may reach another device: no remote copies, remote signals or barrier semaphores. Data moves between devices by JAX's collectives and lax.ppermute only.
A program may use at most 64 MiB of HBM per device.

```python
import math
import jax
import jax.numpy as jnp
import numpy as np
from jax import lax

TILE = 8
STEPS = 4
HOLD_DEV = 32
OWN_DEV = 128
COLUMNS = 64
GROUPS = 8
GROUP_TILES = 2048
SLOTS = 65536


def draw_neighbours(key, part):
    tile_count = GROUP_TILES
    tile_ids = jnp.arange(tile_count, dtype=jnp.int32)
    column = tile_ids % COLUMNS
    sheet_row = tile_ids // COLUMNS
    group_index = jnp.arange(GROUPS, dtype=jnp.int32)[:, None]
    subkeys = jax.random.split(jax.random.fold_in(key, 7), 3)
    link_x = jax.random.randint(subkeys[0], (GROUPS, tile_count), 0, 4) < 3
    link_y = jax.random.randint(subkeys[1], (GROUPS, tile_count), 0, 4) < 3
    link_z = jax.random.randint(subkeys[2], (GROUPS, tile_count), 0, 4) < 3
    group_base = group_index * tile_count
    present = [(column > 0) & jnp.roll(link_x, 1, axis=1), (column < COLUMNS - 1) & link_x, (sheet_row > 0) & jnp.roll(link_y, COLUMNS, axis=1), (sheet_row < HOLD_DEV - 1) & link_y, (group_index > 0) & jnp.roll(link_z, 1, axis=0), (group_index < GROUPS - 1) & link_z]
    targets = [group_base + tile_ids - 1, group_base + tile_ids + 1, group_base + tile_ids - COLUMNS, group_base + tile_ids + COLUMNS, group_base - tile_count + tile_ids, group_base + tile_count + tile_ids]
    stacked = [jnp.where(linked, target, -1) for linked, target in zip(present, targets)]
    return jnp.stack(stacked, axis=1).astype(jnp.int32)


def block_scale(key, dims, cuts, smallest, high):
    level = 1.0
    for position, shards_of in cuts:
        heights = jax.random.uniform(jax.random.fold_in(jax.random.fold_in(key, 6), position), (shards_of,), jnp.float32, smallest / len(cuts), high / len(cuts))
        level = level * jnp.repeat(jnp.exp(heights), dims[position] // shards_of).reshape((-1,) + (1,) * (len(dims) - 1 - position))
    return level


def length_profile(amount, total, limit, lean):
    weights = [(1 << 20) // math.isqrt(grade ** lean) + 1 for grade in range(2, amount + 1)]
    spare, holding = total - limit - (amount - 1), [1] * (amount - 1)
    while spare > 0:
        movable = [i for i in range(amount - 1) if holding[i] < limit]
        mass, budget = sum([weights[i] for i in movable]), spare
        for i in movable:
            addition = min(limit - holding[i], max(1, budget * weights[i] // mass), spare)
            holding[i] = holding[i] + addition
            spare = spare - addition
    return np.array([limit] + holding)


def ragged_sizes(key, amount, total, bound, slope):
    if amount == 2:
        one = jax.random.randint(key, (), max(1, total - bound), min(bound, total - 1) + 1)
        return jnp.stack([one, total - one])
    sizes = jnp.asarray(length_profile(amount, total, bound, slope), jnp.int32)
    pairs = (amount - 1) // 2
    giver, sink = sizes[1:1 + 2 * pairs:2], sizes[2:2 + 2 * pairs:2]
    slack = jnp.minimum(giver - 1, bound - sink)
    passed = jax.random.randint(jax.random.fold_in(key, 1), (pairs,), 0, 1 << 20) % (slack + 1)
    sizes = sizes.at[1:1 + 2 * pairs:2].set(giver - passed).at[2:2 + 2 * pairs:2].set(sink + passed)
    return sizes[jax.random.permutation(jax.random.fold_in(key, 2), amount)]


def gaussian(rng, dims, spread, limit, shards=(), kind=jnp.bfloat16):
    values = jax.random.normal(rng, dims, jnp.float32) * spread
    if len(shards) > 0:
        values = block_scale(rng, dims, shards, -0.22, 0.18) * values
    return jnp.clip(values, min=-limit, max=limit).astype(kind)


def setup_inputs(seed: int = 0) -> dict:
    arg_keys = jax.random.split(jax.random.key(seed), 4)
    phi_owned = gaussian(arg_keys[0], (TILE, TILE, TILE, SLOTS), 1.0, 6.0, ((3, 512),), jnp.float32)
    band_counts = jax.vmap(lambda own: ragged_sizes(own, COLUMNS, GROUP_TILES, OWN_DEV, 2))(jax.random.split(arg_keys[1], GROUPS)).reshape((GROUPS, COLUMNS)).astype(jnp.int32)
    neighbours = draw_neighbours(jax.random.fold_in(arg_keys[3], 71), 0)
    return {"phi_owned": phi_owned, "band_counts": band_counts, "neighbours": neighbours}


TIME_STEP = 0.5
EPSILON = 1e-06

def upwind(backward, forward, positive):
    rising = jnp.maximum(jnp.square(jnp.maximum(backward, 0.0)), jnp.square(jnp.minimum(forward, 0.0)))
    falling = jnp.maximum(jnp.square(jnp.minimum(backward, 0.0)), jnp.square(jnp.maximum(forward, 0.0)))
    return jnp.where(positive, rising, falling)

def reference(phi_owned, band_counts, neighbours):
    tile_edge = phi_owned.shape[0]
    groups, columns = band_counts.shape
    tile_total = neighbours.shape[2]
    own_slots = phi_owned.shape[3] // (groups * columns)
    counts = band_counts.astype(jnp.int32)
    starts = (jnp.cumsum(counts, axis=1) - counts).astype(jnp.int32)
    tile_ids = jnp.arange(tile_total, dtype=jnp.int32)
    owner_mask = (starts[:, None, :] <= tile_ids[None, :, None]).astype(jnp.int32)
    owner_of = (lax.optimization_barrier(jnp.sum(owner_mask, axis=2)) - 1).astype(jnp.int32)
    first_tile = jnp.take_along_axis(starts, owner_of, axis=1).astype(jnp.int32)
    group_ids = jnp.arange(groups, dtype=jnp.int32)[:, None]
    slot_index = ((group_ids * columns + owner_of) * own_slots + tile_ids[None, :] - first_tile).reshape(-1).astype(jnp.int32)
    level_set = jnp.take(phi_owned, slot_index, axis=3)
    sign_field = level_set / jnp.sqrt(level_set * level_set + 1.0)
    positive = sign_field > 0
    link_table = jnp.transpose(neighbours, (1, 0, 2)).reshape(6, groups * tile_total)
    present = link_table >= 0
    safe_ids = jnp.maximum(link_table, 0).astype(jnp.int32)
    for sweep in range(STEPS):
        squares = jnp.zeros_like(level_set)
        for direction in range(3):
            low_layer = lax.index_in_dim(level_set, 0, direction, keepdims=True)
            high_layer = lax.index_in_dim(level_set, tile_edge - 1, direction, keepdims=True)
            below = jnp.where(present[2 * direction], jnp.take(high_layer, safe_ids[2 * direction], axis=3), low_layer)
            above = jnp.where(present[2 * direction + 1], jnp.take(low_layer, safe_ids[2 * direction + 1], axis=3), high_layer)
            extended = jnp.concatenate([below, level_set, above], axis=direction)
            backward = level_set - lax.slice_in_dim(extended, 0, tile_edge, axis=direction)
            forward = lax.slice_in_dim(extended, 2, tile_edge + 2, axis=direction) - level_set
            squares = squares + upwind(backward, forward, positive)
        level_set = level_set - TIME_STEP * sign_field * (jnp.sqrt(squares + EPSILON) - 1.0)
    return jnp.zeros_like(phi_owned).at[:, :, :, slot_index].set(level_set)
```

```python
import functools

import jax
import jax.numpy as jnp
from jax import lax
from jax.experimental import pallas as pl
from jax.experimental.pallas import tpu as pltpu
from jax.sharding import PartitionSpec as P

STEPS = 4
TIME_STEP = 0.5
EPSILON = 1e-06

TILE = 8
ROWS = 32
COLUMNS = 64
SLOTS = 128
CELLS = TILE**3
DEPTH = SLOTS // COLUMNS
WIDE = 16
TABLE = 40

F32 = jnp.float32
I32 = jnp.int32


def shift(x, amount, axis):
    return pltpu.roll(x, amount % x.shape[axis] if isinstance(amount, int) else amount, axis)


def iota(shape, axis):
    return lax.broadcasted_iota(I32, shape, axis)


def own_start(counts_ref, me):
    total = jnp.int32(0)
    for owner in range(COLUMNS - 1):
        total = total + jnp.where(owner < me, counts_ref[0, owner], 0)
    return total


def pack_kernel(where_am_i, *refs):
    counts_ref, phi_ref, out_ref = refs[-3:]
    turn = own_start(counts_ref, where_am_i(refs)) & (COLUMNS - 1)
    low_half = iota((TILE, SLOTS), 0) < TILE // 2
    for z in range(TILE):
        blocks = []
        for y in range(TILE):
            tiles = phi_ref[pl.ds(y * TILE + z, TILE, stride=TILE * TILE), :]
            here = pltpu.roll(tiles, turn, 1)
            left = shift(here, 1, 1)
            right = shift(here, -1, 1)
            blocks.append(shift(jnp.where(low_half, here, left), 4, 0))
            blocks.append(shift(jnp.where(low_half, right, here), 4, 0))
        turned = jnp.concatenate(blocks, axis=0).T
        for d in range(DEPTH):
            out_ref[pl.ds(d * TILE + z, COLUMNS, stride=DEPTH * TILE), :] = turned[
                d * COLUMNS : (d + 1) * COLUMNS
            ]


def mask_kernel(where_am_i, *refs):
    links_ref, out_ref, lhs_ref, found_ref = refs[-4:]
    me = where_am_i(refs)
    pairs = ROWS // 2
    for v in range(pairs):
        lhs_ref[v * 8 : v * 8 + 6, :] = jnp.where(
            links_ref[0, :, v * 128 : (v + 1) * 128] >= 0, 1.0, 0.0
        )
        lhs_ref[v * 8 + 6 : v * 8 + 8, :] = jnp.zeros((2, 128), F32)
    source = iota((128, 256), 0)
    target = iota((128, 256), 1)
    x16 = target % WIDE
    column = me + jnp.where(x16 < 4, -1, jnp.where(x16 >= 12, 1, 0))
    pick = (source % COLUMNS == column) & (source // COLUMNS == target // 128)
    found = jnp.dot(
        lhs_ref[...].astype(jnp.bfloat16),
        jnp.where(pick, 1.0, 0.0).astype(jnp.bfloat16),
        preferred_element_type=F32,
    )
    for v in range(pairs):
        for half in range(2):
            found_ref[pl.ds(2 * v + half, 8, stride=ROWS), :] = found[
                v * 8 : v * 8 + 8, half * 128 : (half + 1) * 128
            ]
    lane = iota((ROWS, 128), 1)
    x16 = lane % WIDE
    out_ref[0] = jnp.where((x16 == 3) | (x16 == 11), found_ref[ROWS : 2 * ROWS, :], 1.0)
    out_ref[1] = jnp.where(lane >= 112, found_ref[3 * ROWS : 4 * ROWS, :], 1.0)
    out_ref[2] = found_ref[4 * ROWS : 5 * ROWS, :]
    out_ref[3] = found_ref[5 * ROWS : 6 * ROWS, :]


def fill_table(counts_ref, table_ref, column):
    for entry in range(3):
        table_ref[entry, 1] = jnp.int32(0)
        table_ref[entry, ROWS] = jnp.int32(0)

    def body(owner, start):
        turn = start & (COLUMNS - 1)
        for entry in range(3):
            delta = entry - 1
            first = (column + delta - turn) & (COLUMNS - 1)
            row = (start + first - delta) >> 6
            slot = ((first + turn - delta) & (SLOTS - 1)) >> 6
            table_ref[entry, row + 1] = owner * DEPTH + slot
            table_ref[entry, row + 2] = owner * DEPTH + (1 - slot)
        return start + counts_ref[0, owner]

    lax.fori_loop(0, COLUMNS, body, jnp.int32(0), unroll=8)


def unpack_kernel(where_am_i, *refs):
    counts_ref, received_ref, masks_ref, low_ref, high_ref, table_out_ref, table_ref, tiles_ref = refs[-8:]
    fill_table(counts_ref, table_ref, where_am_i(refs))
    x16 = iota((TILE, 128), 1) % WIDE
    for r in range(ROWS):
        left = received_ref[table_ref[0, r + 1]]
        here = received_ref[table_ref[1, r + 1]]
        right = received_ref[table_ref[2, r + 1]]
        tile = jnp.where(x16 < 4, left, jnp.where(x16 >= 12, right, here))
        tiles_ref[pl.ds(r, TILE, stride=ROWS), :] = tile
        table_out_ref[0, r] = table_ref[1, r + 1]
    half = TILE // 2
    for z in range(half):
        low_ref[z] = tiles_ref[z * ROWS : (z + 1) * ROWS, :]
        high_ref[z] = tiles_ref[(z + half) * ROWS : (z + half + 1) * ROWS, :]
    for i in range(2):
        low_ref[half + i] = masks_ref[i]
        high_ref[half + i] = masks_ref[i]


def march_kernel(*refs):
    (
        table_ref,
        below_ref,
        low_ref,
        high_ref,
        above_ref,
        masks_ref,
        out_ref,
        even_ref,
        odd_ref,
        sign_ref,
        done_ref,
    ) = refs
    half = TILE // 2
    lane = iota((ROWS, 128), 1)
    first_y = lane < WIDE
    last_y = lane >= 128 - WIDE
    sources = (below_ref, low_ref, high_ref, above_ref)
    for z in range(1, 2 * TILE - 1):
        level = sources[z // half][z % half]
        sign_ref[z] = level / jnp.sqrt(level * level + 1.0)

    def load(step, z):
        if step == 0:
            return sources[z // half][z % half]
        return (odd_ref if step % 2 else even_ref)[z]

    for step in range(STEPS):
        target_ref = even_ref if step % 2 else odd_ref
        level = load(step, step)
        after = load(step, step + 1)
        ahead_z = after - level
        if step == 3:
            ahead_z = ahead_z * masks_ref[2]
        for z in range(step + 1, 2 * TILE - 1 - step):
            back_z = ahead_z
            level = after
            after = load(step, z + 1)
            ahead_z = after - level
            if z == 3:
                ahead_z = ahead_z * masks_ref[2]
            if z == 11:
                ahead_z = ahead_z * masks_ref[3]
            links = (below_ref, low_ref, low_ref, above_ref)[z // half]
            sign_field = sign_ref[z]
            up = jnp.where(sign_field > 0, 1.0, -1.0)
            down = -up
            squares = None
            ahead = (shift(level, -1, 1) - level) * links[half]
            back = shift(ahead, 1, 1)
            squares = jnp.square(jnp.maximum(jnp.maximum(up * back, down * ahead), 0.0))
            beyond = jnp.where(first_y, shift(level, -1, 0), level)
            ahead = (shift(beyond, -WIDE, 1) - level) * links[half + 1]
            back = shift(jnp.where(last_y, shift(ahead, 1, 0), ahead), WIDE, 1)
            squares = squares + jnp.square(
                jnp.maximum(jnp.maximum(up * back, down * ahead), 0.0)
            )
            squares = squares + jnp.square(
                jnp.maximum(jnp.maximum(up * back_z, down * ahead_z), 0.0)
            )
            target_ref[z] = level - TIME_STEP * sign_field * (jnp.sqrt(squares + EPSILON) - 1.0)
    final_ref = even_ref
    left_half = lane % WIDE < TILE
    for q in range(half):
        done_ref[q * ROWS : (q + 1) * ROWS, :] = jnp.where(
            left_half, shift(final_ref[half + q], -4, 1), shift(final_ref[2 * half + q], 4, 1)
        )
    for r in range(ROWS):
        out_ref[table_ref[0, r]] = done_ref[pl.ds(r, half, stride=ROWS), :]


def deliver_kernel(where_am_i, *refs):
    counts_ref, returned_ref, out_ref = refs[-3:]
    me = where_am_i(refs)
    turn = own_start(counts_ref, me) & (COLUMNS - 1)
    live = iota((SLOTS, SLOTS), 1) < counts_ref[0, me]
    half = TILE // 2
    for q in range(half):
        rows = [
            returned_ref[pl.ds(d * half + q, COLUMNS, stride=DEPTH * half), :] for d in range(DEPTH)
        ]
        turned = jnp.concatenate(rows, axis=0).T
        turned = pltpu.roll(turned, (SLOTS - turn) & (SLOTS - 1), 1)
        turned = jnp.where(live, turned, 0.0)
        for y in range(TILE):
            for upper in range(2):
                row = y * WIDE + upper * TILE
                out_ref[pl.ds(y * TILE + q + upper * half, TILE, stride=TILE * TILE), :] = turned[
                    row : row + TILE
                ]


def spec(space=pltpu.VMEM):
    return pl.BlockSpec(memory_space=space)


def run(kernel, operands, shapes, scratch, me=None, spaces=None, out_spaces=None, cost=(0, 0)):
    spaces = spaces or [pltpu.VMEM] * len(operands)
    out_spaces = out_spaces or [pltpu.VMEM] * len(shapes)
    if me is not None:
        operands = (me, *operands)
        spaces = [pltpu.SMEM, *spaces]
    out = pl.pallas_call(
        kernel,
        out_shape=[jax.ShapeDtypeStruct(s, t) for s, t in shapes],
        in_specs=[spec(s) for s in spaces],
        out_specs=[spec(s) for s in out_spaces],
        scratch_shapes=scratch,
        compiler_params=pltpu.CompilerParams(vmem_limit_bytes=32 << 20),
        cost_estimate=pl.CostEstimate(flops=cost[0], bytes_accessed=cost[1], transcendentals=0),
        name=getattr(kernel, "func", kernel).__name__,
    )(*operands)
    return out


def position(refs):
    return lax.axis_index("mem")


def given(refs):
    return refs[0][0]


def bind(kernel, me):
    return functools.partial(kernel, position if me is None else given)


def pack(counts, phi, me=None):
    (out,) = run(
        bind(pack_kernel, me),
        (counts, phi.reshape(CELLS, SLOTS)),
        [((COLUMNS * DEPTH * TILE, 128), F32)],
        [],
        me,
        [pltpu.SMEM, pltpu.VMEM],
    )
    return out.reshape(COLUMNS, DEPTH * TILE, 128)


def masks_of(neighbours, me=None):
    (out,) = run(
        bind(mask_kernel, me),
        (neighbours,),
        [((4, ROWS, 128), F32)],
        [pltpu.VMEM((128, 128), F32), pltpu.VMEM((8 * ROWS, 128), F32)],
        me,
        cost=(1 << 22, 1 << 17),
    )
    return out


def unpack(counts, received, masks, me=None):
    half = TILE // 2
    return run(
        bind(unpack_kernel, me),
        (counts, received.reshape(COLUMNS * DEPTH, TILE, 128), masks),
        [((half + 2, ROWS, 128), F32), ((half + 2, ROWS, 128), F32), ((1, ROWS), I32)],
        [pltpu.SMEM((3, TABLE), I32), pltpu.VMEM((TILE * ROWS, 128), F32)],
        me,
        [pltpu.SMEM, pltpu.VMEM, pltpu.VMEM],
        [pltpu.VMEM, pltpu.VMEM, pltpu.SMEM],
    )


def march(table, below, low, high, above, masks):
    half = TILE // 2
    (out,) = run(
        march_kernel,
        (table, below, low, high, above, masks),
        [((COLUMNS * DEPTH, half, 128), F32)],
        [pltpu.VMEM((2 * TILE, ROWS, 128), F32)] * 3 + [pltpu.VMEM((half * ROWS, 128), F32)],
        None,
        [pltpu.SMEM] + [pltpu.VMEM] * 5,
    )
    return out.reshape(COLUMNS, DEPTH * half, 128)


def deliver(counts, returned, me=None):
    (out,) = run(
        bind(deliver_kernel, me),
        (counts, returned.reshape(COLUMNS * TILE, 128)),
        [((CELLS, SLOTS), F32)],
        [],
        me,
        [pltpu.SMEM, pltpu.VMEM],
    )
    return out.reshape(TILE, TILE, TILE, SLOTS)


def exchange(x):
    return lax.all_to_all(x, "mem", split_axis=0, concat_axis=0, tiled=True)


def on_device(phi_owned, band_counts, neighbours):
    received = exchange(pack(band_counts, phi_owned))
    masks = masks_of(neighbours)
    low, high, table = unpack(band_counts, received, masks)
    groups = lax.axis_size("grp")
    rising = [(g, g + 1) for g in range(groups - 1)]
    falling = [(g + 1, g) for g in range(groups - 1)]
    below = lax.ppermute(high, "grp", rising)
    above = lax.ppermute(low, "grp", falling)
    returned = exchange(march(table, below, low, high, above, masks))
    return deliver(band_counts, returned)


def solution(mesh):
    return jax.shard_map(
        on_device,
        mesh=mesh,
        in_specs=(P(None, None, None, ("grp", "mem")), P("grp", None), P("grp", None, None)),
        out_specs=P(None, None, None, ("grp", "mem")),
        check_vma=False,
    )
```

```python
import functools

import jax
import jax.numpy as jnp
from jax import lax
from jax.experimental import pallas as pl
from jax.experimental.pallas import tpu as pltpu
from jax.sharding import PartitionSpec as P

STEPS = 4
TIME_STEP = 0.5
EPSILON = 1e-06

TILE = 8
ROWS = 32
COLUMNS = 64
SLOTS = 128
CELLS = TILE**3
DEPTH = SLOTS // COLUMNS
WIDE = 16
TABLE = 40

F32 = jnp.float32
I32 = jnp.int32


def shift(x, amount, axis):
    return pltpu.roll(x, amount % x.shape[axis] if isinstance(amount, int) else amount, axis)


def iota(shape, axis):
    return lax.broadcasted_iota(I32, shape, axis)


def own_start(counts_ref, me):
    total = jnp.int32(0)
    for owner in range(COLUMNS - 1):
        total = total + jnp.where(owner < me, counts_ref[0, owner], 0)
    return total


def pack_kernel(where_am_i, *refs):
    counts_hbm, phi_hbm, out_ref, counts_ref, phi_ref, sems = refs[-6:]
    half = TILE // 2
    copies = [
        pltpu.make_async_copy(counts_hbm, counts_ref, sems.at[0]),
        pltpu.make_async_copy(phi_hbm.at[pl.ds(half, half)], phi_ref.at[pl.ds(0, half)], sems.at[1]),
        pltpu.make_async_copy(phi_hbm.at[pl.ds(0, half)], phi_ref.at[pl.ds(half, half)], sems.at[2]),
    ]
    for copy in copies:
        copy.start()
    copies[0].wait()
    turn = own_start(counts_ref, where_am_i(refs)) & (COLUMNS - 1)
    copies[1].wait()
    copies[2].wait()
    layers = phi_ref.reshape(CELLS, SLOTS)
    low_half = iota((TILE, SLOTS), 0) < half
    for z in range(TILE):
        blocks = []
        for y in range(TILE):
            tiles = layers[pl.ds(y * TILE + z, TILE, stride=TILE * TILE), :]
            here = pltpu.roll(tiles, turn, 1)
            left = shift(here, 1, 1)
            right = shift(here, -1, 1)
            blocks.append(jnp.where(low_half, left, here))
            blocks.append(jnp.where(low_half, here, right))
        turned = jnp.concatenate(blocks, axis=0).T
        for d in range(DEPTH):
            out_ref[pl.ds(d * TILE + z, COLUMNS, stride=DEPTH * TILE), :] = turned[
                d * COLUMNS : (d + 1) * COLUMNS
            ]


def mask_kernel(where_am_i, *refs):
    counts_ref, links_ref, out_ref, table_ref, lhs_ref, found_ref = refs[-6:]
    me = where_am_i(refs)
    fill_table(counts_ref, table_ref, me)
    pairs = ROWS // 2
    for v in range(pairs):
        lhs_ref[v * 8 : v * 8 + 6, :] = jnp.where(
            links_ref[0, :, v * 128 : (v + 1) * 128] >= 0, 1.0, 0.0
        )
        lhs_ref[v * 8 + 6 : v * 8 + 8, :] = jnp.zeros((2, 128), F32)
    source = iota((128, 256), 0)
    target = iota((128, 256), 1)
    x16 = target % WIDE
    column = me + jnp.where(x16 < 4, -1, jnp.where(x16 >= 12, 1, 0))
    pick = (source % COLUMNS == column) & (source // COLUMNS == target // 128)
    found = jnp.dot(
        lhs_ref[...].astype(jnp.bfloat16),
        jnp.where(pick, 1.0, 0.0).astype(jnp.bfloat16),
        preferred_element_type=F32,
    )
    for v in range(pairs):
        for half in range(2):
            found_ref[pl.ds(2 * v + half, 8, stride=ROWS), :] = found[
                v * 8 : v * 8 + 8, half * 128 : (half + 1) * 128
            ]
    lane = iota((ROWS, 128), 1)
    x16 = lane % WIDE
    out_ref[0] = jnp.where((x16 == 3) | (x16 == 11), found_ref[ROWS : 2 * ROWS, :], 1.0)
    out_ref[1] = jnp.where(lane >= 112, found_ref[3 * ROWS : 4 * ROWS, :], 1.0)
    out_ref[2] = found_ref[4 * ROWS : 5 * ROWS, :]
    out_ref[3] = found_ref[5 * ROWS : 6 * ROWS, :]


def fill_table(counts_ref, table_ref, column):
    for entry in range(3):
        table_ref[entry, 1] = jnp.int32(0)
        table_ref[entry, ROWS] = jnp.int32(0)

    def body(owner, start):
        turn = start & (COLUMNS - 1)
        for entry in range(3):
            delta = entry - 1
            first = (column + delta - turn) & (COLUMNS - 1)
            row = (start + first - delta) >> 6
            slot = ((first + turn - delta) & (SLOTS - 1)) >> 6
            table_ref[entry, row + 1] = owner * DEPTH + slot
            table_ref[entry, row + 2] = owner * DEPTH + (1 - slot)
        return start + counts_ref[0, owner]

    lax.fori_loop(0, COLUMNS, body, jnp.int32(0), unroll=8)


def unpack_kernel(*refs):
    table_ref, received_ref, masks_ref, low_ref, high_ref, tiles_ref = refs
    x16 = iota((TILE, 128), 1) % WIDE
    for r in range(ROWS):
        left = received_ref[table_ref[0, r + 1]]
        here = received_ref[table_ref[1, r + 1]]
        right = received_ref[table_ref[2, r + 1]]
        tile = jnp.where(x16 < 4, left, jnp.where(x16 >= 12, right, here))
        tiles_ref[pl.ds(r, TILE, stride=ROWS), :] = tile
    half = TILE // 2
    for z in range(half):
        low_ref[z] = tiles_ref[z * ROWS : (z + 1) * ROWS, :]
        high_ref[z] = tiles_ref[(z + half) * ROWS : (z + half + 1) * ROWS, :]
    for i in range(2):
        low_ref[half + i] = masks_ref[i]
        high_ref[half + i] = masks_ref[i]


def march_kernel(*refs):
    (
        table_ref,
        below_ref,
        low_ref,
        high_ref,
        above_ref,
        masks_ref,
        out_ref,
        even_ref,
        odd_ref,
        sign_ref,
        done_ref,
    ) = refs
    half = TILE // 2
    lane = iota((ROWS, 128), 1)
    first_y = lane < WIDE
    last_y = lane >= 128 - WIDE
    sources = (below_ref, low_ref, high_ref, above_ref)
    for z in range(1, 2 * TILE - 1):
        level = sources[z // half][z % half]
        sign_ref[z] = level / jnp.sqrt(level * level + 1.0)

    def load(step, z):
        if step == 0:
            return sources[z // half][z % half]
        return (odd_ref if step % 2 else even_ref)[z]

    for step in range(STEPS):
        target_ref = even_ref if step % 2 else odd_ref
        level = load(step, step)
        after = load(step, step + 1)
        ahead_z = after - level
        if step == 3:
            ahead_z = ahead_z * masks_ref[2]
        for z in range(step + 1, 2 * TILE - 1 - step):
            back_z = ahead_z
            level = after
            after = load(step, z + 1)
            ahead_z = after - level
            if z == 3:
                ahead_z = ahead_z * masks_ref[2]
            if z == 11:
                ahead_z = ahead_z * masks_ref[3]
            links = (below_ref, low_ref, low_ref, above_ref)[z // half]
            sign_field = sign_ref[z]
            up = jnp.where(sign_field > 0, 1.0, -1.0)
            down = -up
            squares = None
            ahead = (shift(level, -1, 1) - level) * links[half]
            back = shift(ahead, 1, 1)
            squares = jnp.square(jnp.maximum(jnp.maximum(up * back, down * ahead), 0.0))
            beyond = jnp.where(first_y, shift(level, -1, 0), level)
            ahead = (shift(beyond, -WIDE, 1) - level) * links[half + 1]
            back = shift(jnp.where(last_y, shift(ahead, 1, 0), ahead), WIDE, 1)
            squares = squares + jnp.square(
                jnp.maximum(jnp.maximum(up * back, down * ahead), 0.0)
            )
            squares = squares + jnp.square(
                jnp.maximum(jnp.maximum(up * back_z, down * ahead_z), 0.0)
            )
            target_ref[z] = level - TIME_STEP * sign_field * (jnp.sqrt(squares + EPSILON) - 1.0)
    final_ref = even_ref
    left_half = lane % WIDE < TILE
    for q in range(half):
        done_ref[q * ROWS : (q + 1) * ROWS, :] = jnp.where(
            left_half, shift(final_ref[half + q], -4, 1), shift(final_ref[2 * half + q], 4, 1)
        )
    for r in range(ROWS):
        out_ref[table_ref[1, r + 1]] = done_ref[pl.ds(r, half, stride=ROWS), :]


def deliver_kernel(where_am_i, *refs):
    counts_ref, returned_ref, out_ref = refs[-3:]
    me = where_am_i(refs)
    turn = own_start(counts_ref, me) & (COLUMNS - 1)
    live = iota((SLOTS, SLOTS), 1) < counts_ref[0, me]
    half = TILE // 2
    for q in range(half):
        rows = [
            returned_ref[pl.ds(d * half + q, COLUMNS, stride=DEPTH * half), :] for d in range(DEPTH)
        ]
        turned = jnp.concatenate(rows, axis=0).T
        turned = pltpu.roll(turned, (SLOTS - turn) & (SLOTS - 1), 1)
        turned = jnp.where(live, turned, 0.0)
        for y in range(TILE):
            for upper in range(2):
                row = y * WIDE + upper * TILE
                out_ref[pl.ds(y * TILE + q + upper * half, TILE, stride=TILE * TILE), :] = turned[
                    row : row + TILE
                ]


def spec(space=pltpu.VMEM):
    return pl.BlockSpec(memory_space=space)


def run(
    kernel, operands, shapes, scratch, me=None, spaces=None, out_spaces=None, cost=(0, 0), grant=32
):
    spaces = spaces or [pltpu.VMEM] * len(operands)
    out_spaces = out_spaces or [pltpu.VMEM] * len(shapes)
    if me is not None:
        operands = (me, *operands)
        spaces = [pltpu.SMEM, *spaces]
    out = pl.pallas_call(
        kernel,
        out_shape=[jax.ShapeDtypeStruct(s, t) for s, t in shapes],
        in_specs=[spec(s) for s in spaces],
        out_specs=[spec(s) for s in out_spaces],
        scratch_shapes=scratch,
        compiler_params=pltpu.CompilerParams(vmem_limit_bytes=grant << 20),
        cost_estimate=pl.CostEstimate(flops=cost[0], bytes_accessed=cost[1], transcendentals=0),
        name=getattr(kernel, "func", kernel).__name__,
    )(*operands)
    return out


def position(refs):
    return lax.axis_index("mem")


def given(refs):
    return refs[0][0]


def bind(kernel, me):
    return functools.partial(kernel, position if me is None else given)


def pack(counts, phi, me=None):
    layers = (TILE, TILE * TILE, SLOTS)
    (out,) = run(
        bind(pack_kernel, me),
        (counts, phi.reshape(layers)),
        [((COLUMNS * DEPTH * TILE, 128), F32)],
        [
            pltpu.SMEM((1, COLUMNS), I32),
            pltpu.VMEM(layers, F32),
            pltpu.SemaphoreType.DMA((3,)),
        ],
        me,
        [pltpu.HBM, pltpu.HBM],
        grant=62,
    )
    return out.reshape(COLUMNS, DEPTH * TILE, 128)


def masks_of(counts, neighbours, me=None):
    return run(
        bind(mask_kernel, me),
        (counts, neighbours),
        [((4, ROWS, 128), F32), ((3, TABLE), I32)],
        [pltpu.VMEM((128, 128), F32), pltpu.VMEM((8 * ROWS, 128), F32)],
        me,
        [pltpu.SMEM, pltpu.VMEM],
        [pltpu.VMEM, pltpu.SMEM],
        cost=(1 << 22, 1 << 17),
    )


def unpack(table, received, masks):
    half = TILE // 2
    return run(
        unpack_kernel,
        (table, received.reshape(COLUMNS * DEPTH, TILE, 128), masks),
        [((half + 2, ROWS, 128), F32), ((half + 2, ROWS, 128), F32)],
        [pltpu.VMEM((TILE * ROWS, 128), F32)],
        None,
        [pltpu.SMEM, pltpu.VMEM, pltpu.VMEM],
    )


def march(table, below, low, high, above, masks):
    half = TILE // 2
    (out,) = run(
        march_kernel,
        (table, below, low, high, above, masks),
        [((COLUMNS * DEPTH, half, 128), F32)],
        [pltpu.VMEM((2 * TILE, ROWS, 128), F32)] * 3 + [pltpu.VMEM((half * ROWS, 128), F32)],
        None,
        [pltpu.SMEM] + [pltpu.VMEM] * 5,
    )
    return out.reshape(COLUMNS, DEPTH * half, 128)


def deliver(counts, returned, me=None):
    (out,) = run(
        bind(deliver_kernel, me),
        (counts, returned.reshape(COLUMNS * TILE, 128)),
        [((CELLS, SLOTS), F32)],
        [],
        me,
        [pltpu.SMEM, pltpu.VMEM],
    )
    return out.reshape(TILE, TILE, TILE, SLOTS)


def exchange(x):
    return lax.all_to_all(x, "mem", split_axis=0, concat_axis=0, tiled=True)


def on_device(phi_owned, band_counts, neighbours):
    received = exchange(pack(band_counts, phi_owned))
    masks, table = masks_of(band_counts, neighbours)
    low, high = unpack(table, received, masks)
    groups = lax.axis_size("grp")
    rising = [(g, g + 1) for g in range(groups - 1)]
    falling = [(g + 1, g) for g in range(groups - 1)]
    below = lax.ppermute(high, "grp", rising)
    above = lax.ppermute(low, "grp", falling)
    returned = exchange(march(table, below, low, high, above, masks))
    return deliver(band_counts, returned)


def solution(mesh):
    return jax.shard_map(
        on_device,
        mesh=mesh,
        in_specs=(P(None, None, None, ("grp", "mem")), P("grp", None), P("grp", None, None)),
        out_specs=P(None, None, None, ("grp", "mem")),
        check_vma=False,
    )
```

```python
import functools

import jax
import jax.numpy as jnp
from jax import lax
from jax.experimental import pallas as pl
from jax.experimental.pallas import tpu as pltpu
from jax.sharding import PartitionSpec as P

STEPS = 4
TIME_STEP = 0.5
EPSILON = 1e-06

TILE = 8
ROWS = 32
COLUMNS = 64
SLOTS = 128
CELLS = TILE**3
DEPTH = SLOTS // COLUMNS
WIDE = 16
TABLE = 40

F32 = jnp.float32
I32 = jnp.int32


def shift(x, amount, axis):
    return pltpu.roll(x, amount % x.shape[axis] if isinstance(amount, int) else amount, axis)


def iota(shape, axis):
    return lax.broadcasted_iota(I32, shape, axis)


def own_start(counts_ref, me):
    total = jnp.int32(0)
    for owner in range(COLUMNS - 1):
        total = total + jnp.where(owner < me, counts_ref[0, owner], 0)
    return total


def pack_kernel(where_am_i, *refs):
    counts_hbm, phi_hbm, out_ref, counts_ref, phi_ref, sems = refs[-6:]
    half = TILE // 2
    copies = [
        pltpu.make_async_copy(counts_hbm, counts_ref, sems.at[0]),
        pltpu.make_async_copy(phi_hbm.at[pl.ds(half, half)], phi_ref.at[pl.ds(0, half)], sems.at[1]),
        pltpu.make_async_copy(phi_hbm.at[pl.ds(0, half)], phi_ref.at[pl.ds(half, half)], sems.at[2]),
    ]
    for copy in copies:
        copy.start()
    copies[0].wait()
    turn = own_start(counts_ref, where_am_i(refs)) & (COLUMNS - 1)
    copies[1].wait()
    copies[2].wait()
    layers = phi_ref.reshape(CELLS, SLOTS)
    low_half = iota((TILE, SLOTS), 0) < half
    for z in range(TILE):
        blocks = []
        for y in range(TILE):
            tiles = layers[pl.ds(y * TILE + z, TILE, stride=TILE * TILE), :]
            here = pltpu.roll(tiles, turn, 1)
            left = shift(here, 1, 1)
            right = shift(here, -1, 1)
            blocks.append(jnp.where(low_half, left, here))
            blocks.append(jnp.where(low_half, here, right))
        turned = jnp.concatenate(blocks, axis=0).T
        for d in range(DEPTH):
            out_ref[pl.ds(d * TILE + z, COLUMNS, stride=DEPTH * TILE), :] = turned[
                d * COLUMNS : (d + 1) * COLUMNS
            ]


def mask_kernel(where_am_i, *refs):
    counts_ref, links_ref, out_ref, table_ref, lhs_ref, found_ref = refs[-6:]
    me = where_am_i(refs)
    fill_table(counts_ref, table_ref, me)
    pairs = ROWS // 2
    for v in range(pairs):
        lhs_ref[v * 8 : v * 8 + 6, :] = jnp.where(
            links_ref[0, :, v * 128 : (v + 1) * 128] >= 0, 1.0, 0.0
        )
        lhs_ref[v * 8 + 6 : v * 8 + 8, :] = jnp.zeros((2, 128), F32)
    source = iota((128, 256), 0)
    target = iota((128, 256), 1)
    x16 = target % WIDE
    column = me + jnp.where(x16 < 4, -1, jnp.where(x16 >= 12, 1, 0))
    pick = (source % COLUMNS == column) & (source // COLUMNS == target // 128)
    found = jnp.dot(
        lhs_ref[...].astype(jnp.bfloat16),
        jnp.where(pick, 1.0, 0.0).astype(jnp.bfloat16),
        preferred_element_type=F32,
    )
    for v in range(pairs):
        for half in range(2):
            found_ref[pl.ds(2 * v + half, 8, stride=ROWS), :] = found[
                v * 8 : v * 8 + 8, half * 128 : (half + 1) * 128
            ]
    lane = iota((ROWS, 128), 1)
    x16 = lane % WIDE
    out_ref[0] = jnp.where((x16 == 3) | (x16 == 11), found_ref[ROWS : 2 * ROWS, :], 1.0)
    out_ref[1] = jnp.where(lane >= 112, found_ref[3 * ROWS : 4 * ROWS, :], 1.0)
    out_ref[2] = found_ref[4 * ROWS : 5 * ROWS, :]
    out_ref[3] = found_ref[5 * ROWS : 6 * ROWS, :]


def fill_table(counts_ref, table_ref, column):
    for entry in range(3):
        table_ref[entry, 1] = jnp.int32(0)
        table_ref[entry, ROWS] = jnp.int32(0)

    def body(owner, start):
        turn = start & (COLUMNS - 1)
        for entry in range(3):
            delta = entry - 1
            first = (column + delta - turn) & (COLUMNS - 1)
            row = (start + first - delta) >> 6
            slot = ((first + turn - delta) & (SLOTS - 1)) >> 6
            table_ref[entry, row + 1] = owner * DEPTH + slot
            table_ref[entry, row + 2] = owner * DEPTH + (1 - slot)
        return start + counts_ref[0, owner]

    lax.fori_loop(0, COLUMNS, body, jnp.int32(0), unroll=8)


def unpack_kernel(*refs):
    table_ref, received_ref, masks_ref, low_ref, high_ref, tiles_ref = refs
    x16 = iota((TILE, 128), 1) % WIDE
    for r in range(ROWS):
        left = received_ref[table_ref[0, r + 1]]
        here = received_ref[table_ref[1, r + 1]]
        right = received_ref[table_ref[2, r + 1]]
        tile = jnp.where(x16 < 4, left, jnp.where(x16 >= 12, right, here))
        tiles_ref[pl.ds(r, TILE, stride=ROWS), :] = tile
    half = TILE // 2
    for z in range(half):
        low_ref[z] = tiles_ref[z * ROWS : (z + 1) * ROWS, :]
        high_ref[z] = tiles_ref[(z + half) * ROWS : (z + half + 1) * ROWS, :]
    for i in range(2):
        low_ref[half + i] = masks_ref[i]
        high_ref[half + i] = masks_ref[i]


def march_kernel(*refs):
    (
        table_ref,
        below_ref,
        low_ref,
        high_ref,
        above_ref,
        masks_ref,
        out_ref,
        even_ref,
        odd_ref,
        sign_ref,
        done_ref,
    ) = refs
    half = TILE // 2
    lane = iota((ROWS, 128), 1)
    first_y = lane < WIDE
    last_y = lane >= 128 - WIDE
    sources = (below_ref, low_ref, high_ref, above_ref)
    for z in range(1, 2 * TILE - 1):
        level = sources[z // half][z % half]
        sign_ref[z] = level * lax.rsqrt(level * level + 1.0)

    def load(step, z):
        if step == 0:
            return sources[z // half][z % half]
        return (odd_ref if step % 2 else even_ref)[z]

    def one_step(step, lo, hi):
        target_ref = even_ref if step % 2 else odd_ref
        level = load(step, lo - 1)
        after = load(step, lo)
        ahead_z = after - level
        if lo == 4:
            ahead_z = ahead_z * masks_ref[2]
        if lo == 12:
            ahead_z = ahead_z * masks_ref[3]
        for z in range(lo, hi):
            back_z = ahead_z
            level = after
            after = load(step, z + 1)
            ahead_z = after - level
            if z == 3:
                ahead_z = ahead_z * masks_ref[2]
            if z == 11:
                ahead_z = ahead_z * masks_ref[3]
            links = (below_ref, low_ref, low_ref, above_ref)[z // half]
            sign_field = sign_ref[z]
            up = jnp.where(sign_field > 0, 1.0, -1.0)
            down = -up
            squares = None
            ahead = (shift(level, -1, 1) - level) * links[half]
            back = shift(ahead, 1, 1)
            squares = jnp.square(jnp.maximum(jnp.maximum(up * back, down * ahead), 0.0))
            beyond = jnp.where(first_y, shift(level, -1, 0), level)
            ahead = (shift(beyond, -WIDE, 1) - level) * links[half + 1]
            back = shift(jnp.where(last_y, shift(ahead, 1, 0), ahead), WIDE, 1)
            squares = squares + jnp.square(
                jnp.maximum(jnp.maximum(up * back, down * ahead), 0.0)
            )
            squares = squares + jnp.square(
                jnp.maximum(jnp.maximum(up * back_z, down * ahead_z), 0.0)
            )
            length = squares + EPSILON
            target_ref[z] = level - TIME_STEP * sign_field * (length * lax.rsqrt(length) - 1.0)

    first, last = 1, 2 * TILE - 1
    for step in range(STEPS):
        middle = TILE
        for lo, hi in ((first + step, middle), (middle, last - step)):
            pl.when(table_ref[1, 1] >= 0)(functools.partial(one_step, step, lo, hi))
    final_ref = even_ref
    left_half = lane % WIDE < TILE
    for q in range(half):
        done_ref[q * ROWS : (q + 1) * ROWS, :] = jnp.where(
            left_half, shift(final_ref[half + q], -4, 1), shift(final_ref[2 * half + q], 4, 1)
        )
    for r in range(ROWS):
        out_ref[table_ref[1, r + 1]] = done_ref[pl.ds(r, half, stride=ROWS), :]


def deliver_kernel(where_am_i, *refs):
    counts_ref, returned_ref, out_ref = refs[-3:]
    me = where_am_i(refs)
    turn = own_start(counts_ref, me) & (COLUMNS - 1)
    live = iota((SLOTS, SLOTS), 1) < counts_ref[0, me]
    half = TILE // 2
    for q in range(half):
        rows = [
            returned_ref[pl.ds(d * half + q, COLUMNS, stride=DEPTH * half), :] for d in range(DEPTH)
        ]
        turned = jnp.concatenate(rows, axis=0).T
        turned = pltpu.roll(turned, (SLOTS - turn) & (SLOTS - 1), 1)
        turned = jnp.where(live, turned, 0.0)
        for y in range(TILE):
            for upper in range(2):
                row = y * WIDE + upper * TILE
                out_ref[pl.ds(y * TILE + q + upper * half, TILE, stride=TILE * TILE), :] = turned[
                    row : row + TILE
                ]


def spec(space=pltpu.VMEM):
    return pl.BlockSpec(memory_space=space)


def run(
    kernel, operands, shapes, scratch, me=None, spaces=None, out_spaces=None, cost=(0, 0), grant=32
):
    spaces = spaces or [pltpu.VMEM] * len(operands)
    out_spaces = out_spaces or [pltpu.VMEM] * len(shapes)
    if me is not None:
        operands = (me, *operands)
        spaces = [pltpu.SMEM, *spaces]
    out = pl.pallas_call(
        kernel,
        out_shape=[jax.ShapeDtypeStruct(s, t) for s, t in shapes],
        in_specs=[spec(s) for s in spaces],
        out_specs=[spec(s) for s in out_spaces],
        scratch_shapes=scratch,
        compiler_params=pltpu.CompilerParams(vmem_limit_bytes=grant << 20),
        cost_estimate=pl.CostEstimate(flops=cost[0], bytes_accessed=cost[1], transcendentals=0),
        name=getattr(kernel, "func", kernel).__name__,
    )(*operands)
    return out


def position(refs):
    return lax.axis_index("mem")


def given(refs):
    return refs[0][0]


def bind(kernel, me):
    return functools.partial(kernel, position if me is None else given)


def pack(counts, phi, me=None):
    layers = (TILE, TILE * TILE, SLOTS)
    (out,) = run(
        bind(pack_kernel, me),
        (counts, phi.reshape(layers)),
        [((COLUMNS * DEPTH * TILE, 128), F32)],
        [
            pltpu.SMEM((1, COLUMNS), I32),
            pltpu.VMEM(layers, F32),
            pltpu.SemaphoreType.DMA((3,)),
        ],
        me,
        [pltpu.HBM, pltpu.HBM],
        grant=62,
    )
    return out.reshape(COLUMNS, DEPTH * TILE, 128)


def masks_of(counts, neighbours, me=None):
    return run(
        bind(mask_kernel, me),
        (counts, neighbours),
        [((4, ROWS, 128), F32), ((3, TABLE), I32)],
        [pltpu.VMEM((128, 128), F32), pltpu.VMEM((8 * ROWS, 128), F32)],
        me,
        [pltpu.SMEM, pltpu.VMEM],
        [pltpu.VMEM, pltpu.SMEM],
        cost=(1 << 22, 1 << 17),
    )


def unpack(table, received, masks):
    half = TILE // 2
    return run(
        unpack_kernel,
        (table, received.reshape(COLUMNS * DEPTH, TILE, 128), masks),
        [((half + 2, ROWS, 128), F32), ((half + 2, ROWS, 128), F32)],
        [pltpu.VMEM((TILE * ROWS, 128), F32)],
        None,
        [pltpu.SMEM, pltpu.VMEM, pltpu.VMEM],
    )


def march(table, below, low, high, above, masks):
    half = TILE // 2
    (out,) = run(
        march_kernel,
        (table, below, low, high, above, masks),
        [((COLUMNS * DEPTH, half, 128), F32)],
        [pltpu.VMEM((2 * TILE, ROWS, 128), F32)] * 3 + [pltpu.VMEM((half * ROWS, 128), F32)],
        None,
        [pltpu.SMEM] + [pltpu.VMEM] * 5,
    )
    return out.reshape(COLUMNS, DEPTH * half, 128)


def deliver(counts, returned, me=None):
    (out,) = run(
        bind(deliver_kernel, me),
        (counts, returned.reshape(COLUMNS * TILE, 128)),
        [((CELLS, SLOTS), F32)],
        [],
        me,
        [pltpu.SMEM, pltpu.VMEM],
    )
    return out.reshape(TILE, TILE, TILE, SLOTS)


def exchange(x):
    return lax.all_to_all(x, "mem", split_axis=0, concat_axis=0, tiled=True)


def on_device(phi_owned, band_counts, neighbours):
    received = exchange(pack(band_counts, phi_owned))
    masks, table = masks_of(band_counts, neighbours)
    low, high = unpack(table, received, masks)
    groups = lax.axis_size("grp")
    rising = [(g, g + 1) for g in range(groups - 1)]
    falling = [(g + 1, g) for g in range(groups - 1)]
    below = lax.ppermute(high, "grp", rising)
    above = lax.ppermute(low, "grp", falling)
    returned = exchange(march(table, below, low, high, above, masks))
    return deliver(band_counts, returned)


def solution(mesh):
    return jax.shard_map(
        on_device,
        mesh=mesh,
        in_specs=(P(None, None, None, ("grp", "mem")), P("grp", None), P("grp", None, None)),
        out_specs=P(None, None, None, ("grp", "mem")),
        check_vma=False,
    )
```

```python
import functools

import jax
import jax.numpy as jnp
from jax import lax
from jax.experimental import pallas as pl
from jax.experimental.pallas import tpu as pltpu
from jax.sharding import PartitionSpec as P

STEPS = 4
TIME_STEP = 0.5
EPSILON = 1e-06

TILE = 8
ROWS = 32
COLUMNS = 64
SLOTS = 128
CELLS = TILE**3
DEPTH = SLOTS // COLUMNS
WIDE = 16
TABLE = 40
HALF = TILE // 2
PAIRS = HALF // 2
SENT = 3 * DEPTH * PAIRS
BACK = 2 * DEPTH * PAIRS

F32 = jnp.float32
I32 = jnp.int32


def shift(x, amount, axis):
    return pltpu.roll(x, amount % x.shape[axis] if isinstance(amount, int) else amount, axis)


def iota(shape, axis):
    return lax.broadcasted_iota(I32, shape, axis)


def own_start(counts_ref, me):
    total = jnp.int32(0)
    for owner in range(COLUMNS - 1):
        total = total + jnp.where(owner < me, counts_ref[0, owner], 0)
    return total


def plane_of(core, pair, upper):
    w = pair + PAIRS * upper
    return TILE - 1 - w if core else w


def pack_kernel(where_am_i, *refs):
    counts_hbm, phi_hbm, out_ref, counts_ref, phi_ref, turned_ref, sems = refs[-7:]
    copies = [
        pltpu.make_async_copy(counts_hbm, counts_ref, sems.at[0]),
        pltpu.make_async_copy(phi_hbm, phi_ref, sems.at[1]),
    ]
    for copy in copies:
        copy.start()
    copies[0].wait()
    turn = own_start(counts_ref, where_am_i(refs)) & (COLUMNS - 1)
    copies[1].wait()
    chips = COLUMNS // 2
    upper_x = iota((chips, 128), 1) % TILE >= HALF
    for core in range(2):
        for pair in range(PAIRS):
            blocks = []
            for y in range(TILE):
                for upper in range(2):
                    z = plane_of(core, pair, upper)
                    tiles = phi_ref[pl.ds(y * TILE + z, TILE, stride=TILE * TILE), :]
                    blocks.append(pltpu.roll(tiles, turn, 1))
            turned = jnp.concatenate(blocks, axis=0).T
            held_ref = turned_ref.at[core * PAIRS + pair]
            held_ref[8 : 8 + SLOTS, :] = turned
            held_ref[7:8, :] = turned[SLOTS - 1 :]
            held_ref[8 + SLOTS : 9 + SLOTS, :] = turned[:1]
            for d in range(DEPTH):
                first = 8 + d * COLUMNS
                base = core * SENT + d * PAIRS + pair
                for column in range(2):
                    out_ref[
                        pl.ds(base + column * DEPTH * PAIRS, chips, stride=2 * SENT), :
                    ] = held_ref[pl.ds(first + column, chips, stride=2), :]
                left = held_ref[pl.ds(first - 1, chips, stride=2), :]
                right = held_ref[pl.ds(first + 2, chips, stride=2), :]
                out_ref[pl.ds(base + 2 * DEPTH * PAIRS, chips, stride=2 * SENT), :] = jnp.where(
                    upper_x, left, right
                )


def fill_table(counts_ref, table_ref, column):
    for entry in range(6):
        table_ref[entry, 1] = jnp.int32(0)
        table_ref[entry, ROWS] = jnp.int32(0)

    def body(owner, start):
        turn = start & (COLUMNS - 1)
        for entry, delta in enumerate((0, 1, -1, 2)):
            first = (column + delta - turn) & (COLUMNS - 1)
            row = (start + first - delta) >> 6
            slot = ((first + turn - delta) & (SLOTS - 1)) >> 6
            base = owner * (3 * DEPTH) + min(entry, 2) * DEPTH
            table_ref[entry, row + 1] = base + slot
            table_ref[entry, row + 2] = base + (1 - slot)
            if entry < 2:
                base = owner * (2 * DEPTH) + entry * DEPTH
                table_ref[4 + entry, row + 1] = base + slot
                table_ref[4 + entry, row + 2] = base + (1 - slot)
        return start + counts_ref[0, owner]

    lax.fori_loop(0, COLUMNS, body, jnp.int32(0), unroll=8)


def mask_kernel(where_am_i, *refs):
    counts_ref, links_ref, flat_ref, outer_ref, table_ref, lhs_ref, found_ref = refs[-7:]
    me = where_am_i(refs)
    chip, core = me >> 1, me & 1
    fill_table(counts_ref, table_ref, 2 * chip)
    blocks = ROWS // 2
    for v in range(blocks):
        lhs_ref[v * 8 : v * 8 + 6, :] = jnp.where(
            links_ref[0, :, v * 128 : (v + 1) * 128] >= 0, 1.0, 0.0
        )
        lhs_ref[v * 8 + 6 : v * 8 + 8, :] = jnp.zeros((2, 128), F32)
    source = iota((128, 256), 0)
    target = iota((128, 256), 1)
    x16 = target % WIDE
    lane = iota((ROWS, 128), 1)
    for column in range(2):
        wanted = 2 * chip + column + jnp.where(x16 < 4, -1, jnp.where(x16 >= 12, 1, 0))
        pick = (source % COLUMNS == wanted) & (source // COLUMNS == target // 128)
        found = jnp.dot(
            lhs_ref[...].astype(jnp.bfloat16),
            jnp.where(pick, 1.0, 0.0).astype(jnp.bfloat16),
            preferred_element_type=F32,
        )
        for v in range(blocks):
            for odd in range(2):
                found_ref[pl.ds(2 * v + odd, 8, stride=ROWS), :] = found[
                    v * 8 : v * 8 + 8, odd * 128 : (odd + 1) * 128
                ]
        edge = (lane % WIDE == 3) | (lane % WIDE == 11)
        flat_ref[column] = jnp.where(edge, found_ref[ROWS : 2 * ROWS, :], 1.0)
        flat_ref[2 + column] = jnp.where(lane >= 112, found_ref[3 * ROWS : 4 * ROWS, :], 1.0)
        outer_ref[column] = jnp.where(
            core == 0, found_ref[4 * ROWS : 5 * ROWS, :], found_ref[5 * ROWS : 6 * ROWS, :]
        )


def unpack_kernel(table_ref, received_ref, planes_ref, packed_ref):
    for r in range(ROWS):
        for entry in range(4):
            packed_ref[pl.ds(entry * PAIRS * ROWS + r, PAIRS, stride=ROWS), :] = received_ref[
                table_ref[entry, r + 1]
            ]
    lane = iota((ROWS, 128), 1)
    x16 = lane % WIDE
    for pair in range(PAIRS):
        first, second, left, right = (
            packed_ref[(entry * PAIRS + pair) * ROWS : (entry * PAIRS + pair + 1) * ROWS, :]
            for entry in range(4)
        )
        outside = jnp.where(lane % TILE >= HALF, left, right)

        def join(left, here, right):
            return jnp.where(x16 < 4, left, jnp.where(x16 >= 12, right, here))

        second_4 = shift(second, 4, 1)
        first_m4 = shift(first, -4, 1)
        planes_ref[pair] = join(shift(outside, -4, 1), shift(first, 4, 1), shift(second, 12, 1))
        planes_ref[PAIRS + pair] = join(shift(outside, -12, 1), first_m4, second_4)
        planes_ref[HALF + pair] = join(first_m4, second_4, shift(outside, 12, 1))
        planes_ref[HALF + PAIRS + pair] = join(
            shift(first, -12, 1), shift(second, -4, 1), shift(outside, 4, 1)
        )


def march_kernel(*refs):
    (
        table_ref,
        outer_ref,
        own_ref,
        inner_ref,
        far_ref,
        near_ref,
        faces_ref,
        out_ref,
        even_ref,
        odd_ref,
        sign_ref,
        done_ref,
    ) = refs
    depth = 3 * HALF
    lane = iota((ROWS, 128), 1)
    first_y = lane < WIDE
    last_y = lane >= 128 - WIDE

    def start(column, p):
        base = column * HALF
        if p < HALF:
            return outer_ref[base + HALF - 1 - p]
        if p < 2 * HALF:
            return own_ref[base + p - HALF]
        return inner_ref[base + depth - 1 - p]

    def load(step, column, p):
        if step == 0:
            return start(column, p)
        return (odd_ref if step % 2 else even_ref)[column * depth + p]

    def one_step(step, column, lo, hi):
        target_ref = even_ref if step % 2 else odd_ref
        level = load(step, column, lo - 1)
        after = load(step, column, lo)
        ahead_z = after - level
        if lo == HALF:
            ahead_z = ahead_z * faces_ref[column]
        for p in range(lo, hi):
            back_z = ahead_z
            level = after
            after = load(step, column, p + 1)
            ahead_z = after - level
            if p == HALF - 1:
                ahead_z = ahead_z * faces_ref[column]
            links = far_ref if p < HALF else near_ref
            if step == 0:
                sign_field = level * lax.rsqrt(level * level + 1.0)
                sign_ref[column * depth + p] = sign_field
            else:
                sign_field = sign_ref[column * depth + p]
            up = jnp.where(sign_field > 0, 1.0, -1.0)
            down = -up
            ahead = (shift(level, -1, 1) - level) * links[column]
            back = shift(ahead, 1, 1)
            squares = jnp.square(jnp.maximum(jnp.maximum(up * back, down * ahead), 0.0))
            beyond = jnp.where(first_y, shift(level, -1, 0), level)
            ahead = (shift(beyond, -WIDE, 1) - level) * links[2 + column]
            back = shift(jnp.where(last_y, shift(ahead, 1, 0), ahead), WIDE, 1)
            squares = squares + jnp.square(
                jnp.maximum(jnp.maximum(up * back, down * ahead), 0.0)
            )
            squares = squares + jnp.square(
                jnp.maximum(jnp.maximum(up * back_z, down * ahead_z), 0.0)
            )
            length = squares + EPSILON
            target_ref[column * depth + p] = level - TIME_STEP * sign_field * (
                length * lax.rsqrt(length) - 1.0
            )

    for step, cuts in enumerate(((1, 6, 11), (2, 6, 10), (3, 9), (4, 8))):
        for column in range(2):
            for lo, hi in zip(cuts[:-1], cuts[1:]):
                pl.when(table_ref[0, 1] >= 0)(
                    functools.partial(one_step, step, column, lo, hi)
                )
    lower = lane % WIDE < TILE
    for column in range(2):
        for pair in range(PAIRS):
            p = column * depth + HALF + pair
            row = (column * PAIRS + pair) * ROWS
            done_ref[row : row + ROWS, :] = jnp.where(
                lower, shift(even_ref[p], -4, 1), shift(even_ref[p + PAIRS], 4, 1)
            )
    for r in range(ROWS):
        for column in range(2):
            out_ref[table_ref[4 + column, r + 1]] = done_ref[
                pl.ds(column * PAIRS * ROWS + r, PAIRS, stride=ROWS), :
            ]


def deliver_kernel(where_am_i, *refs):
    counts_ref, returned_ref, out_ref, turned_ref = refs[-4:]
    me = where_am_i(refs)
    turn = own_start(counts_ref, me) & (COLUMNS - 1)
    live = iota((SLOTS, SLOTS), 1) < counts_ref[0, me]
    chips = COLUMNS // 2
    for core in range(2):
        for pair in range(PAIRS):
            held_ref = turned_ref.at[core * PAIRS + pair]
            for d in range(DEPTH):
                for column in range(2):
                    row = core * BACK + (column * DEPTH + d) * PAIRS + pair
                    held_ref[pl.ds(d * COLUMNS + column, chips, stride=2), :] = returned_ref[
                        pl.ds(row, chips, stride=2 * BACK), :
                    ]
            turned = pltpu.roll(held_ref[...].T, (SLOTS - turn) & (SLOTS - 1), 1)
            turned = jnp.where(live, turned, 0.0)
            for y in range(TILE):
                for upper in range(2):
                    row = y * WIDE + upper * TILE
                    z = plane_of(core, pair, upper)
                    out_ref[pl.ds(y * TILE + z, TILE, stride=TILE * TILE), :] = turned[
                        row : row + TILE
                    ]


def spec(space=pltpu.VMEM):
    return pl.BlockSpec(memory_space=space)


def run(
    kernel, operands, shapes, scratch, me=None, spaces=None, out_spaces=None, cost=(0, 0), grant=32
):
    spaces = spaces or [pltpu.VMEM] * len(operands)
    out_spaces = out_spaces or [pltpu.VMEM] * len(shapes)
    if me is not None:
        operands = (me, *operands)
        spaces = [pltpu.SMEM, *spaces]
    out = pl.pallas_call(
        kernel,
        out_shape=[jax.ShapeDtypeStruct(s, t) for s, t in shapes],
        in_specs=[spec(s) for s in spaces],
        out_specs=[spec(s) for s in out_spaces],
        scratch_shapes=scratch,
        compiler_params=pltpu.CompilerParams(vmem_limit_bytes=grant << 20),
        cost_estimate=pl.CostEstimate(flops=cost[0], bytes_accessed=cost[1], transcendentals=0),
        name=getattr(kernel, "func", kernel).__name__,
    )(*operands)
    return out


def position(refs):
    return lax.axis_index("mem")


def given(refs):
    return refs[0][0]


def bind(kernel, me):
    return functools.partial(kernel, position if me is None else given)


def pack(counts, phi, me=None):
    (out,) = run(
        bind(pack_kernel, me),
        (counts, phi.reshape(CELLS, SLOTS)),
        [((COLUMNS * SENT, 128), F32)],
        [
            pltpu.SMEM((1, COLUMNS), I32),
            pltpu.VMEM((CELLS, SLOTS), F32),
            pltpu.VMEM((2 * PAIRS, SLOTS + 16, 128), F32),
            pltpu.SemaphoreType.DMA((2,)),
        ],
        me,
        [pltpu.HBM, pltpu.HBM],
        grant=62,
    )
    return out.reshape(COLUMNS * SENT // 4, 4, 128)


def masks_of(counts, neighbours, me=None):
    return run(
        bind(mask_kernel, me),
        (counts, neighbours),
        [((4, ROWS, 128), F32), ((2, ROWS, 128), F32), ((6, TABLE), I32)],
        [pltpu.VMEM((128, 128), F32), pltpu.VMEM((8 * ROWS, 128), F32)],
        me,
        [pltpu.SMEM, pltpu.VMEM],
        [pltpu.VMEM, pltpu.VMEM, pltpu.SMEM],
        cost=(1 << 22, 1 << 17),
    )


def unpack(table, received):
    (out,) = run(
        unpack_kernel,
        (table, received.reshape(COLUMNS * SENT // PAIRS, PAIRS, 128)),
        [((TILE, ROWS, 128), F32)],
        [pltpu.VMEM((4 * PAIRS * ROWS, 128), F32)],
        None,
        [pltpu.SMEM, pltpu.VMEM],
    )
    return out


def march(table, outer, own, inner, far, near, faces):
    (out,) = run(
        march_kernel,
        (table, outer, own, inner, far, near, faces),
        [((COLUMNS * BACK // PAIRS, PAIRS, 128), F32)],
        [pltpu.VMEM((6 * HALF, ROWS, 128), F32)] * 3 + [pltpu.VMEM((TILE // 2 * ROWS, 128), F32)],
        None,
        [pltpu.SMEM] + [pltpu.VMEM] * 6,
    )
    return out.reshape(COLUMNS, BACK, 128)


def deliver(counts, returned, me=None):
    (out,) = run(
        bind(deliver_kernel, me),
        (counts, returned.reshape(COLUMNS * BACK, 128)),
        [((CELLS, SLOTS), F32)],
        [pltpu.VMEM((2 * PAIRS, SLOTS, 128), F32)],
        me,
        [pltpu.SMEM, pltpu.VMEM],
    )
    return out.reshape(TILE, TILE, TILE, SLOTS)


def exchange(x):
    return lax.all_to_all(x, "mem", split_axis=0, concat_axis=0, tiled=True)


def on_device(phi_owned, band_counts, neighbours):
    groups, members = lax.axis_size("grp"), lax.axis_size("mem")
    mates = [(m, m ^ 1) for m in range(members)]
    across = []
    for g in range(groups - 1):
        for m in range(0, members, 2):
            low, high = g * members + m + 1, (g + 1) * members + m
            across += [(low, high), (high, low)]
    received = exchange(pack(band_counts, phi_owned))
    near, faces, table = masks_of(band_counts, neighbours)
    far = lax.ppermute(near, ("grp", "mem"), across)
    received, far = lax.optimization_barrier((received, far))
    own = unpack(table, received)
    outer = lax.ppermute(own, ("grp", "mem"), across)
    inner = lax.ppermute(own, "mem", mates)
    returned = exchange(march(table, outer, own, inner, far, near, faces))
    return deliver(band_counts, returned)


def solution(mesh):
    return jax.shard_map(
        on_device,
        mesh=mesh,
        in_specs=(P(None, None, None, ("grp", "mem")), P("grp", None), P("grp", None, None)),
        out_specs=P(None, None, None, ("grp", "mem")),
        check_vma=False,
    )
```

```python
import functools

import jax
import jax.numpy as jnp
from jax import lax
from jax.experimental import pallas as pl
from jax.experimental.pallas import tpu as pltpu
from jax.sharding import PartitionSpec as P

STEPS = 4
TIME_STEP = 0.5
EPSILON = 1e-06

TILE = 8
ROWS = 32
COLUMNS = 64
SLOTS = 128
CELLS = TILE**3
DEPTH = SLOTS // COLUMNS
WIDE = 16
TABLE = 40
HALF = TILE // 2
PAIRS = HALF // 2
SENT = 3 * DEPTH * PAIRS
BACK = 2 * DEPTH * PAIRS

F32 = jnp.float32
I32 = jnp.int32


def shift(x, amount, axis):
    return pltpu.roll(x, amount % x.shape[axis] if isinstance(amount, int) else amount, axis)


def iota(shape, axis):
    return lax.broadcasted_iota(I32, shape, axis)


def own_start(counts_ref, me):
    total = jnp.int32(0)
    for owner in range(COLUMNS - 1):
        total = total + jnp.where(owner < me, counts_ref[0, owner], 0)
    return total


def plane_of(core, pair, upper):
    w = pair + PAIRS * upper
    return TILE - 1 - w if core else w


def pack_kernel(where_am_i, *refs):
    counts_hbm, phi_hbm, out_ref, counts_ref, phi_ref, turned_ref, sems = refs[-7:]
    copies = [
        pltpu.make_async_copy(counts_hbm, counts_ref, sems.at[0]),
        pltpu.make_async_copy(phi_hbm, phi_ref, sems.at[1]),
    ]
    for copy in copies:
        copy.start()
    copies[0].wait()
    turn = own_start(counts_ref, where_am_i(refs)) & (COLUMNS - 1)
    copies[1].wait()
    chips = COLUMNS // 2
    upper_x = iota((chips, 128), 1) % TILE >= HALF
    for core in range(2):
        for pair in range(PAIRS):
            blocks = []
            for y in range(TILE):
                for upper in range(2):
                    z = plane_of(core, pair, upper)
                    tiles = phi_ref[pl.ds(y * TILE + z, TILE, stride=TILE * TILE), :]
                    blocks.append(pltpu.roll(tiles, turn, 1))
            turned = jnp.concatenate(blocks, axis=0).T
            held_ref = turned_ref.at[core * PAIRS + pair]
            held_ref[8 : 8 + SLOTS, :] = turned
            held_ref[7:8, :] = turned[SLOTS - 1 :]
            held_ref[8 + SLOTS : 9 + SLOTS, :] = turned[:1]
            for d in range(DEPTH):
                first = 8 + d * COLUMNS
                base = core * SENT + d * PAIRS + pair
                for column in range(2):
                    out_ref[
                        pl.ds(base + column * DEPTH * PAIRS, chips, stride=2 * SENT), :
                    ] = held_ref[pl.ds(first + column, chips, stride=2), :]
                left = held_ref[pl.ds(first - 1, chips, stride=2), :]
                right = held_ref[pl.ds(first + 2, chips, stride=2), :]
                out_ref[pl.ds(base + 2 * DEPTH * PAIRS, chips, stride=2 * SENT), :] = jnp.where(
                    upper_x, left, right
                )


def fill_table(counts_ref, table_ref, column):
    for entry in range(6):
        table_ref[entry, 1] = jnp.int32(0)
        table_ref[entry, ROWS] = jnp.int32(0)

    def body(owner, start):
        turn = start & (COLUMNS - 1)
        for entry, delta in enumerate((0, 1, -1, 2)):
            first = (column + delta - turn) & (COLUMNS - 1)
            row = (start + first - delta) >> 6
            slot = ((first + turn - delta) & (SLOTS - 1)) >> 6
            base = owner * (3 * DEPTH) + min(entry, 2) * DEPTH
            table_ref[entry, row + 1] = base + slot
            table_ref[entry, row + 2] = base + (1 - slot)
            if entry < 2:
                base = owner * (2 * DEPTH) + entry * DEPTH
                table_ref[4 + entry, row + 1] = base + slot
                table_ref[4 + entry, row + 2] = base + (1 - slot)
        return start + counts_ref[0, owner]

    lax.fori_loop(0, COLUMNS, body, jnp.int32(0), unroll=8)


def mask_kernel(where_am_i, *refs):
    counts_ref, links_ref, flat_ref, outer_ref, table_ref, lhs_ref, found_ref = refs[-7:]
    me = where_am_i(refs)
    chip, core = me >> 1, me & 1
    fill_table(counts_ref, table_ref, 2 * chip)
    blocks = ROWS // 2
    for v in range(blocks):
        lhs_ref[v * 8 : v * 8 + 6, :] = jnp.where(
            links_ref[0, :, v * 128 : (v + 1) * 128] >= 0, 1.0, 0.0
        )
        lhs_ref[v * 8 + 6 : v * 8 + 8, :] = jnp.zeros((2, 128), F32)
    source = iota((128, 256), 0)
    target = iota((128, 256), 1)
    x16 = target % WIDE
    lane = iota((ROWS, 128), 1)
    for column in range(2):
        wanted = 2 * chip + column + jnp.where(x16 < 4, -1, jnp.where(x16 >= 12, 1, 0))
        pick = (source % COLUMNS == wanted) & (source // COLUMNS == target // 128)
        found = jnp.dot(
            lhs_ref[...].astype(jnp.bfloat16),
            jnp.where(pick, 1.0, 0.0).astype(jnp.bfloat16),
            preferred_element_type=F32,
        )
        for v in range(blocks):
            for odd in range(2):
                found_ref[pl.ds(2 * v + odd, 8, stride=ROWS), :] = found[
                    v * 8 : v * 8 + 8, odd * 128 : (odd + 1) * 128
                ]
        edge = (lane % WIDE == 3) | (lane % WIDE == 11)
        flat_ref[column] = jnp.where(edge, found_ref[ROWS : 2 * ROWS, :], 1.0)
        flat_ref[2 + column] = jnp.where(lane >= 112, found_ref[3 * ROWS : 4 * ROWS, :], 1.0)
        outer_ref[column] = jnp.where(
            core == 0, found_ref[4 * ROWS : 5 * ROWS, :], found_ref[5 * ROWS : 6 * ROWS, :]
        )


def unpack_kernel(table_ref, received_ref, planes_ref, packed_ref):
    for r in range(ROWS):
        for entry in range(4):
            packed_ref[pl.ds(entry * PAIRS * ROWS + r, PAIRS, stride=ROWS), :] = received_ref[
                table_ref[entry, r + 1]
            ]
    lane = iota((ROWS, 128), 1)
    x16 = lane % WIDE
    for pair in range(PAIRS):
        first, second, left, right = (
            packed_ref[(entry * PAIRS + pair) * ROWS : (entry * PAIRS + pair + 1) * ROWS, :]
            for entry in range(4)
        )
        outside = jnp.where(lane % TILE >= HALF, left, right)

        def join(left, here, right):
            return jnp.where(x16 < 4, left, jnp.where(x16 >= 12, right, here))

        second_4 = shift(second, 4, 1)
        first_m4 = shift(first, -4, 1)
        planes_ref[pair] = join(shift(outside, -4, 1), shift(first, 4, 1), shift(second, 12, 1))
        planes_ref[PAIRS + pair] = join(shift(outside, -12, 1), first_m4, second_4)
        planes_ref[HALF + pair] = join(first_m4, second_4, shift(outside, 12, 1))
        planes_ref[HALF + PAIRS + pair] = join(
            shift(first, -12, 1), shift(second, -4, 1), shift(outside, 4, 1)
        )


def march_kernel(where_am_i, *refs):
    (
        table_vmem,
        outer_ref,
        own_ref,
        inner_ref,
        far_ref,
        near_ref,
        faces_ref,
        out_ref,
        even_ref,
        odd_ref,
        pull_ref,
        side_ref,
        done_ref,
        table_ref,
        sem,
    ) = refs[-15:]
    here = where_am_i(refs)
    fetch = pltpu.make_async_copy(table_vmem, table_ref, sem)
    fetch.start()
    depth = 3 * HALF
    lane = iota((ROWS, 128), 1)
    first_y = lane < WIDE
    last_y = lane >= 128 - WIDE

    def start(column, p):
        base = column * HALF
        if p < HALF:
            return outer_ref[base + HALF - 1 - p]
        if p < 2 * HALF:
            return own_ref[base + p - HALF]
        return inner_ref[base + depth - 1 - p]

    def load(step, column, p):
        if step == 0:
            return start(column, p)
        return (odd_ref if step % 2 else even_ref)[column * depth + p]

    def one_step(step, column, lo, hi):
        target_ref = even_ref if step % 2 else odd_ref
        level = load(step, column, lo - 1)
        after = load(step, column, lo)
        ahead_z = after - level
        if lo == HALF:
            ahead_z = ahead_z * faces_ref[column]
        for p in range(lo, hi):
            back_z = ahead_z
            level = after
            after = load(step, column, p + 1)
            ahead_z = after - level
            if p == HALF - 1:
                ahead_z = ahead_z * faces_ref[column]
            links = far_ref if p < HALF else near_ref
            if step == 0:
                sign_field = level * lax.rsqrt(level * level + 1.0)
                pull = TIME_STEP * sign_field
                up = jnp.where(sign_field > 0, 1.0, -1.0)
                pull_ref[column * depth + p] = pull
                side_ref[column * depth + p] = up
            else:
                pull = pull_ref[column * depth + p]
                up = side_ref[column * depth + p]
            down = -up
            ahead = (shift(level, -1, 1) - level) * links[column]
            back = shift(ahead, 1, 1)
            squares = jnp.square(jnp.maximum(jnp.maximum(up * back, down * ahead), 0.0))
            beyond = jnp.where(first_y, shift(level, -1, 0), level)
            ahead = (shift(beyond, -WIDE, 1) - level) * links[2 + column]
            back = shift(jnp.where(last_y, shift(ahead, 1, 0), ahead), WIDE, 1)
            squares = squares + jnp.square(
                jnp.maximum(jnp.maximum(up * back, down * ahead), 0.0)
            )
            squares = squares + jnp.square(
                jnp.maximum(jnp.maximum(up * back_z, down * ahead_z), 0.0)
            )
            length = squares + EPSILON
            target_ref[column * depth + p] = level - pull * (
                length * lax.rsqrt(length) - 1.0
            )

    spans = ((1, 11), (2, 10), (3, 9), (4, 8))

    def several(steps, columns):
        for step in steps:
            for column in columns:
                one_step(step, column, *spans[step])

    for block, (steps, columns) in enumerate((((0,), (0,)), ((0,), (1,)), ((1,), (0,)), ((1,), (1,)), ((2,), (0,)), ((2,), (1,)), ((3,), (0, 1)))):
        pl.when(here > -1 - block)(functools.partial(several, steps, columns))
    lower = lane % WIDE < TILE
    for column in range(2):
        for pair in range(PAIRS):
            p = column * depth + HALF + pair
            row = (column * PAIRS + pair) * ROWS
            done_ref[row : row + ROWS, :] = jnp.where(
                lower, shift(even_ref[p], -4, 1), shift(even_ref[p + PAIRS], 4, 1)
            )
    fetch.wait()
    for r in range(ROWS):
        for column in range(2):
            out_ref[table_ref[4 + column, r + 1]] = done_ref[
                pl.ds(column * PAIRS * ROWS + r, PAIRS, stride=ROWS), :
            ]


def deliver_kernel(where_am_i, *refs):
    counts_ref, returned_ref, out_ref, turned_ref = refs[-4:]
    me = where_am_i(refs)
    counts = counts_ref[...]
    owner = iota((1, COLUMNS), 1)
    turn = jnp.sum(jnp.where(owner < me, counts, 0)) & (COLUMNS - 1)
    live = iota((SLOTS, SLOTS), 1) < jnp.sum(jnp.where(owner == me, counts, 0))
    chips = COLUMNS // 2
    for core in range(2):
        for pair in range(PAIRS):
            held_ref = turned_ref.at[core * PAIRS + pair]
            for d in range(DEPTH):
                for column in range(2):
                    row = core * BACK + (column * DEPTH + d) * PAIRS + pair
                    held_ref[pl.ds(d * COLUMNS + column, chips, stride=2), :] = returned_ref[
                        pl.ds(row, chips, stride=2 * BACK), :
                    ]
            turned = pltpu.roll(held_ref[...].T, (SLOTS - turn) & (SLOTS - 1), 1)
            turned = jnp.where(live, turned, 0.0)
            for y in range(TILE):
                for upper in range(2):
                    row = y * WIDE + upper * TILE
                    z = plane_of(core, pair, upper)
                    out_ref[pl.ds(y * TILE + z, TILE, stride=TILE * TILE), :] = turned[
                        row : row + TILE
                    ]


def spec(space=pltpu.VMEM):
    return pl.BlockSpec(memory_space=space)


def run(
    kernel, operands, shapes, scratch, me=None, spaces=None, out_spaces=None, cost=(0, 0), grant=32
):
    spaces = spaces or [pltpu.VMEM] * len(operands)
    out_spaces = out_spaces or [pltpu.VMEM] * len(shapes)
    if me is not None:
        operands = (me, *operands)
        spaces = [pltpu.SMEM, *spaces]
    out = pl.pallas_call(
        kernel,
        out_shape=[jax.ShapeDtypeStruct(s, t) for s, t in shapes],
        in_specs=[spec(s) for s in spaces],
        out_specs=[spec(s) for s in out_spaces],
        scratch_shapes=scratch,
        compiler_params=pltpu.CompilerParams(vmem_limit_bytes=grant << 20),
        cost_estimate=pl.CostEstimate(flops=cost[0], bytes_accessed=cost[1], transcendentals=0),
        name=getattr(kernel, "func", kernel).__name__,
    )(*operands)
    return out


def position(refs):
    return lax.axis_index("mem")


def given(refs):
    return refs[0][0]


def bind(kernel, me):
    return functools.partial(kernel, position if me is None else given)


def pack(counts, phi, me=None):
    (out,) = run(
        bind(pack_kernel, me),
        (counts, phi.reshape(CELLS, SLOTS)),
        [((COLUMNS * SENT, 128), F32)],
        [
            pltpu.SMEM((1, COLUMNS), I32),
            pltpu.VMEM((CELLS, SLOTS), F32),
            pltpu.VMEM((2 * PAIRS, SLOTS + 16, 128), F32),
            pltpu.SemaphoreType.DMA((2,)),
        ],
        me,
        [pltpu.HBM, pltpu.HBM],
        grant=62,
    )
    return out.reshape(COLUMNS * SENT // 4, 4, 128)


def masks_of(counts, neighbours, me=None):
    return run(
        bind(mask_kernel, me),
        (counts, neighbours),
        [((4, ROWS, 128), F32), ((2, ROWS, 128), F32), ((6, TABLE), I32)],
        [pltpu.VMEM((128, 128), F32), pltpu.VMEM((8 * ROWS, 128), F32)],
        me,
        [pltpu.SMEM, pltpu.VMEM],
        [pltpu.VMEM, pltpu.VMEM, pltpu.SMEM],
        cost=(1 << 22, 1 << 17),
    )


def unpack(table, received):
    (out,) = run(
        unpack_kernel,
        (table, received.reshape(COLUMNS * SENT // PAIRS, PAIRS, 128)),
        [((TILE, ROWS, 128), F32)],
        [pltpu.VMEM((4 * PAIRS * ROWS, 128), F32)],
        None,
        [pltpu.SMEM, pltpu.VMEM],
    )
    return out


def march(table, outer, own, inner, far, near, faces, me=None):
    (out,) = run(
        bind(march_kernel, me),
        (table, outer, own, inner, far, near, faces),
        [((COLUMNS * BACK // PAIRS, PAIRS, 128), F32)],
        [pltpu.VMEM((6 * HALF, ROWS, 128), F32)] * 4
        + [
            pltpu.VMEM((2 * PAIRS * ROWS, 128), F32),
            pltpu.SMEM((6, TABLE), I32),
            pltpu.SemaphoreType.DMA,
        ],
        me,
    )
    return out.reshape(COLUMNS, BACK, 128)


def deliver(counts, returned, me=None):
    (out,) = run(
        bind(deliver_kernel, me),
        (counts, returned.reshape(COLUMNS * BACK, 128)),
        [((CELLS, SLOTS), F32)],
        [pltpu.VMEM((2 * PAIRS, SLOTS, 128), F32)],
        me,
    )
    return out.reshape(TILE, TILE, TILE, SLOTS)


def exchange(x):
    return lax.all_to_all(x, "mem", split_axis=0, concat_axis=0, tiled=True)


def on_device(phi_owned, band_counts, neighbours):
    groups, members = lax.axis_size("grp"), lax.axis_size("mem")
    mates = [(m, m ^ 1) for m in range(members)]
    across = []
    for g in range(groups - 1):
        for m in range(0, members, 2):
            low, high = g * members + m + 1, (g + 1) * members + m
            across += [(low, high), (high, low)]
    received = exchange(pack(band_counts, phi_owned))
    near, faces, table = masks_of(band_counts, neighbours)
    far = lax.ppermute(near, ("grp", "mem"), across)
    received, far = lax.optimization_barrier((received, far))
    own = unpack(table, received)
    outer = lax.ppermute(own, ("grp", "mem"), across)
    inner = lax.ppermute(own, "mem", mates)
    returned = exchange(march(table, outer, own, inner, far, near, faces))
    return deliver(band_counts, returned)


def solution(mesh):
    return jax.shard_map(
        on_device,
        mesh=mesh,
        in_specs=(P(None, None, None, ("grp", "mem")), P("grp", None), P("grp", None, None)),
        out_specs=P(None, None, None, ("grp", "mem")),
        check_vma=False,
    )
```

```python
import functools

import jax
import jax.numpy as jnp
from jax import lax
from jax.experimental import pallas as pl
from jax.experimental.pallas import tpu as pltpu
from jax.sharding import PartitionSpec as P

STEPS = 4
TIME_STEP = 0.5
EPSILON = 1e-06

TILE = 8
ROWS = 32
COLUMNS = 64
SLOTS = 128
CELLS = TILE**3
DEPTH = SLOTS // COLUMNS
WIDE = 16
TABLE = 40
HALF = TILE // 2
PAIRS = HALF // 2
SENT = 3 * DEPTH * PAIRS
BACK = 2 * DEPTH * PAIRS

F32 = jnp.float32
I32 = jnp.int32


def shift(x, amount, axis):
    return pltpu.roll(x, amount % x.shape[axis] if isinstance(amount, int) else amount, axis)


def iota(shape, axis):
    return lax.broadcasted_iota(I32, shape, axis)


def own_start(counts_ref, me):
    total = jnp.int32(0)
    for owner in range(COLUMNS - 1):
        total = total + jnp.where(owner < me, counts_ref[0, owner], 0)
    return total


def plane_of(core, pair, upper):
    w = pair + PAIRS * upper
    return TILE - 1 - w if core else w


def pack_kernel(where_am_i, *refs):
    counts_hbm, phi_hbm, blocks_ref, counts_ref, phi_ref, turned_ref, sems = refs[-7:]
    out_ref = blocks_ref.reshape(COLUMNS * SENT, 128)
    copies = [
        pltpu.make_async_copy(counts_hbm, counts_ref, sems.at[0]),
        pltpu.make_async_copy(phi_hbm, phi_ref, sems.at[1]),
    ]
    for copy in copies:
        copy.start()
    copies[0].wait()
    turn = own_start(counts_ref, where_am_i(refs)) & (COLUMNS - 1)
    copies[1].wait()
    chips = COLUMNS // 2
    upper_x = iota((chips, 128), 1) % TILE >= HALF
    for core in range(2):
        for pair in range(PAIRS):
            blocks = []
            for y in range(TILE):
                for upper in range(2):
                    z = plane_of(core, pair, upper)
                    tiles = phi_ref[pl.ds(y * TILE + z, TILE, stride=TILE * TILE), :]
                    blocks.append(pltpu.roll(tiles, turn, 1))
            turned = jnp.concatenate(blocks, axis=0).T
            held_ref = turned_ref.at[core * PAIRS + pair]
            held_ref[8 : 8 + SLOTS, :] = turned
            held_ref[7:8, :] = turned[SLOTS - 1 :]
            held_ref[8 + SLOTS : 9 + SLOTS, :] = turned[:1]
            for d in range(DEPTH):
                first = 8 + d * COLUMNS
                base = core * SENT + d * PAIRS + pair
                for column in range(2):
                    out_ref[
                        pl.ds(base + column * DEPTH * PAIRS, chips, stride=2 * SENT), :
                    ] = held_ref[pl.ds(first + column, chips, stride=2), :]
                left = held_ref[pl.ds(first - 1, chips, stride=2), :]
                right = held_ref[pl.ds(first + 2, chips, stride=2), :]
                out_ref[pl.ds(base + 2 * DEPTH * PAIRS, chips, stride=2 * SENT), :] = jnp.where(
                    upper_x, left, right
                )


def fill_table(counts_ref, table_ref, column):
    for entry in range(6):
        table_ref[entry, 1] = jnp.int32(0)
        table_ref[entry, ROWS] = jnp.int32(0)

    def body(owner, start):
        turn = start & (COLUMNS - 1)
        for entry, delta in enumerate((0, 1, -1, 2)):
            first = (column + delta - turn) & (COLUMNS - 1)
            row = (start + first - delta) >> 6
            slot = ((first + turn - delta) & (SLOTS - 1)) >> 6
            base = owner * (3 * DEPTH) + min(entry, 2) * DEPTH
            table_ref[entry, row + 1] = base + slot
            table_ref[entry, row + 2] = base + (1 - slot)
            if entry < 2:
                base = owner * (2 * DEPTH) + entry * DEPTH
                table_ref[4 + entry, row + 1] = base + slot
                table_ref[4 + entry, row + 2] = base + (1 - slot)
        return start + counts_ref[0, owner]

    lax.fori_loop(0, COLUMNS, body, jnp.int32(0), unroll=8)


def mask_kernel(where_am_i, *refs):
    counts_ref, links_ref, flat_ref, outer_ref, table_ref, lhs_ref, found_ref = refs[-7:]
    me = where_am_i(refs)
    chip, core = me >> 1, me & 1
    fill_table(counts_ref, table_ref, 2 * chip)
    blocks = ROWS // 2
    for v in range(blocks):
        lhs_ref[v * 8 : v * 8 + 6, :] = jnp.where(
            links_ref[0, :, v * 128 : (v + 1) * 128] >= 0, 1.0, 0.0
        )
        lhs_ref[v * 8 + 6 : v * 8 + 8, :] = jnp.zeros((2, 128), F32)
    source = iota((128, 256), 0)
    target = iota((128, 256), 1)
    x16 = target % WIDE
    lane = iota((ROWS, 128), 1)
    for column in range(2):
        wanted = 2 * chip + column + jnp.where(x16 < 4, -1, jnp.where(x16 >= 12, 1, 0))
        pick = (source % COLUMNS == wanted) & (source // COLUMNS == target // 128)
        found = jnp.dot(
            lhs_ref[...].astype(jnp.bfloat16),
            jnp.where(pick, 1.0, 0.0).astype(jnp.bfloat16),
            preferred_element_type=F32,
        )
        for v in range(blocks):
            for odd in range(2):
                found_ref[pl.ds(2 * v + odd, 8, stride=ROWS), :] = found[
                    v * 8 : v * 8 + 8, odd * 128 : (odd + 1) * 128
                ]
        edge = (lane % WIDE == 3) | (lane % WIDE == 11)
        flat_ref[column] = jnp.where(edge, found_ref[ROWS : 2 * ROWS, :], 1.0)
        flat_ref[2 + column] = jnp.where(lane >= 112, found_ref[3 * ROWS : 4 * ROWS, :], 1.0)
        outer_ref[column] = jnp.where(
            core == 0, found_ref[4 * ROWS : 5 * ROWS, :], found_ref[5 * ROWS : 6 * ROWS, :]
        )


def unpack_kernel(table_ref, received_ref, planes_ref, packed_ref):
    for r in range(ROWS):
        for entry in range(4):
            packed_ref[pl.ds(entry * PAIRS * ROWS + r, PAIRS, stride=ROWS), :] = received_ref[
                table_ref[entry, r + 1]
            ]
    lane = iota((ROWS, 128), 1)
    x16 = lane % WIDE
    for pair in range(PAIRS):
        first, second, left, right = (
            packed_ref[(entry * PAIRS + pair) * ROWS : (entry * PAIRS + pair + 1) * ROWS, :]
            for entry in range(4)
        )
        outside = jnp.where(lane % TILE >= HALF, left, right)

        def join(left, here, right):
            return jnp.where(x16 < 4, left, jnp.where(x16 >= 12, right, here))

        second_4 = shift(second, 4, 1)
        first_m4 = shift(first, -4, 1)
        planes_ref[pair] = join(shift(outside, -4, 1), shift(first, 4, 1), shift(second, 12, 1))
        planes_ref[PAIRS + pair] = join(shift(outside, -12, 1), first_m4, second_4)
        planes_ref[HALF + pair] = join(first_m4, second_4, shift(outside, 12, 1))
        planes_ref[HALF + PAIRS + pair] = join(
            shift(first, -12, 1), shift(second, -4, 1), shift(outside, 4, 1)
        )


def march_kernel(where_am_i, *refs):
    (
        table_vmem,
        outer_ref,
        own_ref,
        inner_ref,
        far_ref,
        near_ref,
        faces_ref,
        out_ref,
        even_ref,
        odd_ref,
        pull_ref,
        side_ref,
        done_ref,
        table_ref,
        sem,
    ) = refs[-15:]
    here = where_am_i(refs)
    fetch = pltpu.make_async_copy(table_vmem, table_ref, sem)
    fetch.start()
    depth = 3 * HALF
    lane = iota((ROWS, 128), 1)
    first_y = lane < WIDE
    last_y = lane >= 128 - WIDE

    def start(column, p):
        base = column * HALF
        if p < HALF:
            return outer_ref[base + HALF - 1 - p]
        if p < 2 * HALF:
            return own_ref[base + p - HALF]
        return inner_ref[base + depth - 1 - p]

    def load(step, column, p):
        if step == 0:
            return start(column, p)
        return (odd_ref if step % 2 else even_ref)[column * depth + p]

    def one_step(step, column, lo, hi):
        target_ref = even_ref if step % 2 else odd_ref
        level = load(step, column, lo - 1)
        after = load(step, column, lo)
        ahead_z = after - level
        if lo == HALF:
            ahead_z = ahead_z * faces_ref[column]
        for p in range(lo, hi):
            back_z = ahead_z
            level = after
            after = load(step, column, p + 1)
            ahead_z = after - level
            if p == HALF - 1:
                ahead_z = ahead_z * faces_ref[column]
            links = far_ref if p < HALF else near_ref
            if step == 0:
                sign_field = level * lax.rsqrt(level * level + 1.0)
                pull = TIME_STEP * sign_field
                up = jnp.where(sign_field > 0, 1.0, -1.0)
                pull_ref[column * depth + p] = pull
                side_ref[column * depth + p] = up
            else:
                pull = pull_ref[column * depth + p]
                up = side_ref[column * depth + p]
            down = -up
            ahead = (shift(level, -1, 1) - level) * links[column]
            back = shift(ahead, 1, 1)
            squares = jnp.square(jnp.maximum(jnp.maximum(up * back, down * ahead), 0.0))
            beyond = jnp.where(first_y, shift(level, -1, 0), level)
            ahead = (shift(beyond, -WIDE, 1) - level) * links[2 + column]
            back = shift(jnp.where(last_y, shift(ahead, 1, 0), ahead), WIDE, 1)
            squares = squares + jnp.square(
                jnp.maximum(jnp.maximum(up * back, down * ahead), 0.0)
            )
            squares = squares + jnp.square(
                jnp.maximum(jnp.maximum(up * back_z, down * ahead_z), 0.0)
            )
            length = squares + EPSILON
            target_ref[column * depth + p] = level - pull * (
                length * lax.rsqrt(length) - 1.0
            )

    spans = ((1, 11), (2, 10), (3, 9), (4, 8))

    def several(steps, columns):
        for step in steps:
            for column in columns:
                one_step(step, column, *spans[step])

    for block, (steps, columns) in enumerate((((0,), (0,)), ((0,), (1,)), ((1,), (0,)), ((1,), (1,)), ((2,), (0,)), ((2,), (1,)), ((3,), (0, 1)))):
        pl.when(here > -1 - block)(functools.partial(several, steps, columns))
    lower = lane % WIDE < TILE
    for column in range(2):
        for pair in range(PAIRS):
            p = column * depth + HALF + pair
            row = (column * PAIRS + pair) * ROWS
            done_ref[row : row + ROWS, :] = jnp.where(
                lower, shift(even_ref[p], -4, 1), shift(even_ref[p + PAIRS], 4, 1)
            )
    fetch.wait()
    for r in range(ROWS):
        for column in range(2):
            out_ref[table_ref[4 + column, r + 1]] = done_ref[
                pl.ds(column * PAIRS * ROWS + r, PAIRS, stride=ROWS), :
            ]


def deliver_kernel(where_am_i, *refs):
    counts_ref, returned_ref, out_ref, turned_ref = refs[-4:]
    me = where_am_i(refs)
    counts = counts_ref[...]
    owner = iota((1, COLUMNS), 1)
    turn = jnp.sum(jnp.where(owner < me, counts, 0)) & (COLUMNS - 1)
    live = iota((SLOTS, SLOTS), 1) < jnp.sum(jnp.where(owner == me, counts, 0))
    chips = COLUMNS // 2
    for core in range(2):
        for pair in range(PAIRS):
            held_ref = turned_ref.at[core * PAIRS + pair]
            for d in range(DEPTH):
                for column in range(2):
                    row = core * BACK + (column * DEPTH + d) * PAIRS + pair
                    held_ref[pl.ds(d * COLUMNS + column, chips, stride=2), :] = returned_ref[
                        pl.ds(row, chips, stride=2 * BACK), :
                    ]
            turned = pltpu.roll(held_ref[...].T, (SLOTS - turn) & (SLOTS - 1), 1)
            turned = jnp.where(live, turned, 0.0)
            for y in range(TILE):
                for upper in range(2):
                    row = y * WIDE + upper * TILE
                    z = plane_of(core, pair, upper)
                    out_ref[pl.ds(y * TILE + z, TILE, stride=TILE * TILE), :] = turned[
                        row : row + TILE
                    ]


def spec(space=pltpu.VMEM):
    return pl.BlockSpec(memory_space=space)


def run(
    kernel, operands, shapes, scratch, me=None, spaces=None, out_spaces=None, cost=(0, 0), grant=32, kinds=None
):
    spaces = spaces or [pltpu.VMEM] * len(operands)
    out_spaces = out_spaces or [pltpu.VMEM] * len(shapes)
    if me is not None:
        operands = (me, *operands)
        spaces = [pltpu.SMEM, *spaces]
    out = pl.pallas_call(
        kernel,
        out_shape=[o(s, t) for (s, t), o in zip(shapes, kinds or [jax.ShapeDtypeStruct] * len(shapes))],
        in_specs=[spec(s) for s in spaces],
        out_specs=[spec(s) for s in out_spaces],
        scratch_shapes=scratch,
        compiler_params=pltpu.CompilerParams(vmem_limit_bytes=grant << 20),
        cost_estimate=pl.CostEstimate(flops=cost[0], bytes_accessed=cost[1], transcendentals=0),
        name=getattr(kernel, "func", kernel).__name__,
    )(*operands)
    return out


def position(refs):
    return lax.axis_index("mem")


def given(refs):
    return refs[0][0]


def bind(kernel, me):
    return functools.partial(kernel, position if me is None else given)


def pack(counts, phi, me=None):
    (out,) = run(
        bind(pack_kernel, me),
        (
            pltpu.with_memory_space_constraint(counts, pltpu.HBM),
            pltpu.with_memory_space_constraint(phi.reshape(CELLS, SLOTS), pltpu.HBM),
        ),
        [((COLUMNS * SENT // 4, 4, 128), F32)],
        [
            pltpu.SMEM((1, COLUMNS), I32),
            pltpu.VMEM((CELLS, SLOTS), F32),
            pltpu.VMEM((2 * PAIRS, SLOTS + 16, 128), F32),
            pltpu.SemaphoreType.DMA((2,)),
        ],
        me,
        [pltpu.HBM, pltpu.HBM],
        grant=32,
        kinds=[pltpu.VMEM],
    )
    return out


def masks_of(counts, neighbours, me=None):
    return run(
        bind(mask_kernel, me),
        (counts, neighbours),
        [((4, ROWS, 128), F32), ((2, ROWS, 128), F32), ((6, TABLE), I32)],
        [pltpu.VMEM((128, 128), F32), pltpu.VMEM((8 * ROWS, 128), F32)],
        me,
        [pltpu.SMEM, pltpu.VMEM],
        [pltpu.VMEM, pltpu.VMEM, pltpu.SMEM],
        cost=(1 << 22, 1 << 17),
    )


def unpack(table, received):
    (out,) = run(
        unpack_kernel,
        (table, received.reshape(COLUMNS * SENT // PAIRS, PAIRS, 128)),
        [((TILE, ROWS, 128), F32)],
        [pltpu.VMEM((4 * PAIRS * ROWS, 128), F32)],
        None,
        [pltpu.SMEM, pltpu.VMEM],
    )
    return out


def march(table, outer, own, inner, far, near, faces, me=None):
    (out,) = run(
        bind(march_kernel, me),
        (table, outer, own, inner, far, near, faces),
        [((COLUMNS * BACK // PAIRS, PAIRS, 128), F32)],
        [pltpu.VMEM((6 * HALF, ROWS, 128), F32)] * 4
        + [
            pltpu.VMEM((2 * PAIRS * ROWS, 128), F32),
            pltpu.SMEM((6, TABLE), I32),
            pltpu.SemaphoreType.DMA,
        ],
        me,
    )
    return out.reshape(COLUMNS, BACK, 128)


def deliver(counts, returned, me=None):
    (out,) = run(
        bind(deliver_kernel, me),
        (counts, returned.reshape(COLUMNS * BACK, 128)),
        [((CELLS, SLOTS), F32)],
        [pltpu.VMEM((2 * PAIRS, SLOTS, 128), F32)],
        me,
    )
    return out.reshape(TILE, TILE, TILE, SLOTS)


def exchange(x):
    return lax.all_to_all(x, "mem", split_axis=0, concat_axis=0, tiled=True)


def on_device(phi_owned, band_counts, neighbours):
    groups, members = lax.axis_size("grp"), lax.axis_size("mem")
    mates = [(m, m ^ 1) for m in range(members)]
    across = []
    for g in range(groups - 1):
        for m in range(0, members, 2):
            low, high = g * members + m + 1, (g + 1) * members + m
            across += [(low, high), (high, low)]
    received = exchange(pack(band_counts, phi_owned))
    near, faces, table = masks_of(band_counts, neighbours)
    far = lax.ppermute(near, ("grp", "mem"), across)
    received, far = lax.optimization_barrier((received, far))
    own = unpack(table, received)
    outer = lax.ppermute(own, ("grp", "mem"), across)
    inner = lax.ppermute(own, "mem", mates)
    returned = exchange(march(table, outer, own, inner, far, near, faces))
    return deliver(band_counts, returned)


def solution(mesh):
    return jax.shard_map(
        on_device,
        mesh=mesh,
        in_specs=(P(None, None, None, ("grp", "mem")), P("grp", None), P("grp", None, None)),
        out_specs=P(None, None, None, ("grp", "mem")),
        check_vma=False,
    )
```

```python
import functools

import jax
import jax.numpy as jnp
from jax import lax
from jax.experimental import pallas as pl
from jax.experimental.pallas import tpu as pltpu
from jax.sharding import PartitionSpec as P

STEPS = 4
TIME_STEP = 0.5
EPSILON = 1e-06

TILE = 8
ROWS = 32
COLUMNS = 64
SLOTS = 128
CELLS = TILE**3
DEPTH = SLOTS // COLUMNS
WIDE = 16
TABLE = 40
HALF = TILE // 2
PAIRS = HALF // 2
SENT = 3 * DEPTH * PAIRS
BACK = 2 * DEPTH * PAIRS

F32 = jnp.float32
I32 = jnp.int32


def shift(x, amount, axis):
    return pltpu.roll(x, amount % x.shape[axis] if isinstance(amount, int) else amount, axis)


def iota(shape, axis):
    return lax.broadcasted_iota(I32, shape, axis)


def own_start(counts_ref, me):
    total = jnp.int32(0)
    for owner in range(COLUMNS - 1):
        total = total + jnp.where(owner < me, counts_ref[0, owner], 0)
    return total


def plane_of(core, pair, upper):
    w = pair + PAIRS * upper
    return TILE - 1 - w if core else w


def pack_kernel(where_am_i, *refs):
    counts_hbm, phi_hbm, out_ref, counts_ref, phi_ref, turned_ref, sems = refs[-7:]
    copies = [
        pltpu.make_async_copy(counts_hbm, counts_ref, sems.at[0]),
        pltpu.make_async_copy(phi_hbm, phi_ref, sems.at[1]),
    ]
    for copy in copies:
        copy.start()
    copies[0].wait()
    turn = own_start(counts_ref, where_am_i(refs)) & (COLUMNS - 1)
    copies[1].wait()
    chips = COLUMNS // 2
    upper_x = iota((chips, 128), 1) % TILE >= HALF
    for core in range(2):
        for pair in range(PAIRS):
            blocks = []
            for y in range(TILE):
                for upper in range(2):
                    z = plane_of(core, pair, upper)
                    tiles = phi_ref[pl.ds(y * TILE + z, TILE, stride=TILE * TILE), :]
                    blocks.append(pltpu.roll(tiles, turn, 1))
            turned = jnp.concatenate(blocks, axis=0).T
            held_ref = turned_ref.at[core * PAIRS + pair]
            held_ref[8 : 8 + SLOTS, :] = turned
            held_ref[7:8, :] = turned[SLOTS - 1 :]
            held_ref[8 + SLOTS : 9 + SLOTS, :] = turned[:1]
            for d in range(DEPTH):
                first = 8 + d * COLUMNS
                base = core * SENT + d * PAIRS + pair
                for column in range(2):
                    out_ref[
                        pl.ds(base + column * DEPTH * PAIRS, chips, stride=2 * SENT), :
                    ] = held_ref[pl.ds(first + column, chips, stride=2), :]
                left = held_ref[pl.ds(first - 1, chips, stride=2), :]
                right = held_ref[pl.ds(first + 2, chips, stride=2), :]
                out_ref[pl.ds(base + 2 * DEPTH * PAIRS, chips, stride=2 * SENT), :] = jnp.where(
                    upper_x, left, right
                )


def fill_table(counts_ref, table_ref, column):
    for entry in range(6):
        table_ref[entry, 1] = jnp.int32(0)
        table_ref[entry, ROWS] = jnp.int32(0)

    def body(owner, start):
        turn = start & (COLUMNS - 1)
        for entry, delta in enumerate((0, 1, -1, 2)):
            first = (column + delta - turn) & (COLUMNS - 1)
            row = (start + first - delta) >> 6
            slot = ((first + turn - delta) & (SLOTS - 1)) >> 6
            base = owner * (3 * DEPTH) + min(entry, 2) * DEPTH
            table_ref[entry, row + 1] = base + slot
            table_ref[entry, row + 2] = base + (1 - slot)
            if entry < 2:
                base = owner * (2 * DEPTH) + entry * DEPTH
                table_ref[4 + entry, row + 1] = base + slot
                table_ref[4 + entry, row + 2] = base + (1 - slot)
        return start + counts_ref[0, owner]

    lax.fori_loop(0, COLUMNS, body, jnp.int32(0), unroll=8)


def mask_kernel(where_am_i, *refs):
    counts_ref, links_ref, flat_ref, outer_ref, table_ref, lhs_ref, found_ref = refs[-7:]
    me = where_am_i(refs)
    chip, core = me >> 1, me & 1
    fill_table(counts_ref, table_ref, 2 * chip)
    blocks = ROWS // 2
    for v in range(blocks):
        lhs_ref[v * 8 : v * 8 + 6, :] = jnp.where(
            links_ref[0, :, v * 128 : (v + 1) * 128] >= 0, 1.0, 0.0
        )
        lhs_ref[v * 8 + 6 : v * 8 + 8, :] = jnp.zeros((2, 128), F32)
    source = iota((128, 256), 0)
    target = iota((128, 256), 1)
    x16 = target % WIDE
    lane = iota((ROWS, 128), 1)
    for column in range(2):
        wanted = 2 * chip + column + jnp.where(x16 < 4, -1, jnp.where(x16 >= 12, 1, 0))
        pick = (source % COLUMNS == wanted) & (source // COLUMNS == target // 128)
        found = jnp.dot(
            lhs_ref[...].astype(jnp.bfloat16),
            jnp.where(pick, 1.0, 0.0).astype(jnp.bfloat16),
            preferred_element_type=F32,
        )
        for v in range(blocks):
            for odd in range(2):
                found_ref[pl.ds(2 * v + odd, 8, stride=ROWS), :] = found[
                    v * 8 : v * 8 + 8, odd * 128 : (odd + 1) * 128
                ]
        edge = (lane % WIDE == 3) | (lane % WIDE == 11)
        flat_ref[column] = jnp.where(edge, found_ref[ROWS : 2 * ROWS, :], 1.0)
        flat_ref[2 + column] = jnp.where(lane >= 112, found_ref[3 * ROWS : 4 * ROWS, :], 1.0)
        outer_ref[column] = jnp.where(
            core == 0, found_ref[4 * ROWS : 5 * ROWS, :], found_ref[5 * ROWS : 6 * ROWS, :]
        )


def unpack_kernel(table_ref, received_ref, planes_ref, packed_ref):
    for r in range(ROWS):
        for entry in range(4):
            packed_ref[pl.ds(entry * PAIRS * ROWS + r, PAIRS, stride=ROWS), :] = received_ref[
                table_ref[entry, r + 1]
            ]
    lane = iota((ROWS, 128), 1)
    x16 = lane % WIDE
    for pair in range(PAIRS):
        first, second, left, right = (
            packed_ref[(entry * PAIRS + pair) * ROWS : (entry * PAIRS + pair + 1) * ROWS, :]
            for entry in range(4)
        )
        outside = jnp.where(lane % TILE >= HALF, left, right)

        def join(left, here, right):
            return jnp.where(x16 < 4, left, jnp.where(x16 >= 12, right, here))

        second_4 = shift(second, 4, 1)
        first_m4 = shift(first, -4, 1)
        planes_ref[pair] = join(shift(outside, -4, 1), shift(first, 4, 1), shift(second, 12, 1))
        planes_ref[PAIRS + pair] = join(shift(outside, -12, 1), first_m4, second_4)
        planes_ref[HALF + pair] = join(first_m4, second_4, shift(outside, 12, 1))
        planes_ref[HALF + PAIRS + pair] = join(
            shift(first, -12, 1), shift(second, -4, 1), shift(outside, 4, 1)
        )


def march_kernel(where_am_i, *refs):
    (
        table_ref,
        outer_ref,
        own_ref,
        inner_ref,
        far_ref,
        near_ref,
        faces_ref,
        out_ref,
        even_ref,
        odd_ref,
        pull_ref,
        side_ref,
        done_ref,
    ) = refs[-13:]
    here = where_am_i(refs)
    depth = 3 * HALF
    lane = iota((ROWS, 128), 1)
    first_y = lane < WIDE
    last_y = lane >= 128 - WIDE

    def start(column, p):
        base = column * HALF
        if p < HALF:
            return outer_ref[base + HALF - 1 - p]
        if p < 2 * HALF:
            return own_ref[base + p - HALF]
        return inner_ref[base + depth - 1 - p]

    def load(step, column, p):
        if step == 0:
            return start(column, p)
        return (odd_ref if step % 2 else even_ref)[column * depth + p]

    def one_step(step, column, lo, hi):
        target_ref = even_ref if step % 2 else odd_ref
        level = load(step, column, lo - 1)
        after = load(step, column, lo)
        ahead_z = after - level
        if lo == HALF:
            ahead_z = ahead_z * faces_ref[column]
        for p in range(lo, hi):
            back_z = ahead_z
            level = after
            after = load(step, column, p + 1)
            ahead_z = after - level
            if p == HALF - 1:
                ahead_z = ahead_z * faces_ref[column]
            links = far_ref if p < HALF else near_ref
            if step == 0:
                sign_field = level * lax.rsqrt(level * level + 1.0)
                pull = TIME_STEP * sign_field
                up = jnp.where(sign_field > 0, 1.0, -1.0)
                pull_ref[column * depth + p] = pull
                side_ref[column * depth + p] = up
            else:
                pull = pull_ref[column * depth + p]
                up = side_ref[column * depth + p]
            down = -up
            ahead = (shift(level, -1, 1) - level) * links[column]
            back = shift(ahead, 1, 1)
            squares = jnp.square(jnp.maximum(jnp.maximum(up * back, down * ahead), 0.0))
            beyond = jnp.where(first_y, shift(level, -1, 0), level)
            ahead = (shift(beyond, -WIDE, 1) - level) * links[2 + column]
            back = shift(jnp.where(last_y, shift(ahead, 1, 0), ahead), WIDE, 1)
            squares = squares + jnp.square(
                jnp.maximum(jnp.maximum(up * back, down * ahead), 0.0)
            )
            squares = squares + jnp.square(
                jnp.maximum(jnp.maximum(up * back_z, down * ahead_z), 0.0)
            )
            length = squares + EPSILON
            target_ref[column * depth + p] = level - pull * (
                length * lax.rsqrt(length) - 1.0
            )

    spans = ((1, 11), (2, 10), (3, 9), (4, 8))

    def several(steps, columns):
        for step in steps:
            for column in columns:
                one_step(step, column, *spans[step])

    for block, (steps, columns) in enumerate((((0,), (0,)), ((0,), (1,)), ((1,), (0,)), ((1,), (1,)), ((2,), (0,)), ((2,), (1,)), ((3,), (0, 1)))):
        pl.when(here > -1 - block)(functools.partial(several, steps, columns))
    lower = lane % WIDE < TILE
    for column in range(2):
        for pair in range(PAIRS):
            p = column * depth + HALF + pair
            row = (column * PAIRS + pair) * ROWS
            done_ref[row : row + ROWS, :] = jnp.where(
                lower, shift(even_ref[p], -4, 1), shift(even_ref[p + PAIRS], 4, 1)
            )
    for r in range(ROWS):
        for column in range(2):
            out_ref[table_ref[4 + column, r + 1]] = done_ref[
                pl.ds(column * PAIRS * ROWS + r, PAIRS, stride=ROWS), :
            ]


def deliver_kernel(where_am_i, *refs):
    counts_ref, returned_ref, out_ref, turned_ref = refs[-4:]
    me = where_am_i(refs)
    counts = counts_ref[...]
    owner = iota((1, COLUMNS), 1)
    turn = jnp.sum(jnp.where(owner < me, counts, 0)) & (COLUMNS - 1)
    live = iota((SLOTS, SLOTS), 1) < jnp.sum(jnp.where(owner == me, counts, 0))
    chips = COLUMNS // 2
    for core in range(2):
        for pair in range(PAIRS):
            held_ref = turned_ref.at[core * PAIRS + pair]
            for d in range(DEPTH):
                for column in range(2):
                    row = core * BACK + (column * DEPTH + d) * PAIRS + pair
                    held_ref[pl.ds(d * COLUMNS + column, chips, stride=2), :] = returned_ref[
                        pl.ds(row, chips, stride=2 * BACK), :
                    ]
            turned = pltpu.roll(held_ref[...].T, (SLOTS - turn) & (SLOTS - 1), 1)
            turned = jnp.where(live, turned, 0.0)
            for y in range(TILE):
                for upper in range(2):
                    row = y * WIDE + upper * TILE
                    z = plane_of(core, pair, upper)
                    out_ref[pl.ds(y * TILE + z, TILE, stride=TILE * TILE), :] = turned[
                        row : row + TILE
                    ]


def spec(space=pltpu.VMEM):
    return pl.BlockSpec(memory_space=space)


def run(
    kernel, operands, shapes, scratch, me=None, spaces=None, out_spaces=None, cost=(0, 0), grant=32
):
    spaces = spaces or [pltpu.VMEM] * len(operands)
    out_spaces = out_spaces or [pltpu.VMEM] * len(shapes)
    if me is not None:
        operands = (me, *operands)
        spaces = [pltpu.SMEM, *spaces]
    out = pl.pallas_call(
        kernel,
        out_shape=[
            (pltpu.SMEM if space == pltpu.SMEM else jax.ShapeDtypeStruct)(*shape)
            for shape, space in zip(shapes, out_spaces)
        ],
        in_specs=[spec(s) for s in spaces],
        out_specs=[spec(s) for s in out_spaces],
        scratch_shapes=scratch,
        compiler_params=pltpu.CompilerParams(vmem_limit_bytes=grant << 20),
        cost_estimate=pl.CostEstimate(flops=cost[0], bytes_accessed=cost[1], transcendentals=0),
        name=getattr(kernel, "func", kernel).__name__,
    )(*operands)
    return out


def position(refs):
    return lax.axis_index("mem")


def given(refs):
    return refs[0][0]


def bind(kernel, me):
    return functools.partial(kernel, position if me is None else given)


def pack(counts, phi, me=None):
    (out,) = run(
        bind(pack_kernel, me),
        (counts, phi.reshape(CELLS, SLOTS)),
        [((COLUMNS * SENT, 128), F32)],
        [
            pltpu.SMEM((1, COLUMNS), I32),
            pltpu.VMEM((CELLS, SLOTS), F32),
            pltpu.VMEM((2 * PAIRS, SLOTS + 16, 128), F32),
            pltpu.SemaphoreType.DMA((2,)),
        ],
        me,
        [pltpu.HBM, pltpu.HBM],
        grant=62,
    )
    return out.reshape(COLUMNS * SENT // 4, 4, 128)


def masks_of(counts, neighbours, me=None):
    return run(
        bind(mask_kernel, me),
        (counts, neighbours),
        [((4, ROWS, 128), F32), ((2, ROWS, 128), F32), ((6, TABLE), I32)],
        [pltpu.VMEM((128, 128), F32), pltpu.VMEM((8 * ROWS, 128), F32)],
        me,
        [pltpu.SMEM, pltpu.VMEM],
        [pltpu.VMEM, pltpu.VMEM, pltpu.SMEM],
        cost=(1 << 22, 1 << 17),
    )


def unpack(table, received):
    (out,) = run(
        unpack_kernel,
        (pltpu.with_memory_space_constraint(table, pltpu.SMEM), received.reshape(COLUMNS * SENT // PAIRS, PAIRS, 128)),
        [((TILE, ROWS, 128), F32)],
        [pltpu.VMEM((4 * PAIRS * ROWS, 128), F32)],
        None,
        [pltpu.SMEM, pltpu.VMEM],
    )
    return out


def march(table, outer, own, inner, far, near, faces, me=None):
    (out,) = run(
        bind(march_kernel, me),
        (pltpu.with_memory_space_constraint(table, pltpu.SMEM), outer, own, inner, far, near, faces),
        [((COLUMNS * BACK // PAIRS, PAIRS, 128), F32)],
        [pltpu.VMEM((6 * HALF, ROWS, 128), F32)] * 4
        + [
            pltpu.VMEM((2 * PAIRS * ROWS, 128), F32),
        ],
        me,
        [pltpu.SMEM] + [pltpu.VMEM] * 6,
    )
    return out.reshape(COLUMNS, BACK, 128)


def deliver(counts, returned, me=None):
    (out,) = run(
        bind(deliver_kernel, me),
        (counts, returned.reshape(COLUMNS * BACK, 128)),
        [((CELLS, SLOTS), F32)],
        [pltpu.VMEM((2 * PAIRS, SLOTS, 128), F32)],
        me,
    )
    return out.reshape(TILE, TILE, TILE, SLOTS)


def exchange(x):
    return lax.all_to_all(x, "mem", split_axis=0, concat_axis=0, tiled=True)


def on_device(phi_owned, band_counts, neighbours):
    groups, members = lax.axis_size("grp"), lax.axis_size("mem")
    mates = [(m, m ^ 1) for m in range(members)]
    across = []
    for g in range(groups - 1):
        for m in range(0, members, 2):
            low, high = g * members + m + 1, (g + 1) * members + m
            across += [(low, high), (high, low)]
    received = exchange(pack(band_counts, phi_owned))
    near, faces, table = masks_of(band_counts, neighbours)
    far = lax.ppermute(near, ("grp", "mem"), across)
    received, far = lax.optimization_barrier((received, far))
    own = unpack(table, received)
    outer = lax.ppermute(own, ("grp", "mem"), across)
    inner = lax.ppermute(own, "mem", mates)
    returned = exchange(march(table, outer, own, inner, far, near, faces))
    return deliver(band_counts, returned)


def solution(mesh):
    return jax.shard_map(
        on_device,
        mesh=mesh,
        in_specs=(P(None, None, None, ("grp", "mem")), P("grp", None), P("grp", None, None)),
        out_specs=P(None, None, None, ("grp", "mem")),
        check_vma=False,
    )
```

```python
import functools

import jax
import jax.numpy as jnp
from jax import lax
from jax.experimental import pallas as pl
from jax.experimental.pallas import tpu as pltpu
from jax.sharding import PartitionSpec as P

STEPS = 4
TIME_STEP = 0.5
EPSILON = 1e-06

TILE = 8
ROWS = 32
COLUMNS = 64
SLOTS = 128
CELLS = TILE**3
DEPTH = SLOTS // COLUMNS
WIDE = 16
TABLE = 40
HALF = TILE // 2
PAIRS = HALF // 2
SENT = 3 * DEPTH * PAIRS
BACK = 2 * DEPTH * PAIRS

F32 = jnp.float32
I32 = jnp.int32


def shift(x, amount, axis):
    return pltpu.roll(x, amount % x.shape[axis] if isinstance(amount, int) else amount, axis)


def iota(shape, axis):
    return lax.broadcasted_iota(I32, shape, axis)


def own_start(counts_ref, me):
    total = jnp.int32(0)
    for owner in range(COLUMNS - 1):
        total = total + jnp.where(owner < me, counts_ref[0, owner], 0)
    return total


def plane_of(core, pair, upper):
    w = pair + PAIRS * upper
    return TILE - 1 - w if core else w


def pack_kernel(where_am_i, *refs):
    counts_hbm, phi_hbm, out_ref, counts_ref, phi_ref, turned_ref, sems = refs[-7:]
    copies = [
        pltpu.make_async_copy(counts_hbm, counts_ref, sems.at[0]),
        pltpu.make_async_copy(phi_hbm, phi_ref, sems.at[1]),
    ]
    for copy in copies:
        copy.start()
    copies[0].wait()
    turn = own_start(counts_ref, where_am_i(refs)) & (COLUMNS - 1)
    copies[1].wait()
    chips = COLUMNS // 2
    upper_x = iota((chips, 128), 1) % TILE >= HALF
    for core in range(2):
        for pair in range(PAIRS):
            blocks = []
            for y in range(TILE):
                for upper in range(2):
                    z = plane_of(core, pair, upper)
                    tiles = phi_ref[pl.ds(y * TILE + z, TILE, stride=TILE * TILE), :]
                    blocks.append(pltpu.roll(tiles, turn, 1))
            turned = jnp.concatenate(blocks, axis=0).T
            held_ref = turned_ref.at[core * PAIRS + pair]
            held_ref[8 : 8 + SLOTS, :] = turned
            held_ref[7:8, :] = turned[SLOTS - 1 :]
            held_ref[8 + SLOTS : 9 + SLOTS, :] = turned[:1]
            for d in range(DEPTH):
                first = 8 + d * COLUMNS
                base = core * SENT + d * PAIRS + pair
                for column in range(2):
                    out_ref[
                        pl.ds(base + column * DEPTH * PAIRS, chips, stride=2 * SENT), :
                    ] = held_ref[pl.ds(first + column, chips, stride=2), :]
                left = held_ref[pl.ds(first - 1, chips, stride=2), :]
                right = held_ref[pl.ds(first + 2, chips, stride=2), :]
                out_ref[pl.ds(base + 2 * DEPTH * PAIRS, chips, stride=2 * SENT), :] = jnp.where(
                    upper_x, left, right
                )


def fill_table(counts_ref, table_ref, column):
    for entry in range(6):
        table_ref[entry, 1] = jnp.int32(0)
        table_ref[entry, ROWS] = jnp.int32(0)

    def body(owner, start):
        turn = start & (COLUMNS - 1)
        for entry, delta in enumerate((0, 1, -1, 2)):
            first = (column + delta - turn) & (COLUMNS - 1)
            row = (start + first - delta) >> 6
            slot = ((first + turn - delta) & (SLOTS - 1)) >> 6
            base = owner * (3 * DEPTH) + min(entry, 2) * DEPTH
            table_ref[entry, row + 1] = base + slot
            table_ref[entry, row + 2] = base + (1 - slot)
            if entry < 2:
                base = owner * (2 * DEPTH) + entry * DEPTH
                table_ref[4 + entry, row + 1] = base + slot
                table_ref[4 + entry, row + 2] = base + (1 - slot)
        return start + counts_ref[0, owner]

    lax.fori_loop(0, COLUMNS, body, jnp.int32(0), unroll=8)


def mask_kernel(where_am_i, *refs):
    counts_ref, links_ref, flat_ref, outer_ref, table_ref, lhs_ref, found_ref = refs[-7:]
    me = where_am_i(refs)
    chip, core = me >> 1, me & 1
    fill_table(counts_ref, table_ref, 2 * chip)
    blocks = ROWS // 2
    for v in range(blocks):
        lhs_ref[v * 8 : v * 8 + 6, :] = jnp.where(
            links_ref[0, :, v * 128 : (v + 1) * 128] >= 0, 1.0, 0.0
        )
        lhs_ref[v * 8 + 6 : v * 8 + 8, :] = jnp.zeros((2, 128), F32)
    source = iota((128, 256), 0)
    target = iota((128, 256), 1)
    x16 = target % WIDE
    lane = iota((ROWS, 128), 1)
    for column in range(2):
        wanted = 2 * chip + column + jnp.where(x16 < 4, -1, jnp.where(x16 >= 12, 1, 0))
        pick = (source % COLUMNS == wanted) & (source // COLUMNS == target // 128)
        found = jnp.dot(
            lhs_ref[...].astype(jnp.bfloat16),
            jnp.where(pick, 1.0, 0.0).astype(jnp.bfloat16),
            preferred_element_type=F32,
        )
        for v in range(blocks):
            for odd in range(2):
                found_ref[pl.ds(2 * v + odd, 8, stride=ROWS), :] = found[
                    v * 8 : v * 8 + 8, odd * 128 : (odd + 1) * 128
                ]
        edge = (lane % WIDE == 3) | (lane % WIDE == 11)
        flat_ref[column] = jnp.where(edge, found_ref[ROWS : 2 * ROWS, :], 1.0)
        flat_ref[2 + column] = jnp.where(lane >= 112, found_ref[3 * ROWS : 4 * ROWS, :], 1.0)
        outer_ref[column] = jnp.where(
            core == 0, found_ref[4 * ROWS : 5 * ROWS, :], found_ref[5 * ROWS : 6 * ROWS, :]
        )


def unpack_kernel(table_ref, received_ref, planes_ref, packed_ref):
    for r in range(ROWS):
        for entry in range(4):
            packed_ref[pl.ds(entry * PAIRS * ROWS + r, PAIRS, stride=ROWS), :] = received_ref[
                table_ref[entry, r + 1]
            ]
    lane = iota((ROWS, 128), 1)
    x16 = lane % WIDE
    for pair in range(PAIRS):
        first, second, left, right = (
            packed_ref[(entry * PAIRS + pair) * ROWS : (entry * PAIRS + pair + 1) * ROWS, :]
            for entry in range(4)
        )
        outside = jnp.where(lane % TILE >= HALF, left, right)

        def join(left, here, right):
            return jnp.where(x16 < 4, left, jnp.where(x16 >= 12, right, here))

        second_4 = shift(second, 4, 1)
        first_m4 = shift(first, -4, 1)
        planes_ref[pair] = join(shift(outside, -4, 1), shift(first, 4, 1), shift(second, 12, 1))
        planes_ref[PAIRS + pair] = join(shift(outside, -12, 1), first_m4, second_4)
        planes_ref[HALF + pair] = join(first_m4, second_4, shift(outside, 12, 1))
        planes_ref[HALF + PAIRS + pair] = join(
            shift(first, -12, 1), shift(second, -4, 1), shift(outside, 4, 1)
        )


EARLY = HALF + 1
EARLY_PLANES = TILE - 2


def stepper(load, keep, signs, links, faces_ref):
    lane = iota((ROWS, 128), 1)
    first_y = lane < WIDE
    last_y = lane >= 128 - WIDE

    def one_step(step, column, lo, hi):
        level = load(step, column, lo - 1)
        after = load(step, column, lo)
        ahead_z = after - level
        if lo == HALF:
            ahead_z = ahead_z * faces_ref[column]
        for p in range(lo, hi):
            back_z = ahead_z
            level = after
            after = load(step, column, p + 1)
            ahead_z = after - level
            if p == HALF - 1:
                ahead_z = ahead_z * faces_ref[column]
            pull_ref, side_ref, at = signs(column, p)
            if step == 0:
                sign_field = level * lax.rsqrt(level * level + 1.0)
                pull = TIME_STEP * sign_field
                up = jnp.where(sign_field > 0, 1.0, -1.0)
                pull_ref[at] = pull
                side_ref[at] = up
            else:
                pull = pull_ref[at]
                up = side_ref[at]
            down = -up
            ahead = (shift(level, -1, 1) - level) * links(p)[column]
            back = shift(ahead, 1, 1)
            squares = jnp.square(jnp.maximum(jnp.maximum(up * back, down * ahead), 0.0))
            beyond = jnp.where(first_y, shift(level, -1, 0), level)
            ahead = (shift(beyond, -WIDE, 1) - level) * links(p)[2 + column]
            back = shift(jnp.where(last_y, shift(ahead, 1, 0), ahead), WIDE, 1)
            squares = squares + jnp.square(
                jnp.maximum(jnp.maximum(up * back, down * ahead), 0.0)
            )
            squares = squares + jnp.square(
                jnp.maximum(jnp.maximum(up * back_z, down * ahead_z), 0.0)
            )
            length = squares + EPSILON
            keep(step, column, p, level - pull * (length * lax.rsqrt(length) - 1.0))

    return one_step


def in_blocks(here, one_step, plan):
    def several(step, columns, lo, hi):
        for column in columns:
            one_step(step, column, lo, hi)

    for block, entry in enumerate(plan):
        pl.when(here > -1 - block)(functools.partial(several, *entry))


def early_kernel(where_am_i, *refs):
    own_ref, inner_ref, near_ref, odd_ref, even_ref, pull_ref, side_ref = refs[-7:]

    def at(column, p):
        return column * EARLY_PLANES + p - EARLY

    def load(step, column, p):
        if step == 0:
            base = column * HALF
            return own_ref[base + p - HALF] if p < TILE else inner_ref[base + 3 * HALF - 1 - p]
        return (odd_ref if step % 2 else even_ref)[at(column, p)]

    def keep(step, column, p, value):
        (even_ref if step % 2 else odd_ref)[at(column, p)] = value

    one_step = stepper(
        load, keep, lambda column, p: (pull_ref, side_ref, at(column, p)), lambda p: near_ref, None
    )
    plan = ((0, (0,), 5, 11), (0, (1,), 5, 11), (1, (0, 1), 6, 10), (2, (0, 1), 7, 9))
    in_blocks(where_am_i(refs), one_step, plan)


def late_kernel(where_am_i, *refs):
    (
        table_ref,
        outer_ref,
        own_ref,
        far_ref,
        near_ref,
        faces_ref,
        early_odd_ref,
        early_even_ref,
        early_pull_ref,
        early_side_ref,
        out_ref,
        even_ref,
        odd_ref,
        pull_ref,
        side_ref,
        done_ref,
    ) = refs[-16:]

    def early(column, p):
        return column * EARLY_PLANES + p - EARLY

    def at(column, p):
        return column * TILE + p

    def load(step, column, p):
        if step == 0:
            base = column * HALF
            return outer_ref[base + HALF - 1 - p] if p < HALF else own_ref[base + p - HALF]
        if p >= EARLY + step - 1:
            return (early_odd_ref if step % 2 else early_even_ref)[early(column, p)]
        return (odd_ref if step % 2 else even_ref)[at(column, p)]

    def keep(step, column, p, value):
        (even_ref if step % 2 else odd_ref)[at(column, p)] = value

    def signs(column, p):
        if p >= EARLY:
            return early_pull_ref, early_side_ref, early(column, p)
        return pull_ref, side_ref, at(column, p)

    one_step = stepper(load, keep, signs, lambda p: far_ref if p < HALF else near_ref, faces_ref)
    in_blocks(where_am_i(refs), one_step, [(s, (0, 1), 1 + s, 5 + s) for s in range(STEPS)])
    lower = iota((ROWS, 128), 1) % WIDE < TILE
    for column in range(2):
        for pair in range(PAIRS):
            p = at(column, HALF + pair)
            row = (column * PAIRS + pair) * ROWS
            done_ref[row : row + ROWS, :] = jnp.where(
                lower, shift(even_ref[p], -4, 1), shift(even_ref[p + PAIRS], 4, 1)
            )
    for r in range(ROWS):
        for column in range(2):
            out_ref[table_ref[4 + column, r + 1]] = done_ref[
                pl.ds(column * PAIRS * ROWS + r, PAIRS, stride=ROWS), :
            ]


def deliver_kernel(where_am_i, *refs):
    counts_ref, returned_ref, out_ref, turned_ref = refs[-4:]
    me = where_am_i(refs)
    counts = counts_ref[...]
    owner = iota((1, COLUMNS), 1)
    turn = jnp.sum(jnp.where(owner < me, counts, 0)) & (COLUMNS - 1)
    live = iota((SLOTS, SLOTS), 1) < jnp.sum(jnp.where(owner == me, counts, 0))
    chips = COLUMNS // 2
    for core in range(2):
        for pair in range(PAIRS):
            held_ref = turned_ref.at[core * PAIRS + pair]
            for d in range(DEPTH):
                for column in range(2):
                    row = core * BACK + (column * DEPTH + d) * PAIRS + pair
                    held_ref[pl.ds(d * COLUMNS + column, chips, stride=2), :] = returned_ref[
                        pl.ds(row, chips, stride=2 * BACK), :
                    ]
            turned = pltpu.roll(held_ref[...].T, (SLOTS - turn) & (SLOTS - 1), 1)
            turned = jnp.where(live, turned, 0.0)
            for y in range(TILE):
                for upper in range(2):
                    row = y * WIDE + upper * TILE
                    z = plane_of(core, pair, upper)
                    out_ref[pl.ds(y * TILE + z, TILE, stride=TILE * TILE), :] = turned[
                        row : row + TILE
                    ]


def spec(space=pltpu.VMEM):
    return pl.BlockSpec(memory_space=space)


def run(
    kernel, operands, shapes, scratch, me=None, spaces=None, out_spaces=None, cost=(0, 0), grant=32
):
    spaces = spaces or [pltpu.VMEM] * len(operands)
    out_spaces = out_spaces or [pltpu.VMEM] * len(shapes)
    if me is not None:
        operands = (me, *operands)
        spaces = [pltpu.SMEM, *spaces]
    out = pl.pallas_call(
        kernel,
        out_shape=[
            (pltpu.SMEM if space == pltpu.SMEM else jax.ShapeDtypeStruct)(*shape)
            for shape, space in zip(shapes, out_spaces)
        ],
        in_specs=[spec(s) for s in spaces],
        out_specs=[spec(s) for s in out_spaces],
        scratch_shapes=scratch,
        compiler_params=pltpu.CompilerParams(vmem_limit_bytes=grant << 20),
        cost_estimate=pl.CostEstimate(flops=cost[0], bytes_accessed=cost[1], transcendentals=0),
        name=getattr(kernel, "func", kernel).__name__,
    )(*operands)
    return out


def position(refs):
    return lax.axis_index("mem")


def given(refs):
    return refs[0][0]


def bind(kernel, me):
    return functools.partial(kernel, position if me is None else given)


def pack(counts, phi, me=None):
    (out,) = run(
        bind(pack_kernel, me),
        (counts, phi.reshape(CELLS, SLOTS)),
        [((COLUMNS * SENT, 128), F32)],
        [
            pltpu.SMEM((1, COLUMNS), I32),
            pltpu.VMEM((CELLS, SLOTS), F32),
            pltpu.VMEM((2 * PAIRS, SLOTS + 16, 128), F32),
            pltpu.SemaphoreType.DMA((2,)),
        ],
        me,
        [pltpu.HBM, pltpu.HBM],
        grant=62,
    )
    return out.reshape(COLUMNS * SENT // 4, 4, 128)


def masks_of(counts, neighbours, me=None):
    return run(
        bind(mask_kernel, me),
        (counts, neighbours),
        [((4, ROWS, 128), F32), ((2, ROWS, 128), F32), ((6, TABLE), I32)],
        [pltpu.VMEM((128, 128), F32), pltpu.VMEM((8 * ROWS, 128), F32)],
        me,
        [pltpu.SMEM, pltpu.VMEM],
        [pltpu.VMEM, pltpu.VMEM, pltpu.SMEM],
        cost=(1 << 22, 1 << 17),
    )


def unpack(table, received):
    (out,) = run(
        unpack_kernel,
        (pltpu.with_memory_space_constraint(table, pltpu.SMEM), received.reshape(COLUMNS * SENT // PAIRS, PAIRS, 128)),
        [((TILE, ROWS, 128), F32)],
        [pltpu.VMEM((4 * PAIRS * ROWS, 128), F32)],
        None,
        [pltpu.SMEM, pltpu.VMEM],
    )
    return out


def start_march(own, inner, near, me=None):
    return run(
        bind(early_kernel, me),
        (own, inner, near),
        [((2 * EARLY_PLANES, ROWS, 128), F32)] * 4,
        [],
        me,
        cost=(1 << 22, 1 << 20),
    )


def end_march(table, outer, own, far, near, faces, early, me=None):
    (out,) = run(
        bind(late_kernel, me),
        (
            pltpu.with_memory_space_constraint(table, pltpu.SMEM),
            outer,
            own,
            far,
            near,
            faces,
            *early,
        ),
        [((COLUMNS * BACK // PAIRS, PAIRS, 128), F32)],
        [pltpu.VMEM((2 * TILE, ROWS, 128), F32)] * 4
        + [pltpu.VMEM((2 * PAIRS * ROWS, 128), F32)],
        me,
        [pltpu.SMEM] + [pltpu.VMEM] * 9,
    )
    return out.reshape(COLUMNS, BACK, 128)


def deliver(counts, returned, me=None):
    (out,) = run(
        bind(deliver_kernel, me),
        (counts, returned.reshape(COLUMNS * BACK, 128)),
        [((CELLS, SLOTS), F32)],
        [pltpu.VMEM((2 * PAIRS, SLOTS, 128), F32)],
        me,
    )
    return out.reshape(TILE, TILE, TILE, SLOTS)


def exchange(x):
    return lax.all_to_all(x, "mem", split_axis=0, concat_axis=0, tiled=True)


def on_device(phi_owned, band_counts, neighbours):
    groups, members = lax.axis_size("grp"), lax.axis_size("mem")
    mates = [(m, m ^ 1) for m in range(members)]
    across = []
    for g in range(groups - 1):
        for m in range(0, members, 2):
            low, high = g * members + m + 1, (g + 1) * members + m
            across += [(low, high), (high, low)]
    received = exchange(pack(band_counts, phi_owned))
    near, faces, table = masks_of(band_counts, neighbours)
    far = lax.ppermute(near, ("grp", "mem"), across)
    received, far = lax.optimization_barrier((received, far))
    own = unpack(table, received)
    inner = lax.ppermute(own, "mem", mates)
    outer = lax.ppermute(own, ("grp", "mem"), across)
    early = start_march(own, inner, near)
    returned = exchange(end_march(table, outer, own, far, near, faces, early))
    return deliver(band_counts, returned)


def solution(mesh):
    return jax.shard_map(
        on_device,
        mesh=mesh,
        in_specs=(P(None, None, None, ("grp", "mem")), P("grp", None), P("grp", None, None)),
        out_specs=P(None, None, None, ("grp", "mem")),
        check_vma=False,
    )
```

```python
import functools

import jax
import jax.numpy as jnp
from jax import lax
from jax.experimental import pallas as pl
from jax.experimental.pallas import tpu as pltpu
from jax.sharding import PartitionSpec as P

STEPS = 4
TIME_STEP = 0.5
EPSILON = 1e-06

TILE = 8
ROWS = 32
COLUMNS = 64
SLOTS = 128
CELLS = TILE**3
DEPTH = SLOTS // COLUMNS
WIDE = 16
TABLE = 40
HALF = TILE // 2
PAIRS = HALF // 2
SENT = 3 * DEPTH * PAIRS
BACK = 2 * DEPTH * PAIRS

F32 = jnp.float32
I32 = jnp.int32


def shift(x, amount, axis):
    return pltpu.roll(x, amount % x.shape[axis] if isinstance(amount, int) else amount, axis)


def iota(shape, axis):
    return lax.broadcasted_iota(I32, shape, axis)


def own_start(counts_ref, me):
    total = jnp.int32(0)
    for owner in range(COLUMNS - 1):
        total = total + jnp.where(owner < me, counts_ref[0, owner], 0)
    return total


def plane_of(core, pair, upper):
    w = pair + PAIRS * upper
    return TILE - 1 - w if core else w


def pack_kernel(where_am_i, *refs):
    counts_hbm, phi_hbm, out_ref, counts_ref, phi_ref, turned_ref, sems = refs[-7:]
    copies = [
        pltpu.make_async_copy(counts_hbm, counts_ref, sems.at[0]),
        pltpu.make_async_copy(phi_hbm, phi_ref, sems.at[1]),
    ]
    for copy in copies:
        copy.start()
    copies[0].wait()
    turn = own_start(counts_ref, where_am_i(refs)) & (COLUMNS - 1)
    copies[1].wait()
    chips = COLUMNS // 2
    upper_x = iota((chips, 128), 1) % TILE >= HALF
    for core in range(2):
        for pair in range(PAIRS):
            blocks = []
            for y in range(TILE):
                for upper in range(2):
                    z = plane_of(core, pair, upper)
                    tiles = phi_ref[pl.ds(y * TILE + z, TILE, stride=TILE * TILE), :]
                    blocks.append(pltpu.roll(tiles, turn, 1))
            turned = jnp.concatenate(blocks, axis=0).T
            held_ref = turned_ref.at[core * PAIRS + pair]
            held_ref[8 : 8 + SLOTS, :] = turned
            held_ref[7:8, :] = turned[SLOTS - 1 :]
            held_ref[8 + SLOTS : 9 + SLOTS, :] = turned[:1]
            for d in range(DEPTH):
                first = 8 + d * COLUMNS
                base = core * SENT + d * PAIRS + pair
                for column in range(2):
                    out_ref[
                        pl.ds(base + column * DEPTH * PAIRS, chips, stride=2 * SENT), :
                    ] = held_ref[pl.ds(first + column, chips, stride=2), :]
                left = held_ref[pl.ds(first - 1, chips, stride=2), :]
                right = held_ref[pl.ds(first + 2, chips, stride=2), :]
                out_ref[pl.ds(base + 2 * DEPTH * PAIRS, chips, stride=2 * SENT), :] = jnp.where(
                    upper_x, left, right
                )


def fill_table(counts_ref, table_ref, column):
    for entry in range(6):
        table_ref[entry, 1] = jnp.int32(0)
        table_ref[entry, ROWS] = jnp.int32(0)

    def body(owner, start):
        turn = start & (COLUMNS - 1)
        for entry, delta in enumerate((0, 1, -1, 2)):
            first = (column + delta - turn) & (COLUMNS - 1)
            row = (start + first - delta) >> 6
            slot = ((first + turn - delta) & (SLOTS - 1)) >> 6
            base = owner * (3 * DEPTH) + min(entry, 2) * DEPTH
            table_ref[entry, row + 1] = base + slot
            table_ref[entry, row + 2] = base + (1 - slot)
            if entry < 2:
                base = owner * (2 * DEPTH) + entry * DEPTH
                table_ref[4 + entry, row + 1] = base + slot
                table_ref[4 + entry, row + 2] = base + (1 - slot)
        return start + counts_ref[0, owner]

    lax.fori_loop(0, COLUMNS, body, jnp.int32(0), unroll=8)


def mask_kernel(where_am_i, *refs):
    counts_ref, links_ref, flat_ref, outer_ref, table_ref, lhs_ref, found_ref = refs[-7:]
    me = where_am_i(refs)
    chip, core = me >> 1, me & 1
    fill_table(counts_ref, table_ref, 2 * chip)
    blocks = ROWS // 2
    for v in range(blocks):
        lhs_ref[v * 8 : v * 8 + 6, :] = jnp.where(
            links_ref[0, :, v * 128 : (v + 1) * 128] >= 0, 1.0, 0.0
        )
        lhs_ref[v * 8 + 6 : v * 8 + 8, :] = jnp.zeros((2, 128), F32)
    source = iota((128, 256), 0)
    target = iota((128, 256), 1)
    x16 = target % WIDE
    lane = iota((ROWS, 128), 1)
    for column in range(2):
        wanted = 2 * chip + column + jnp.where(x16 < 4, -1, jnp.where(x16 >= 12, 1, 0))
        pick = (source % COLUMNS == wanted) & (source // COLUMNS == target // 128)
        found = jnp.dot(
            lhs_ref[...].astype(jnp.bfloat16),
            jnp.where(pick, 1.0, 0.0).astype(jnp.bfloat16),
            preferred_element_type=F32,
        )
        for v in range(blocks):
            for odd in range(2):
                found_ref[pl.ds(2 * v + odd, 8, stride=ROWS), :] = found[
                    v * 8 : v * 8 + 8, odd * 128 : (odd + 1) * 128
                ]
        edge = (lane % WIDE == 3) | (lane % WIDE == 11)
        flat_ref[column] = jnp.where(edge, found_ref[ROWS : 2 * ROWS, :], 1.0)
        flat_ref[2 + column] = jnp.where(lane >= 112, found_ref[3 * ROWS : 4 * ROWS, :], 1.0)
        outer_ref[column] = jnp.where(
            core == 0, found_ref[4 * ROWS : 5 * ROWS, :], found_ref[5 * ROWS : 6 * ROWS, :]
        )


def unpack_kernel(table_ref, received_ref, planes_ref, packed_ref):
    for r in range(ROWS):
        for entry in range(4):
            packed_ref[pl.ds(entry * PAIRS * ROWS + r, PAIRS, stride=ROWS), :] = received_ref[
                table_ref[entry, r + 1]
            ]
    lane = iota((ROWS, 128), 1)
    x16 = lane % WIDE
    for pair in range(PAIRS):
        first, second, left, right = (
            packed_ref[(entry * PAIRS + pair) * ROWS : (entry * PAIRS + pair + 1) * ROWS, :]
            for entry in range(4)
        )
        outside = jnp.where(lane % TILE >= HALF, left, right)

        def join(left, here, right):
            return jnp.where(x16 < 4, left, jnp.where(x16 >= 12, right, here))

        second_4 = shift(second, 4, 1)
        first_m4 = shift(first, -4, 1)
        planes_ref[pair] = join(shift(outside, -4, 1), shift(first, 4, 1), shift(second, 12, 1))
        planes_ref[PAIRS + pair] = join(shift(outside, -12, 1), first_m4, second_4)
        planes_ref[HALF + pair] = join(first_m4, second_4, shift(outside, 12, 1))
        planes_ref[HALF + PAIRS + pair] = join(
            shift(first, -12, 1), shift(second, -4, 1), shift(outside, 4, 1)
        )


EARLY_PLANES = TILE - 2


def stepper(load, keep, signs, links, faces_ref):
    lane = iota((ROWS, 128), 1)
    first_y = lane < WIDE
    last_y = lane >= 128 - WIDE

    def one_step(step, column, lo, hi):
        level = load(step, column, lo - 1)
        after = load(step, column, lo)
        ahead_z = after - level
        if lo == HALF:
            ahead_z = ahead_z * faces_ref[column]
        for p in range(lo, hi):
            back_z = ahead_z
            level = after
            after = load(step, column, p + 1)
            ahead_z = after - level
            if p == HALF - 1:
                ahead_z = ahead_z * faces_ref[column]
            pull_ref, side_ref, at = signs(column, p)
            if step == 0:
                sign_field = level * lax.rsqrt(level * level + 1.0)
                pull = TIME_STEP * sign_field
                up = jnp.where(sign_field > 0, 1.0, -1.0)
                pull_ref[at] = pull
                side_ref[at] = up
            else:
                pull = pull_ref[at]
                up = side_ref[at]
            down = -up
            ahead = (shift(level, -1, 1) - level) * links(p)[column]
            back = shift(ahead, 1, 1)
            squares = jnp.square(jnp.maximum(jnp.maximum(up * back, down * ahead), 0.0))
            beyond = jnp.where(first_y, shift(level, -1, 0), level)
            ahead = (shift(beyond, -WIDE, 1) - level) * links(p)[2 + column]
            back = shift(jnp.where(last_y, shift(ahead, 1, 0), ahead), WIDE, 1)
            squares = squares + jnp.square(
                jnp.maximum(jnp.maximum(up * back, down * ahead), 0.0)
            )
            squares = squares + jnp.square(
                jnp.maximum(jnp.maximum(up * back_z, down * ahead_z), 0.0)
            )
            length = squares + EPSILON
            keep(step, column, p, level - pull * (length * lax.rsqrt(length) - 1.0))

    return one_step


def in_blocks(here, one_step, plan):
    def several(step, columns, lo, hi):
        for column in columns:
            one_step(step, column, lo, hi)

    for block, entry in enumerate(plan):
        pl.when(here > -1 - block)(functools.partial(several, *entry))


def early_at(column, p):
    return column * EARLY_PLANES + p - 1


def early_kernel(where_am_i, *refs):
    outer_ref, own_ref, far_ref, near_ref, faces_ref, odd_ref, even_ref, pull_ref, side_ref = refs[-9:]

    def load(step, column, p):
        if step == 0:
            base = column * HALF
            return outer_ref[base + HALF - 1 - p] if p < HALF else own_ref[base + p - HALF]
        return (odd_ref if step % 2 else even_ref)[early_at(column, p)]

    def keep(step, column, p, value):
        (even_ref if step % 2 else odd_ref)[early_at(column, p)] = value

    def signs(column, p):
        return pull_ref, side_ref, early_at(column, p)

    one_step = stepper(load, keep, signs, lambda p: far_ref if p < HALF else near_ref, faces_ref)
    plan = ((0, (0,), 1, 7), (0, (1,), 1, 7), (1, (0, 1), 2, 6), (2, (0, 1), 3, 5))
    in_blocks(where_am_i(refs), one_step, plan)


def late_kernel(where_am_i, *refs):
    (
        table_ref,
        inner_ref,
        own_ref,
        near_ref,
        faces_ref,
        early_odd_ref,
        early_even_ref,
        early_pull_ref,
        early_side_ref,
        out_ref,
        even_ref,
        odd_ref,
        pull_ref,
        side_ref,
        done_ref,
    ) = refs[-15:]

    def at(column, p):
        return column * TILE + p - HALF

    def load(step, column, p):
        if step == 0:
            base = column * HALF
            return own_ref[base + p - HALF] if p < TILE else inner_ref[base + 3 * HALF - 1 - p]
        if p <= EARLY_PLANES + 1 - step:
            return (early_odd_ref if step % 2 else early_even_ref)[early_at(column, p)]
        return (odd_ref if step % 2 else even_ref)[at(column, p)]

    def keep(step, column, p, value):
        (even_ref if step % 2 else odd_ref)[at(column, p)] = value

    def signs(column, p):
        if p <= EARLY_PLANES:
            return early_pull_ref, early_side_ref, early_at(column, p)
        return pull_ref, side_ref, at(column, p)

    one_step = stepper(load, keep, signs, lambda p: near_ref, faces_ref)
    in_blocks(where_am_i(refs), one_step, [(s, (0, 1), 7 - s, 11 - s) for s in range(STEPS)])
    lower = iota((ROWS, 128), 1) % WIDE < TILE
    for column in range(2):
        for pair in range(PAIRS):
            p = at(column, HALF + pair)
            row = (column * PAIRS + pair) * ROWS
            done_ref[row : row + ROWS, :] = jnp.where(
                lower, shift(even_ref[p], -4, 1), shift(even_ref[p + PAIRS], 4, 1)
            )
    for r in range(ROWS):
        for column in range(2):
            out_ref[table_ref[4 + column, r + 1]] = done_ref[
                pl.ds(column * PAIRS * ROWS + r, PAIRS, stride=ROWS), :
            ]


def deliver_kernel(where_am_i, *refs):
    counts_ref, returned_ref, out_ref, turned_ref = refs[-4:]
    me = where_am_i(refs)
    counts = counts_ref[...]
    owner = iota((1, COLUMNS), 1)
    turn = jnp.sum(jnp.where(owner < me, counts, 0)) & (COLUMNS - 1)
    live = iota((SLOTS, SLOTS), 1) < jnp.sum(jnp.where(owner == me, counts, 0))
    chips = COLUMNS // 2
    for core in range(2):
        for pair in range(PAIRS):
            held_ref = turned_ref.at[core * PAIRS + pair]
            for d in range(DEPTH):
                for column in range(2):
                    row = core * BACK + (column * DEPTH + d) * PAIRS + pair
                    held_ref[pl.ds(d * COLUMNS + column, chips, stride=2), :] = returned_ref[
                        pl.ds(row, chips, stride=2 * BACK), :
                    ]
            turned = pltpu.roll(held_ref[...].T, (SLOTS - turn) & (SLOTS - 1), 1)
            turned = jnp.where(live, turned, 0.0)
            for y in range(TILE):
                for upper in range(2):
                    row = y * WIDE + upper * TILE
                    z = plane_of(core, pair, upper)
                    out_ref[pl.ds(y * TILE + z, TILE, stride=TILE * TILE), :] = turned[
                        row : row + TILE
                    ]


def spec(space=pltpu.VMEM):
    return pl.BlockSpec(memory_space=space)


def run(
    kernel, operands, shapes, scratch, me=None, spaces=None, out_spaces=None, cost=(0, 0), grant=32
):
    spaces = spaces or [pltpu.VMEM] * len(operands)
    out_spaces = out_spaces or [pltpu.VMEM] * len(shapes)
    if me is not None:
        operands = (me, *operands)
        spaces = [pltpu.SMEM, *spaces]
    out = pl.pallas_call(
        kernel,
        out_shape=[
            (pltpu.SMEM if space == pltpu.SMEM else jax.ShapeDtypeStruct)(*shape)
            for shape, space in zip(shapes, out_spaces)
        ],
        in_specs=[spec(s) for s in spaces],
        out_specs=[spec(s) for s in out_spaces],
        scratch_shapes=scratch,
        compiler_params=pltpu.CompilerParams(vmem_limit_bytes=grant << 20),
        cost_estimate=pl.CostEstimate(flops=cost[0], bytes_accessed=cost[1], transcendentals=0),
        name=getattr(kernel, "func", kernel).__name__,
    )(*operands)
    return out


def position(refs):
    return lax.axis_index("mem")


def given(refs):
    return refs[0][0]


def bind(kernel, me):
    return functools.partial(kernel, position if me is None else given)


def pack(counts, phi, me=None):
    (out,) = run(
        bind(pack_kernel, me),
        (counts, phi.reshape(CELLS, SLOTS)),
        [((COLUMNS * SENT, 128), F32)],
        [
            pltpu.SMEM((1, COLUMNS), I32),
            pltpu.VMEM((CELLS, SLOTS), F32),
            pltpu.VMEM((2 * PAIRS, SLOTS + 16, 128), F32),
            pltpu.SemaphoreType.DMA((2,)),
        ],
        me,
        [pltpu.HBM, pltpu.HBM],
        grant=62,
    )
    return out.reshape(COLUMNS * SENT // 4, 4, 128)


def masks_of(counts, neighbours, me=None):
    return run(
        bind(mask_kernel, me),
        (counts, neighbours),
        [((4, ROWS, 128), F32), ((2, ROWS, 128), F32), ((6, TABLE), I32)],
        [pltpu.VMEM((128, 128), F32), pltpu.VMEM((8 * ROWS, 128), F32)],
        me,
        [pltpu.SMEM, pltpu.VMEM],
        [pltpu.VMEM, pltpu.VMEM, pltpu.SMEM],
        cost=(1 << 22, 1 << 17),
    )


def unpack(table, received):
    (out,) = run(
        unpack_kernel,
        (pltpu.with_memory_space_constraint(table, pltpu.SMEM), received.reshape(COLUMNS * SENT // PAIRS, PAIRS, 128)),
        [((TILE, ROWS, 128), F32)],
        [pltpu.VMEM((4 * PAIRS * ROWS, 128), F32)],
        None,
        [pltpu.SMEM, pltpu.VMEM],
    )
    return out


def start_march(outer, own, far, near, faces, me=None):
    return run(
        bind(early_kernel, me),
        (outer, own, far, near, faces),
        [((2 * EARLY_PLANES, ROWS, 128), F32)] * 4,
        [],
        me,
        cost=(1 << 22, 1 << 20),
    )


def end_march(table, inner, own, near, faces, early, me=None):
    (out,) = run(
        bind(late_kernel, me),
        (
            pltpu.with_memory_space_constraint(table, pltpu.SMEM),
            inner,
            own,
            near,
            faces,
            *early,
        ),
        [((COLUMNS * BACK // PAIRS, PAIRS, 128), F32)],
        [pltpu.VMEM((2 * TILE, ROWS, 128), F32)] * 4
        + [pltpu.VMEM((2 * PAIRS * ROWS, 128), F32)],
        me,
        [pltpu.SMEM] + [pltpu.VMEM] * 8,
    )
    return out.reshape(COLUMNS, BACK, 128)


def deliver(counts, returned, me=None):
    (out,) = run(
        bind(deliver_kernel, me),
        (counts, returned.reshape(COLUMNS * BACK, 128)),
        [((CELLS, SLOTS), F32)],
        [pltpu.VMEM((2 * PAIRS, SLOTS, 128), F32)],
        me,
    )
    return out.reshape(TILE, TILE, TILE, SLOTS)


def exchange(x):
    return lax.all_to_all(x, "mem", split_axis=0, concat_axis=0, tiled=True)


def on_device(phi_owned, band_counts, neighbours):
    groups, members = lax.axis_size("grp"), lax.axis_size("mem")
    mates = [(m, m ^ 1) for m in range(members)]
    across = []
    for g in range(groups - 1):
        for m in range(0, members, 2):
            low, high = g * members + m + 1, (g + 1) * members + m
            across += [(low, high), (high, low)]
    received = exchange(pack(band_counts, phi_owned))
    near, faces, table = masks_of(band_counts, neighbours)
    far = lax.ppermute(near, ("grp", "mem"), across)
    received, far = lax.optimization_barrier((received, far))
    own = unpack(table, received)
    outer = lax.ppermute(own, ("grp", "mem"), across)
    inner = lax.ppermute(own, "mem", mates)
    early = start_march(outer, own, far, near, faces)
    returned = exchange(end_march(table, inner, own, near, faces, early))
    return deliver(band_counts, returned)


def solution(mesh):
    return jax.shard_map(
        on_device,
        mesh=mesh,
        in_specs=(P(None, None, None, ("grp", "mem")), P("grp", None), P("grp", None, None)),
        out_specs=P(None, None, None, ("grp", "mem")),
        check_vma=False,
    )
```

```python
import functools

import jax
import jax.numpy as jnp
from jax import lax
from jax.experimental import pallas as pl
from jax.experimental.pallas import tpu as pltpu
from jax.sharding import PartitionSpec as P

STEPS = 4
TIME_STEP = 0.5
EPSILON = 1e-06

TILE = 8
ROWS = 32
COLUMNS = 64
SLOTS = 128
CELLS = TILE**3
DEPTH = SLOTS // COLUMNS
WIDE = 16
TABLE = 40
HALF = TILE // 2
PAIRS = HALF // 2
SENT = 3 * DEPTH * PAIRS
BACK = 2 * DEPTH * PAIRS

F32 = jnp.float32
I32 = jnp.int32


def shift(x, amount, axis):
    return pltpu.roll(x, amount % x.shape[axis] if isinstance(amount, int) else amount, axis)


def iota(shape, axis):
    return lax.broadcasted_iota(I32, shape, axis)


def own_start(counts_ref, me):
    total = jnp.int32(0)
    for owner in range(COLUMNS - 1):
        total = total + jnp.where(owner < me, counts_ref[0, owner], 0)
    return total


def plane_of(core, pair, upper):
    w = pair + PAIRS * upper
    return TILE - 1 - w if core else w


def pack_kernel(where_am_i, *refs):
    counts_hbm, phi_hbm, out_ref, counts_ref, phi_ref, turned_ref, sems = refs[-7:]
    copies = [
        pltpu.make_async_copy(counts_hbm, counts_ref, sems.at[0]),
        pltpu.make_async_copy(phi_hbm, phi_ref, sems.at[1]),
    ]
    for copy in copies:
        copy.start()
    copies[0].wait()
    turn = own_start(counts_ref, where_am_i(refs)) & (COLUMNS - 1)
    copies[1].wait()
    chips = COLUMNS // 2
    upper_x = iota((chips, 128), 1) % TILE >= HALF
    for core in range(2):
        for pair in range(PAIRS):
            blocks = []
            for y in range(TILE):
                for upper in range(2):
                    z = plane_of(core, pair, upper)
                    tiles = phi_ref[pl.ds(y * TILE + z, TILE, stride=TILE * TILE), :]
                    blocks.append(pltpu.roll(tiles, turn, 1))
            turned = jnp.concatenate(blocks, axis=0).T
            held_ref = turned_ref.at[core * PAIRS + pair]
            held_ref[8 : 8 + SLOTS, :] = turned
            held_ref[7:8, :] = turned[SLOTS - 1 :]
            held_ref[8 + SLOTS : 9 + SLOTS, :] = turned[:1]
            for d in range(DEPTH):
                first = 8 + d * COLUMNS
                base = core * SENT + d * PAIRS + pair
                for column in range(2):
                    out_ref[
                        pl.ds(base + column * DEPTH * PAIRS, chips, stride=2 * SENT), :
                    ] = held_ref[pl.ds(first + column, chips, stride=2), :]
                left = held_ref[pl.ds(first - 1, chips, stride=2), :]
                right = held_ref[pl.ds(first + 2, chips, stride=2), :]
                out_ref[pl.ds(base + 2 * DEPTH * PAIRS, chips, stride=2 * SENT), :] = jnp.where(
                    upper_x, left, right
                )


def fill_table(counts_ref, table_ref, column):
    for entry in range(6):
        table_ref[entry, 1] = jnp.int32(0)
        table_ref[entry, ROWS] = jnp.int32(0)

    def body(owner, start):
        turn = start & (COLUMNS - 1)
        for entry, delta in enumerate((0, 1, -1, 2)):
            first = (column + delta - turn) & (COLUMNS - 1)
            row = (start + first - delta) >> 6
            slot = ((first + turn - delta) & (SLOTS - 1)) >> 6
            base = owner * (3 * DEPTH) + min(entry, 2) * DEPTH
            table_ref[entry, row + 1] = base + slot
            table_ref[entry, row + 2] = base + (1 - slot)
            if entry < 2:
                base = owner * (2 * DEPTH) + entry * DEPTH
                table_ref[4 + entry, row + 1] = base + slot
                table_ref[4 + entry, row + 2] = base + (1 - slot)
        return start + counts_ref[0, owner]

    lax.fori_loop(0, COLUMNS, body, jnp.int32(0), unroll=8)


def mask_kernel(where_am_i, *refs):
    counts_ref, links_ref, flat_ref, outer_ref, table_ref, lhs_ref, found_ref = refs[-7:]
    me = where_am_i(refs)
    chip, core = me >> 1, me & 1
    fill_table(counts_ref, table_ref, 2 * chip)
    blocks = ROWS // 2
    for v in range(blocks):
        lhs_ref[v * 8 : v * 8 + 6, :] = jnp.where(
            links_ref[0, :, v * 128 : (v + 1) * 128] >= 0, 1.0, 0.0
        )
        lhs_ref[v * 8 + 6 : v * 8 + 8, :] = jnp.zeros((2, 128), F32)
    source = iota((128, 256), 0)
    target = iota((128, 256), 1)
    x16 = target % WIDE
    lane = iota((ROWS, 128), 1)
    for column in range(2):
        wanted = 2 * chip + column + jnp.where(x16 < 4, -1, jnp.where(x16 >= 12, 1, 0))
        pick = (source % COLUMNS == wanted) & (source // COLUMNS == target // 128)
        found = jnp.dot(
            lhs_ref[...].astype(jnp.bfloat16),
            jnp.where(pick, 1.0, 0.0).astype(jnp.bfloat16),
            preferred_element_type=F32,
        )
        for v in range(blocks):
            for odd in range(2):
                found_ref[pl.ds(2 * v + odd, 8, stride=ROWS), :] = found[
                    v * 8 : v * 8 + 8, odd * 128 : (odd + 1) * 128
                ]
        edge = (lane % WIDE == 3) | (lane % WIDE == 11)
        flat_ref[column] = jnp.where(edge, found_ref[ROWS : 2 * ROWS, :], 1.0)
        flat_ref[2 + column] = jnp.where(lane >= 112, found_ref[3 * ROWS : 4 * ROWS, :], 1.0)
        outer_ref[column] = jnp.where(
            core == 0, found_ref[4 * ROWS : 5 * ROWS, :], found_ref[5 * ROWS : 6 * ROWS, :]
        )


def unpack_kernel(table_ref, received_ref, packed_ref, sides_ref):
    span = PAIRS * ROWS
    for r in range(ROWS):
        for entry in range(4):
            rows_ref, first = (packed_ref, entry) if entry < 2 else (sides_ref, entry - 2)
            rows_ref[pl.ds(first * span + r, PAIRS, stride=ROWS), :] = received_ref[
                table_ref[entry, r + 1]
            ]
    upper_x = iota((span, 128), 1) % TILE >= HALF
    packed_ref[2 * span :, :] = jnp.where(upper_x, sides_ref[:span, :], sides_ref[span:, :])


def join_pairs(packed_ref, planes_ref):
    x16 = iota((ROWS, 128), 1) % WIDE

    def join(left, here, right):
        return jnp.where(x16 < 4, left, jnp.where(x16 >= 12, right, here))

    for pair in range(PAIRS):
        first, second, outside = (
            packed_ref[(entry * PAIRS + pair) * ROWS : (entry * PAIRS + pair + 1) * ROWS, :]
            for entry in range(3)
        )
        second_4 = shift(second, 4, 1)
        first_m4 = shift(first, -4, 1)
        planes_ref[pair] = join(shift(outside, -4, 1), shift(first, 4, 1), shift(second, 12, 1))
        planes_ref[PAIRS + pair] = join(shift(outside, -12, 1), first_m4, second_4)
        planes_ref[HALF + pair] = join(first_m4, second_4, shift(outside, 12, 1))
        planes_ref[HALF + PAIRS + pair] = join(
            shift(first, -12, 1), shift(second, -4, 1), shift(outside, 4, 1)
        )


EARLY_PLANES = TILE - 2


def stepper(load, keep, signs, links, faces_ref):
    lane = iota((ROWS, 128), 1)
    first_y = lane < WIDE
    last_y = lane >= 128 - WIDE

    def one_step(step, column, lo, hi):
        level = load(step, column, lo - 1)
        after = load(step, column, lo)
        ahead_z = after - level
        if lo == HALF:
            ahead_z = ahead_z * faces_ref[column]
        for p in range(lo, hi):
            back_z = ahead_z
            level = after
            after = load(step, column, p + 1)
            ahead_z = after - level
            if p == HALF - 1:
                ahead_z = ahead_z * faces_ref[column]
            pull_ref, side_ref, at = signs(column, p)
            if step == 0:
                sign_field = level * lax.rsqrt(level * level + 1.0)
                pull = TIME_STEP * sign_field
                up = jnp.where(sign_field > 0, 1.0, -1.0)
                pull_ref[at] = pull
                side_ref[at] = up
            else:
                pull = pull_ref[at]
                up = side_ref[at]
            down = -up
            ahead = (shift(level, -1, 1) - level) * links(p)[column]
            back = shift(ahead, 1, 1)
            squares = jnp.square(jnp.maximum(jnp.maximum(up * back, down * ahead), 0.0))
            beyond = jnp.where(first_y, shift(level, -1, 0), level)
            ahead = (shift(beyond, -WIDE, 1) - level) * links(p)[2 + column]
            back = shift(jnp.where(last_y, shift(ahead, 1, 0), ahead), WIDE, 1)
            squares = squares + jnp.square(
                jnp.maximum(jnp.maximum(up * back, down * ahead), 0.0)
            )
            squares = squares + jnp.square(
                jnp.maximum(jnp.maximum(up * back_z, down * ahead_z), 0.0)
            )
            length = squares + EPSILON
            keep(step, column, p, level - pull * (length * lax.rsqrt(length) - 1.0))

    return one_step


def in_blocks(here, one_step, plan):
    def several(step, columns, lo, hi):
        for column in columns:
            one_step(step, column, lo, hi)

    for block, entry in enumerate(plan):
        pl.when(here > -1 - block)(functools.partial(several, *entry))


def early_at(column, p):
    return column * EARLY_PLANES + p - 1


def early_kernel(where_am_i, *refs):
    (
        outer_packed_ref,
        own_packed_ref,
        far_ref,
        near_ref,
        faces_ref,
        own_ref,
        odd_ref,
        even_ref,
        pull_ref,
        side_ref,
        outer_ref,
    ) = refs[-11:]
    here = where_am_i(refs)
    pl.when(here > -65)(functools.partial(join_pairs, own_packed_ref, own_ref))
    pl.when(here > -66)(functools.partial(join_pairs, outer_packed_ref, outer_ref))

    def load(step, column, p):
        if step == 0:
            base = column * HALF
            return outer_ref[base + HALF - 1 - p] if p < HALF else own_ref[base + p - HALF]
        return (odd_ref if step % 2 else even_ref)[early_at(column, p)]

    def keep(step, column, p, value):
        (even_ref if step % 2 else odd_ref)[early_at(column, p)] = value

    def signs(column, p):
        return pull_ref, side_ref, early_at(column, p)

    one_step = stepper(load, keep, signs, lambda p: far_ref if p < HALF else near_ref, faces_ref)
    plan = ((0, (0,), 1, 7), (0, (1,), 1, 7), (1, (0, 1), 2, 6), (2, (0, 1), 3, 5))
    in_blocks(here, one_step, plan)


def late_kernel(where_am_i, *refs):
    (
        table_ref,
        inner_packed_ref,
        own_ref,
        near_ref,
        faces_ref,
        early_odd_ref,
        early_even_ref,
        early_pull_ref,
        early_side_ref,
        out_ref,
        even_ref,
        odd_ref,
        pull_ref,
        side_ref,
        done_ref,
        inner_ref,
    ) = refs[-16:]
    here = where_am_i(refs)
    pl.when(here > -65)(functools.partial(join_pairs, inner_packed_ref, inner_ref))

    def at(column, p):
        return column * TILE + p - HALF

    def load(step, column, p):
        if step == 0:
            base = column * HALF
            return own_ref[base + p - HALF] if p < TILE else inner_ref[base + 3 * HALF - 1 - p]
        if p <= EARLY_PLANES + 1 - step:
            return (early_odd_ref if step % 2 else early_even_ref)[early_at(column, p)]
        return (odd_ref if step % 2 else even_ref)[at(column, p)]

    def keep(step, column, p, value):
        (even_ref if step % 2 else odd_ref)[at(column, p)] = value

    def signs(column, p):
        if p <= EARLY_PLANES:
            return early_pull_ref, early_side_ref, early_at(column, p)
        return pull_ref, side_ref, at(column, p)

    one_step = stepper(load, keep, signs, lambda p: near_ref, faces_ref)
    in_blocks(here, one_step, [(s, (0, 1), 7 - s, 11 - s) for s in range(STEPS)])
    lower = iota((ROWS, 128), 1) % WIDE < TILE
    for column in range(2):
        for pair in range(PAIRS):
            p = at(column, HALF + pair)
            row = (column * PAIRS + pair) * ROWS
            done_ref[row : row + ROWS, :] = jnp.where(
                lower, shift(even_ref[p], -4, 1), shift(even_ref[p + PAIRS], 4, 1)
            )
    for r in range(ROWS):
        for column in range(2):
            out_ref[table_ref[4 + column, r + 1]] = done_ref[
                pl.ds(column * PAIRS * ROWS + r, PAIRS, stride=ROWS), :
            ]


def deliver_kernel(where_am_i, *refs):
    counts_ref, returned_ref, out_ref, turned_ref = refs[-4:]
    me = where_am_i(refs)
    counts = counts_ref[...]
    owner = iota((1, COLUMNS), 1)
    turn = jnp.sum(jnp.where(owner < me, counts, 0)) & (COLUMNS - 1)
    live = iota((SLOTS, SLOTS), 1) < jnp.sum(jnp.where(owner == me, counts, 0))
    chips = COLUMNS // 2
    for core in range(2):
        for pair in range(PAIRS):
            held_ref = turned_ref.at[core * PAIRS + pair]
            for d in range(DEPTH):
                for column in range(2):
                    row = core * BACK + (column * DEPTH + d) * PAIRS + pair
                    held_ref[pl.ds(d * COLUMNS + column, chips, stride=2), :] = returned_ref[
                        pl.ds(row, chips, stride=2 * BACK), :
                    ]
            turned = pltpu.roll(held_ref[...].T, (SLOTS - turn) & (SLOTS - 1), 1)
            turned = jnp.where(live, turned, 0.0)
            for y in range(TILE):
                for upper in range(2):
                    row = y * WIDE + upper * TILE
                    z = plane_of(core, pair, upper)
                    out_ref[pl.ds(y * TILE + z, TILE, stride=TILE * TILE), :] = turned[
                        row : row + TILE
                    ]


def spec(space=pltpu.VMEM):
    return pl.BlockSpec(memory_space=space)


def run(
    kernel, operands, shapes, scratch, me=None, spaces=None, out_spaces=None, cost=(0, 0), grant=32
):
    spaces = spaces or [pltpu.VMEM] * len(operands)
    out_spaces = out_spaces or [pltpu.VMEM] * len(shapes)
    if me is not None:
        operands = (me, *operands)
        spaces = [pltpu.SMEM, *spaces]
    out = pl.pallas_call(
        kernel,
        out_shape=[
            (pltpu.SMEM if space == pltpu.SMEM else jax.ShapeDtypeStruct)(*shape)
            for shape, space in zip(shapes, out_spaces)
        ],
        in_specs=[spec(s) for s in spaces],
        out_specs=[spec(s) for s in out_spaces],
        scratch_shapes=scratch,
        compiler_params=pltpu.CompilerParams(vmem_limit_bytes=grant << 20),
        cost_estimate=pl.CostEstimate(flops=cost[0], bytes_accessed=cost[1], transcendentals=0),
        name=getattr(kernel, "func", kernel).__name__,
    )(*operands)
    return out


def position(refs):
    return lax.axis_index("mem")


def given(refs):
    return refs[0][0]


def bind(kernel, me):
    return functools.partial(kernel, position if me is None else given)


def pack(counts, phi, me=None):
    (out,) = run(
        bind(pack_kernel, me),
        (counts, phi.reshape(CELLS, SLOTS)),
        [((COLUMNS * SENT, 128), F32)],
        [
            pltpu.SMEM((1, COLUMNS), I32),
            pltpu.VMEM((CELLS, SLOTS), F32),
            pltpu.VMEM((2 * PAIRS, SLOTS + 16, 128), F32),
            pltpu.SemaphoreType.DMA((2,)),
        ],
        me,
        [pltpu.HBM, pltpu.HBM],
        grant=62,
    )
    return out.reshape(COLUMNS * SENT // 4, 4, 128)


def masks_of(counts, neighbours, me=None):
    return run(
        bind(mask_kernel, me),
        (counts, neighbours),
        [((4, ROWS, 128), F32), ((2, ROWS, 128), F32), ((6, TABLE), I32)],
        [pltpu.VMEM((128, 128), F32), pltpu.VMEM((8 * ROWS, 128), F32)],
        me,
        [pltpu.SMEM, pltpu.VMEM],
        [pltpu.VMEM, pltpu.VMEM, pltpu.SMEM],
        cost=(1 << 22, 1 << 17),
    )


def unpack(table, received):
    (out,) = run(
        unpack_kernel,
        (pltpu.with_memory_space_constraint(table, pltpu.SMEM), received.reshape(COLUMNS * SENT // PAIRS, PAIRS, 128)),
        [((3 * PAIRS * ROWS, 128), F32)],
        [pltpu.VMEM((2 * PAIRS * ROWS, 128), F32)],
        None,
        [pltpu.SMEM, pltpu.VMEM],
    )
    return out


def start_march(outer, own, far, near, faces, me=None):
    return run(
        bind(early_kernel, me),
        (outer, own, far, near, faces),
        [((TILE, ROWS, 128), F32)] + [((2 * EARLY_PLANES, ROWS, 128), F32)] * 4,
        [pltpu.VMEM((TILE, ROWS, 128), F32)],
        me,
        cost=(1 << 22, 1 << 20),
    )


def end_march(table, inner, own, near, faces, early, me=None):
    (out,) = run(
        bind(late_kernel, me),
        (
            pltpu.with_memory_space_constraint(table, pltpu.SMEM),
            inner,
            own,
            near,
            faces,
            *early,
        ),
        [((COLUMNS * BACK // PAIRS, PAIRS, 128), F32)],
        [pltpu.VMEM((2 * TILE, ROWS, 128), F32)] * 4
        + [pltpu.VMEM((2 * PAIRS * ROWS, 128), F32), pltpu.VMEM((TILE, ROWS, 128), F32)],
        me,
        [pltpu.SMEM] + [pltpu.VMEM] * 8,
    )
    return out.reshape(COLUMNS, BACK, 128)


def deliver(counts, returned, me=None):
    (out,) = run(
        bind(deliver_kernel, me),
        (counts, returned.reshape(COLUMNS * BACK, 128)),
        [((CELLS, SLOTS), F32)],
        [pltpu.VMEM((2 * PAIRS, SLOTS, 128), F32)],
        me,
    )
    return out.reshape(TILE, TILE, TILE, SLOTS)


def exchange(x):
    return lax.all_to_all(x, "mem", split_axis=0, concat_axis=0, tiled=True)


def on_device(phi_owned, band_counts, neighbours):
    groups, members = lax.axis_size("grp"), lax.axis_size("mem")
    mates = [(m, m ^ 1) for m in range(members)]
    across = []
    for g in range(groups - 1):
        for m in range(0, members, 2):
            low, high = g * members + m + 1, (g + 1) * members + m
            across += [(low, high), (high, low)]
    received = exchange(pack(band_counts, phi_owned))
    near, faces, table = masks_of(band_counts, neighbours)
    far = lax.ppermute(near, ("grp", "mem"), across)
    received, far = lax.optimization_barrier((received, far))
    packed = unpack(table, received)
    outer = lax.ppermute(packed, ("grp", "mem"), across)
    inner = lax.ppermute(packed, "mem", mates)
    own, *early = start_march(outer, packed, far, near, faces)
    returned = exchange(end_march(table, inner, own, near, faces, early))
    return deliver(band_counts, returned)


def solution(mesh):
    return jax.shard_map(
        on_device,
        mesh=mesh,
        in_specs=(P(None, None, None, ("grp", "mem")), P("grp", None), P("grp", None, None)),
        out_specs=P(None, None, None, ("grp", "mem")),
        check_vma=False,
    )
```

```python
import functools

import jax
import jax.numpy as jnp
from jax import lax
from jax.experimental import pallas as pl
from jax.experimental.pallas import tpu as pltpu
from jax.sharding import PartitionSpec as P

STEPS = 4
TIME_STEP = 0.5
EPSILON = 1e-06

TILE = 8
ROWS = 32
COLUMNS = 64
SLOTS = 128
CELLS = TILE**3
DEPTH = SLOTS // COLUMNS
WIDE = 16
TABLE = 40
HALF = TILE // 2
PAIRS = HALF // 2
SENT = 3 * DEPTH * PAIRS
BACK = 2 * DEPTH * PAIRS

F32 = jnp.float32
I32 = jnp.int32


def shift(x, amount, axis):
    return pltpu.roll(x, amount % x.shape[axis] if isinstance(amount, int) else amount, axis)


def iota(shape, axis):
    return lax.broadcasted_iota(I32, shape, axis)


def own_start(counts_ref, me):
    total = jnp.int32(0)
    for owner in range(COLUMNS - 1):
        total = total + jnp.where(owner < me, counts_ref[0, owner], 0)
    return total


def plane_of(core, pair, upper):
    w = pair + PAIRS * upper
    return TILE - 1 - w if core else w


def pack_kernel(where_am_i, *refs):
    counts_hbm, phi_hbm, out_ref, counts_ref, phi_ref, turned_ref, sems = refs[-7:]
    copies = [
        pltpu.make_async_copy(counts_hbm, counts_ref, sems.at[0]),
        pltpu.make_async_copy(phi_hbm, phi_ref, sems.at[1]),
    ]
    for copy in copies:
        copy.start()
    copies[0].wait()
    turn = own_start(counts_ref, where_am_i(refs)) & (COLUMNS - 1)
    copies[1].wait()
    chips = COLUMNS // 2
    upper_x = iota((chips, 128), 1) % TILE >= HALF
    for core in range(2):
        for pair in range(PAIRS):
            blocks = []
            for y in range(TILE):
                for upper in range(2):
                    z = plane_of(core, pair, upper)
                    tiles = phi_ref[pl.ds(y * TILE + z, TILE, stride=TILE * TILE), :]
                    blocks.append(pltpu.roll(tiles, turn, 1))
            turned = jnp.concatenate(blocks, axis=0).T
            held_ref = turned_ref.at[core * PAIRS + pair]
            held_ref[8 : 8 + SLOTS, :] = turned
            held_ref[7:8, :] = turned[SLOTS - 1 :]
            held_ref[8 + SLOTS : 9 + SLOTS, :] = turned[:1]
            for d in range(DEPTH):
                first = 8 + d * COLUMNS
                base = core * SENT + d * PAIRS + pair
                for column in range(2):
                    out_ref[
                        pl.ds(base + column * DEPTH * PAIRS, chips, stride=2 * SENT), :
                    ] = held_ref[pl.ds(first + column, chips, stride=2), :]
                left = held_ref[pl.ds(first - 1, chips, stride=2), :]
                right = held_ref[pl.ds(first + 2, chips, stride=2), :]
                out_ref[pl.ds(base + 2 * DEPTH * PAIRS, chips, stride=2 * SENT), :] = jnp.where(
                    upper_x, left, right
                )


def fill_table(counts_ref, table_ref, column):
    for entry in range(6):
        table_ref[entry, 1] = jnp.int32(0)
        table_ref[entry, ROWS] = jnp.int32(0)

    def body(owner, start):
        turn = start & (COLUMNS - 1)
        for entry, delta in enumerate((0, 1, -1, 2)):
            first = (column + delta - turn) & (COLUMNS - 1)
            row = (start + first - delta) >> 6
            slot = ((first + turn - delta) & (SLOTS - 1)) >> 6
            base = owner * (3 * DEPTH) + min(entry, 2) * DEPTH
            table_ref[entry, row + 1] = base + slot
            table_ref[entry, row + 2] = base + (1 - slot)
            if entry < 2:
                base = owner * (2 * DEPTH) + entry * DEPTH
                table_ref[4 + entry, row + 1] = base + slot
                table_ref[4 + entry, row + 2] = base + (1 - slot)
        return start + counts_ref[0, owner]

    lax.fori_loop(0, COLUMNS, body, jnp.int32(0), unroll=8)


def mask_kernel(where_am_i, *refs):
    counts_ref, links_ref, flat_ref, outer_ref, table_ref, lhs_ref, found_ref = refs[-7:]
    me = where_am_i(refs)
    chip, core = me >> 1, me & 1
    fill_table(counts_ref, table_ref, 2 * chip)
    blocks = ROWS // 2
    for v in range(blocks):
        lhs_ref[v * 8 : v * 8 + 6, :] = jnp.where(
            links_ref[0, :, v * 128 : (v + 1) * 128] >= 0, 1.0, 0.0
        )
        lhs_ref[v * 8 + 6 : v * 8 + 8, :] = jnp.zeros((2, 128), F32)
    source = iota((128, 256), 0)
    target = iota((128, 256), 1)
    x16 = target % WIDE
    lane = iota((ROWS, 128), 1)
    for column in range(2):
        wanted = 2 * chip + column + jnp.where(x16 < 4, -1, jnp.where(x16 >= 12, 1, 0))
        pick = (source % COLUMNS == wanted) & (source // COLUMNS == target // 128)
        found = jnp.dot(
            lhs_ref[...].astype(jnp.bfloat16),
            jnp.where(pick, 1.0, 0.0).astype(jnp.bfloat16),
            preferred_element_type=F32,
        )
        for v in range(blocks):
            for odd in range(2):
                found_ref[pl.ds(2 * v + odd, 8, stride=ROWS), :] = found[
                    v * 8 : v * 8 + 8, odd * 128 : (odd + 1) * 128
                ]
        edge = (lane % WIDE == 3) | (lane % WIDE == 11)
        flat_ref[column] = jnp.where(edge, found_ref[ROWS : 2 * ROWS, :], 1.0)
        flat_ref[2 + column] = jnp.where(lane >= 112, found_ref[3 * ROWS : 4 * ROWS, :], 1.0)
        outer_ref[column] = jnp.where(
            core == 0, found_ref[4 * ROWS : 5 * ROWS, :], found_ref[5 * ROWS : 6 * ROWS, :]
        )


def unpack_kernel(table_ref, received_ref, planes_ref, packed_ref):
    for r in range(ROWS):
        for entry in range(4):
            packed_ref[pl.ds(entry * PAIRS * ROWS + r, PAIRS, stride=ROWS), :] = received_ref[
                table_ref[entry, r + 1]
            ]
    lane = iota((ROWS, 128), 1)
    x16 = lane % WIDE
    for pair in range(PAIRS):
        first, second, left, right = (
            packed_ref[(entry * PAIRS + pair) * ROWS : (entry * PAIRS + pair + 1) * ROWS, :]
            for entry in range(4)
        )
        outside = jnp.where(lane % TILE >= HALF, left, right)

        def join(left, here, right):
            return jnp.where(x16 < 4, left, jnp.where(x16 >= 12, right, here))

        second_4 = shift(second, 4, 1)
        first_m4 = shift(first, -4, 1)
        planes_ref[pair] = join(shift(outside, -4, 1), shift(first, 4, 1), shift(second, 12, 1))
        planes_ref[PAIRS + pair] = join(shift(outside, -12, 1), first_m4, second_4)
        planes_ref[HALF + pair] = join(first_m4, second_4, shift(outside, 12, 1))
        planes_ref[HALF + PAIRS + pair] = join(
            shift(first, -12, 1), shift(second, -4, 1), shift(outside, 4, 1)
        )


EARLY_PLANES = TILE - 2


def stepper(load, keep, signs, links, lags, faces_ref):
    lane = iota((ROWS, 128), 1)
    first_y = lane < WIDE
    last_y = lane >= 128 - WIDE

    def one_step(step, column, lo, hi):
        level = load(step, column, lo - 1)
        after = load(step, column, lo)
        ahead_z = after - level
        if lo == HALF:
            ahead_z = ahead_z * faces_ref[column]
        for p in range(lo, hi):
            back_z = ahead_z
            level = after
            after = load(step, column, p + 1)
            ahead_z = after - level
            if p == HALF - 1:
                ahead_z = ahead_z * faces_ref[column]
            pull_ref, side_ref, at = signs(column, p)
            if step == 0:
                sign_field = level * lax.rsqrt(level * level + 1.0)
                pull = TIME_STEP * sign_field
                up = jnp.where(sign_field > 0, 1.0, -1.0)
                pull_ref[at] = pull
                side_ref[at] = up
            else:
                pull = pull_ref[at]
                up = side_ref[at]
            down = -up
            ahead = (shift(level, -1, 1) - level) * links(p)[column]
            back = (level - shift(level, 1, 1)) * lags(p, column)
            squares = jnp.square(jnp.maximum(jnp.maximum(up * back, down * ahead), 0.0))
            beyond = jnp.where(first_y, shift(level, -1, 0), level)
            ahead = (shift(beyond, -WIDE, 1) - level) * links(p)[2 + column]
            back = shift(jnp.where(last_y, shift(ahead, 1, 0), ahead), WIDE, 1)
            squares = squares + jnp.square(
                jnp.maximum(jnp.maximum(up * back, down * ahead), 0.0)
            )
            squares = squares + jnp.square(
                jnp.maximum(jnp.maximum(up * back_z, down * ahead_z), 0.0)
            )
            length = squares + EPSILON
            keep(step, column, p, level - pull * (length * lax.rsqrt(length) - 1.0))

    return one_step


def in_blocks(here, one_step, plan):
    def several(step, columns, lo, hi):
        for column in columns:
            one_step(step, column, lo, hi)

    for block, entry in enumerate(plan):
        pl.when(here > -1 - block)(functools.partial(several, *entry))


def early_at(column, p):
    return column * EARLY_PLANES + p - 1


def early_kernel(where_am_i, *refs):
    (
        outer_ref,
        own_ref,
        far_ref,
        near_ref,
        faces_ref,
        odd_ref,
        even_ref,
        pull_ref,
        side_ref,
        lag_ref,
    ) = refs[-10:]
    for column in range(2):
        lag_ref[column] = shift(far_ref[column], 1, 1)
        lag_ref[2 + column] = shift(near_ref[column], 1, 1)

    def load(step, column, p):
        if step == 0:
            base = column * HALF
            return outer_ref[base + HALF - 1 - p] if p < HALF else own_ref[base + p - HALF]
        return (odd_ref if step % 2 else even_ref)[early_at(column, p)]

    def keep(step, column, p, value):
        (even_ref if step % 2 else odd_ref)[early_at(column, p)] = value

    def signs(column, p):
        return pull_ref, side_ref, early_at(column, p)

    def links(p):
        return far_ref if p < HALF else near_ref

    def lags(p, column):
        return lag_ref[column if p < HALF else 2 + column]

    one_step = stepper(load, keep, signs, links, lags, faces_ref)
    plan = ((0, (0,), 1, 7), (0, (1,), 1, 7), (1, (0, 1), 2, 6), (2, (0, 1), 3, 5))
    in_blocks(where_am_i(refs), one_step, plan)


def late_kernel(where_am_i, *refs):
    (
        table_ref,
        inner_ref,
        own_ref,
        near_ref,
        faces_ref,
        early_odd_ref,
        early_even_ref,
        early_pull_ref,
        early_side_ref,
        out_ref,
        even_ref,
        odd_ref,
        pull_ref,
        side_ref,
        done_ref,
        lag_ref,
    ) = refs[-16:]
    for column in range(2):
        lag_ref[column] = shift(near_ref[column], 1, 1)

    def at(column, p):
        return column * TILE + p - HALF

    def load(step, column, p):
        if step == 0:
            base = column * HALF
            return own_ref[base + p - HALF] if p < TILE else inner_ref[base + 3 * HALF - 1 - p]
        if p <= EARLY_PLANES + 1 - step:
            return (early_odd_ref if step % 2 else early_even_ref)[early_at(column, p)]
        return (odd_ref if step % 2 else even_ref)[at(column, p)]

    def keep(step, column, p, value):
        (even_ref if step % 2 else odd_ref)[at(column, p)] = value

    def signs(column, p):
        if p <= EARLY_PLANES:
            return early_pull_ref, early_side_ref, early_at(column, p)
        return pull_ref, side_ref, at(column, p)

    one_step = stepper(
        load, keep, signs, lambda p: near_ref, lambda p, column: lag_ref[column], faces_ref
    )
    in_blocks(where_am_i(refs), one_step, [(s, (0, 1), 7 - s, 11 - s) for s in range(STEPS)])
    lower = iota((ROWS, 128), 1) % WIDE < TILE
    for column in range(2):
        for pair in range(PAIRS):
            p = at(column, HALF + pair)
            row = (column * PAIRS + pair) * ROWS
            done_ref[row : row + ROWS, :] = jnp.where(
                lower, shift(even_ref[p], -4, 1), shift(even_ref[p + PAIRS], 4, 1)
            )
    for r in range(ROWS):
        for column in range(2):
            out_ref[table_ref[4 + column, r + 1]] = done_ref[
                pl.ds(column * PAIRS * ROWS + r, PAIRS, stride=ROWS), :
            ]


def deliver_kernel(where_am_i, *refs):
    counts_ref, returned_ref, out_hbm, turned_ref, planes_ref, sems = refs[-6:]
    me = where_am_i(refs)
    counts = counts_ref[...]
    owner = iota((1, COLUMNS), 1)
    turn = jnp.sum(jnp.where(owner < me, counts, 0)) & (COLUMNS - 1)
    live = iota((SLOTS, SLOTS), 1) < jnp.sum(jnp.where(owner == me, counts, 0))
    chips = COLUMNS // 2
    sends = []
    for core in range(2):
        for pair in range(PAIRS):
            held_ref = turned_ref.at[core * PAIRS + pair]
            for d in range(DEPTH):
                for column in range(2):
                    row = core * BACK + (column * DEPTH + d) * PAIRS + pair
                    held_ref[pl.ds(d * COLUMNS + column, chips, stride=2), :] = returned_ref[
                        pl.ds(row, chips, stride=2 * BACK), :
                    ]
            turned = pltpu.roll(held_ref[...].T, (SLOTS - turn) & (SLOTS - 1), 1)
            turned = jnp.where(live, turned, 0.0)
            for y in range(TILE):
                for upper in range(2):
                    row = y * WIDE + upper * TILE
                    z = plane_of(core, pair, upper)
                    planes_ref[z, pl.ds(y, TILE, stride=TILE), :] = turned[row : row + TILE]
            for upper in range(2):
                z = plane_of(core, pair, upper)
                sends.append(pltpu.make_async_copy(planes_ref.at[z], out_hbm.at[:, z], sems.at[z]))
                sends[-1].start()
    for send in sends:
        send.wait()


def spec(space=pltpu.VMEM):
    return pl.BlockSpec(memory_space=space)


def run(
    kernel, operands, shapes, scratch, me=None, spaces=None, out_spaces=None, cost=(0, 0), grant=32
):
    spaces = spaces or [pltpu.VMEM] * len(operands)
    out_spaces = out_spaces or [pltpu.VMEM] * len(shapes)
    if me is not None:
        operands = (me, *operands)
        spaces = [pltpu.SMEM, *spaces]
    out = pl.pallas_call(
        kernel,
        out_shape=[
            (pltpu.SMEM if space == pltpu.SMEM else jax.ShapeDtypeStruct)(*shape)
            for shape, space in zip(shapes, out_spaces)
        ],
        in_specs=[spec(s) for s in spaces],
        out_specs=[spec(s) for s in out_spaces],
        scratch_shapes=scratch,
        compiler_params=pltpu.CompilerParams(vmem_limit_bytes=grant << 20),
        cost_estimate=pl.CostEstimate(flops=cost[0], bytes_accessed=cost[1], transcendentals=0),
        name=getattr(kernel, "func", kernel).__name__,
    )(*operands)
    return out


def position(refs):
    return lax.axis_index("mem")


def given(refs):
    return refs[0][0]


def bind(kernel, me):
    return functools.partial(kernel, position if me is None else given)


def pack(counts, phi, me=None):
    (out,) = run(
        bind(pack_kernel, me),
        (counts, phi.reshape(CELLS, SLOTS)),
        [((COLUMNS * SENT, 128), F32)],
        [
            pltpu.SMEM((1, COLUMNS), I32),
            pltpu.VMEM((CELLS, SLOTS), F32),
            pltpu.VMEM((2 * PAIRS, SLOTS + 16, 128), F32),
            pltpu.SemaphoreType.DMA((2,)),
        ],
        me,
        [pltpu.HBM, pltpu.HBM],
        grant=62,
    )
    return out.reshape(COLUMNS * SENT // 4, 4, 128)


def masks_of(counts, neighbours, me=None):
    return run(
        bind(mask_kernel, me),
        (counts, neighbours),
        [((4, ROWS, 128), F32), ((2, ROWS, 128), F32), ((6, TABLE), I32)],
        [pltpu.VMEM((128, 128), F32), pltpu.VMEM((8 * ROWS, 128), F32)],
        me,
        [pltpu.SMEM, pltpu.VMEM],
        [pltpu.VMEM, pltpu.VMEM, pltpu.SMEM],
        cost=(1 << 22, 1 << 17),
    )


def unpack(table, received):
    (out,) = run(
        unpack_kernel,
        (pltpu.with_memory_space_constraint(table, pltpu.SMEM), received.reshape(COLUMNS * SENT // PAIRS, PAIRS, 128)),
        [((TILE, ROWS, 128), F32)],
        [pltpu.VMEM((4 * PAIRS * ROWS, 128), F32)],
        None,
        [pltpu.SMEM, pltpu.VMEM],
    )
    return out


def start_march(outer, own, far, near, faces, me=None):
    return run(
        bind(early_kernel, me),
        (outer, own, far, near, faces),
        [((2 * EARLY_PLANES, ROWS, 128), F32)] * 4,
        [pltpu.VMEM((4, ROWS, 128), F32)],
        me,
        cost=(1 << 22, 1 << 20),
    )


def end_march(table, inner, own, near, faces, early, me=None):
    (out,) = run(
        bind(late_kernel, me),
        (
            pltpu.with_memory_space_constraint(table, pltpu.SMEM),
            inner,
            own,
            near,
            faces,
            *early,
        ),
        [((COLUMNS * BACK // PAIRS, PAIRS, 128), F32)],
        [pltpu.VMEM((2 * TILE, ROWS, 128), F32)] * 4
        + [pltpu.VMEM((2 * PAIRS * ROWS, 128), F32), pltpu.VMEM((2, ROWS, 128), F32)],
        me,
        [pltpu.SMEM] + [pltpu.VMEM] * 8,
    )
    return out.reshape(COLUMNS, BACK, 128)


def deliver(counts, returned, me=None):
    (out,) = run(
        bind(deliver_kernel, me),
        (counts, returned.reshape(COLUMNS * BACK, 128)),
        [((TILE * TILE, TILE, SLOTS), F32)],
        [
            pltpu.VMEM((2 * PAIRS, SLOTS, 128), F32),
            pltpu.VMEM((TILE, TILE * TILE, SLOTS), F32),
            pltpu.SemaphoreType.DMA((TILE,)),
        ],
        me,
        None,
        [pltpu.HBM],
    )
    return out.reshape(TILE, TILE, TILE, SLOTS)


def exchange(x):
    return lax.all_to_all(x, "mem", split_axis=0, concat_axis=0, tiled=True)


def on_device(phi_owned, band_counts, neighbours):
    groups, members = lax.axis_size("grp"), lax.axis_size("mem")
    mates = [(m, m ^ 1) for m in range(members)]
    across = []
    for g in range(groups - 1):
        for m in range(0, members, 2):
            low, high = g * members + m + 1, (g + 1) * members + m
            across += [(low, high), (high, low)]
    received = exchange(pack(band_counts, phi_owned))
    near, faces, table = masks_of(band_counts, neighbours)
    far = lax.ppermute(near, ("grp", "mem"), across)
    received, far = lax.optimization_barrier((received, far))
    own = unpack(table, received)
    outer = lax.ppermute(own, ("grp", "mem"), across)
    inner = lax.ppermute(own, "mem", mates)
    early = start_march(outer, own, far, near, faces)
    returned = exchange(end_march(table, inner, own, near, faces, early))
    return deliver(band_counts, returned)


def solution(mesh):
    return jax.shard_map(
        on_device,
        mesh=mesh,
        in_specs=(P(None, None, None, ("grp", "mem")), P("grp", None), P("grp", None, None)),
        out_specs=P(None, None, None, ("grp", "mem")),
        check_vma=False,
    )
```

```python
import functools

import jax
import jax.numpy as jnp
from jax import lax
from jax.experimental import pallas as pl
from jax.experimental.pallas import tpu as pltpu
from jax.sharding import PartitionSpec as P

STEPS = 4
TIME_STEP = 0.5
EPSILON = 1e-06

TILE = 8
ROWS = 32
COLUMNS = 64
SLOTS = 128
CELLS = TILE**3
DEPTH = SLOTS // COLUMNS
WIDE = 16
TABLE = 40
HALF = TILE // 2
PAIRS = HALF // 2
SENT = 3 * DEPTH * PAIRS
BACK = 2 * DEPTH * PAIRS

F32 = jnp.float32
I32 = jnp.int32


def shift(x, amount, axis):
    return pltpu.roll(x, amount % x.shape[axis] if isinstance(amount, int) else amount, axis)


def iota(shape, axis):
    return lax.broadcasted_iota(I32, shape, axis)


def own_start(counts_ref, me):
    total = jnp.int32(0)
    for owner in range(COLUMNS - 1):
        total = total + jnp.where(owner < me, counts_ref[0, owner], 0)
    return total


def plane_of(core, pair, upper):
    w = pair + PAIRS * upper
    return TILE - 1 - w if core else w


def pack_kernel(where_am_i, *refs):
    counts_hbm, phi_hbm, out_ref, counts_ref, phi_ref, turned_ref, sems = refs[-7:]
    copies = [
        pltpu.make_async_copy(counts_hbm, counts_ref, sems.at[0]),
        pltpu.make_async_copy(phi_hbm, phi_ref, sems.at[1]),
    ]
    for copy in copies:
        copy.start()
    copies[0].wait()
    turn = own_start(counts_ref, where_am_i(refs)) & (COLUMNS - 1)
    copies[1].wait()
    chips = COLUMNS // 2
    upper_x = iota((chips, 128), 1) % TILE >= HALF
    for core in range(2):
        for pair in range(PAIRS):
            blocks = []
            for y in range(TILE):
                for upper in range(2):
                    z = plane_of(core, pair, upper)
                    tiles = phi_ref[pl.ds(y * TILE + z, TILE, stride=TILE * TILE), :]
                    blocks.append(pltpu.roll(tiles, turn, 1))
            turned = jnp.concatenate(blocks, axis=0).T
            held_ref = turned_ref.at[core * PAIRS + pair]
            held_ref[8 : 8 + SLOTS, :] = turned
            held_ref[7:8, :] = turned[SLOTS - 1 :]
            held_ref[8 + SLOTS : 9 + SLOTS, :] = turned[:1]
            for d in range(DEPTH):
                first = 8 + d * COLUMNS
                base = core * SENT + d * PAIRS + pair
                for column in range(2):
                    out_ref[
                        pl.ds(base + column * DEPTH * PAIRS, chips, stride=2 * SENT), :
                    ] = held_ref[pl.ds(first + column, chips, stride=2), :]
                left = held_ref[pl.ds(first - 1, chips, stride=2), :]
                right = held_ref[pl.ds(first + 2, chips, stride=2), :]
                out_ref[pl.ds(base + 2 * DEPTH * PAIRS, chips, stride=2 * SENT), :] = jnp.where(
                    upper_x, left, right
                )


def fill_table(counts_ref, table_ref, column):
    for entry in range(6):
        table_ref[entry, 1] = jnp.int32(0)
        table_ref[entry, ROWS] = jnp.int32(0)

    def body(owner, start):
        turn = start & (COLUMNS - 1)
        for entry, delta in enumerate((0, 1, -1, 2)):
            first = (column + delta - turn) & (COLUMNS - 1)
            row = (start + first - delta) >> 6
            slot = ((first + turn - delta) & (SLOTS - 1)) >> 6
            base = owner * (3 * DEPTH) + min(entry, 2) * DEPTH
            table_ref[entry, row + 1] = base + slot
            table_ref[entry, row + 2] = base + (1 - slot)
            if entry < 2:
                base = owner * (2 * DEPTH) + entry * DEPTH
                table_ref[4 + entry, row + 1] = base + slot
                table_ref[4 + entry, row + 2] = base + (1 - slot)
        return start + counts_ref[0, owner]

    lax.fori_loop(0, COLUMNS, body, jnp.int32(0), unroll=8)


def mask_kernel(where_am_i, *refs):
    counts_ref, links_ref, flat_ref, outer_ref, table_ref, lhs_ref, found_ref = refs[-7:]
    me = where_am_i(refs)
    chip, core = me >> 1, me & 1
    fill_table(counts_ref, table_ref, 2 * chip)
    blocks = ROWS // 2
    for v in range(blocks):
        lhs_ref[v * 8 : v * 8 + 6, :] = jnp.where(
            links_ref[0, :, v * 128 : (v + 1) * 128] >= 0, 1.0, 0.0
        )
        lhs_ref[v * 8 + 6 : v * 8 + 8, :] = jnp.zeros((2, 128), F32)
    source = iota((128, 256), 0)
    target = iota((128, 256), 1)
    x16 = target % WIDE
    lane = iota((ROWS, 128), 1)
    for column in range(2):
        wanted = 2 * chip + column + jnp.where(x16 < 4, -1, jnp.where(x16 >= 12, 1, 0))
        pick = (source % COLUMNS == wanted) & (source // COLUMNS == target // 128)
        found = jnp.dot(
            lhs_ref[...].astype(jnp.bfloat16),
            jnp.where(pick, 1.0, 0.0).astype(jnp.bfloat16),
            preferred_element_type=F32,
        )
        for v in range(blocks):
            for odd in range(2):
                found_ref[pl.ds(2 * v + odd, 8, stride=ROWS), :] = found[
                    v * 8 : v * 8 + 8, odd * 128 : (odd + 1) * 128
                ]
        edge = (lane % WIDE == 3) | (lane % WIDE == 11)
        flat_ref[column] = jnp.where(edge, found_ref[ROWS : 2 * ROWS, :], 1.0)
        flat_ref[2 + column] = jnp.where(lane >= 112, found_ref[3 * ROWS : 4 * ROWS, :], 1.0)
        outer_ref[column] = jnp.where(
            core == 0, found_ref[4 * ROWS : 5 * ROWS, :], found_ref[5 * ROWS : 6 * ROWS, :]
        )


def unpack_kernel(table_ref, received_ref, packed_ref, sides_ref):
    span = PAIRS * ROWS
    for r in range(ROWS):
        for entry in range(4):
            rows_ref, first = (packed_ref, entry) if entry < 2 else (sides_ref, entry - 2)
            rows_ref[pl.ds(first * span + r, PAIRS, stride=ROWS), :] = received_ref[
                table_ref[entry, r + 1]
            ]
    upper_x = iota((span, 128), 1) % TILE >= HALF
    packed_ref[2 * span :, :] = jnp.where(upper_x, sides_ref[:span, :], sides_ref[span:, :])


def join_pairs(packed_ref, planes_ref):
    x16 = iota((ROWS, 128), 1) % WIDE

    def join(left, here, right):
        return jnp.where(x16 < 4, left, jnp.where(x16 >= 12, right, here))

    for pair in range(PAIRS):
        first, second, outside = (
            packed_ref[(entry * PAIRS + pair) * ROWS : (entry * PAIRS + pair + 1) * ROWS, :]
            for entry in range(3)
        )
        second_4 = shift(second, 4, 1)
        first_m4 = shift(first, -4, 1)
        planes_ref[pair] = join(shift(outside, -4, 1), shift(first, 4, 1), shift(second, 12, 1))
        planes_ref[PAIRS + pair] = join(shift(outside, -12, 1), first_m4, second_4)
        planes_ref[HALF + pair] = join(first_m4, second_4, shift(outside, 12, 1))
        planes_ref[HALF + PAIRS + pair] = join(
            shift(first, -12, 1), shift(second, -4, 1), shift(outside, 4, 1)
        )


EARLY_PLANES = TILE - 2


def stepper(load, keep, signs, links, faces_ref):
    lane = iota((ROWS, 128), 1)
    first_y = lane < WIDE
    last_y = lane >= 128 - WIDE

    def one_step(step, column, lo, hi):
        level = load(step, column, lo - 1)
        after = load(step, column, lo)
        ahead_z = after - level
        if lo == HALF:
            ahead_z = ahead_z * faces_ref[column]
        for p in range(lo, hi):
            back_z = ahead_z
            level = after
            after = load(step, column, p + 1)
            ahead_z = after - level
            if p == HALF - 1:
                ahead_z = ahead_z * faces_ref[column]
            pull_ref, side_ref, at = signs(column, p)
            if step == 0:
                sign_field = level * lax.rsqrt(level * level + 1.0)
                pull = TIME_STEP * sign_field
                up = jnp.where(sign_field > 0, 1.0, -1.0)
                pull_ref[at] = pull
                side_ref[at] = up
            else:
                pull = pull_ref[at]
                up = side_ref[at]
            down = -up
            ahead = (shift(level, -1, 1) - level) * links(p)[column]
            back = shift(ahead, 1, 1)
            squares = jnp.square(jnp.maximum(jnp.maximum(up * back, down * ahead), 0.0))
            beyond = jnp.where(first_y, shift(level, -1, 0), level)
            ahead = (shift(beyond, -WIDE, 1) - level) * links(p)[2 + column]
            back = shift(jnp.where(last_y, shift(ahead, 1, 0), ahead), WIDE, 1)
            squares = squares + jnp.square(
                jnp.maximum(jnp.maximum(up * back, down * ahead), 0.0)
            )
            squares = squares + jnp.square(
                jnp.maximum(jnp.maximum(up * back_z, down * ahead_z), 0.0)
            )
            length = squares + EPSILON
            keep(step, column, p, level - pull * (length * lax.rsqrt(length) - 1.0))

    return one_step


def in_blocks(here, one_step, plan):
    def several(step, columns, lo, hi):
        for column in columns:
            one_step(step, column, lo, hi)

    for block, entry in enumerate(plan):
        pl.when(here > -1 - block)(functools.partial(several, *entry))


def early_at(column, p):
    return column * EARLY_PLANES + p - 1


def early_kernel(where_am_i, *refs):
    (
        outer_packed_ref,
        own_ref,
        far_ref,
        near_ref,
        faces_ref,
        odd_ref,
        even_ref,
        pull_ref,
        side_ref,
        outer_ref,
    ) = refs[-10:]
    here = where_am_i(refs)
    pl.when(here > -65)(functools.partial(join_pairs, outer_packed_ref, outer_ref))

    def load(step, column, p):
        if step == 0:
            base = column * HALF
            return outer_ref[base + HALF - 1 - p] if p < HALF else own_ref[base + p - HALF]
        return (odd_ref if step % 2 else even_ref)[early_at(column, p)]

    def keep(step, column, p, value):
        (even_ref if step % 2 else odd_ref)[early_at(column, p)] = value

    def signs(column, p):
        return pull_ref, side_ref, early_at(column, p)

    one_step = stepper(load, keep, signs, lambda p: far_ref if p < HALF else near_ref, faces_ref)
    plan = ((0, (0,), 1, 7), (0, (1,), 1, 7), (1, (0, 1), 2, 6), (2, (0, 1), 3, 5))
    in_blocks(here, one_step, plan)


def late_kernel(where_am_i, *refs):
    (
        table_ref,
        inner_packed_ref,
        own_ref,
        near_ref,
        faces_ref,
        early_odd_ref,
        early_even_ref,
        early_pull_ref,
        early_side_ref,
        out_ref,
        even_ref,
        odd_ref,
        pull_ref,
        side_ref,
        done_ref,
        inner_ref,
    ) = refs[-16:]
    here = where_am_i(refs)
    pl.when(here > -65)(functools.partial(join_pairs, inner_packed_ref, inner_ref))

    def at(column, p):
        return column * TILE + p - HALF

    def load(step, column, p):
        if step == 0:
            base = column * HALF
            return own_ref[base + p - HALF] if p < TILE else inner_ref[base + 3 * HALF - 1 - p]
        if p <= EARLY_PLANES + 1 - step:
            return (early_odd_ref if step % 2 else early_even_ref)[early_at(column, p)]
        return (odd_ref if step % 2 else even_ref)[at(column, p)]

    def keep(step, column, p, value):
        (even_ref if step % 2 else odd_ref)[at(column, p)] = value

    def signs(column, p):
        if p <= EARLY_PLANES:
            return early_pull_ref, early_side_ref, early_at(column, p)
        return pull_ref, side_ref, at(column, p)

    one_step = stepper(load, keep, signs, lambda p: near_ref, faces_ref)
    in_blocks(here, one_step, [(s, (0, 1), 7 - s, 11 - s) for s in range(STEPS)])
    lower = iota((ROWS, 128), 1) % WIDE < TILE
    for column in range(2):
        for pair in range(PAIRS):
            p = at(column, HALF + pair)
            row = (column * PAIRS + pair) * ROWS
            done_ref[row : row + ROWS, :] = jnp.where(
                lower, shift(even_ref[p], -4, 1), shift(even_ref[p + PAIRS], 4, 1)
            )
    for r in range(ROWS):
        for column in range(2):
            out_ref[table_ref[4 + column, r + 1]] = done_ref[
                pl.ds(column * PAIRS * ROWS + r, PAIRS, stride=ROWS), :
            ]


def deliver_kernel(where_am_i, *refs):
    counts_ref, returned_ref, out_ref, turned_ref = refs[-4:]
    me = where_am_i(refs)
    counts = counts_ref[...]
    owner = iota((1, COLUMNS), 1)
    turn = jnp.sum(jnp.where(owner < me, counts, 0)) & (COLUMNS - 1)
    live = iota((SLOTS, SLOTS), 1) < jnp.sum(jnp.where(owner == me, counts, 0))
    chips = COLUMNS // 2
    for core in range(2):
        for pair in range(PAIRS):
            held_ref = turned_ref.at[core * PAIRS + pair]
            for d in range(DEPTH):
                for column in range(2):
                    row = core * BACK + (column * DEPTH + d) * PAIRS + pair
                    held_ref[pl.ds(d * COLUMNS + column, chips, stride=2), :] = returned_ref[
                        pl.ds(row, chips, stride=2 * BACK), :
                    ]
            turned = pltpu.roll(held_ref[...].T, (SLOTS - turn) & (SLOTS - 1), 1)
            turned = jnp.where(live, turned, 0.0)
            for y in range(TILE):
                for upper in range(2):
                    row = y * WIDE + upper * TILE
                    z = plane_of(core, pair, upper)
                    out_ref[pl.ds(y * TILE + z, TILE, stride=TILE * TILE), :] = turned[
                        row : row + TILE
                    ]


def spec(space=pltpu.VMEM):
    return pl.BlockSpec(memory_space=space)


def run(
    kernel, operands, shapes, scratch, me=None, spaces=None, out_spaces=None, cost=(0, 0), grant=32
):
    spaces = spaces or [pltpu.VMEM] * len(operands)
    out_spaces = out_spaces or [pltpu.VMEM] * len(shapes)
    if me is not None:
        operands = (me, *operands)
        spaces = [pltpu.SMEM, *spaces]
    out = pl.pallas_call(
        kernel,
        out_shape=[
            (pltpu.SMEM if space == pltpu.SMEM else jax.ShapeDtypeStruct)(*shape)
            for shape, space in zip(shapes, out_spaces)
        ],
        in_specs=[spec(s) for s in spaces],
        out_specs=[spec(s) for s in out_spaces],
        scratch_shapes=scratch,
        compiler_params=pltpu.CompilerParams(vmem_limit_bytes=grant << 20),
        cost_estimate=pl.CostEstimate(flops=cost[0], bytes_accessed=cost[1], transcendentals=0),
        name=getattr(kernel, "func", kernel).__name__,
    )(*operands)
    return out


def position(refs):
    return lax.axis_index("mem")


def given(refs):
    return refs[0][0]


def bind(kernel, me):
    return functools.partial(kernel, position if me is None else given)


def pack(counts, phi, me=None):
    (out,) = run(
        bind(pack_kernel, me),
        (counts, phi.reshape(CELLS, SLOTS)),
        [((COLUMNS * SENT, 128), F32)],
        [
            pltpu.SMEM((1, COLUMNS), I32),
            pltpu.VMEM((CELLS, SLOTS), F32),
            pltpu.VMEM((2 * PAIRS, SLOTS + 16, 128), F32),
            pltpu.SemaphoreType.DMA((2,)),
        ],
        me,
        [pltpu.HBM, pltpu.HBM],
        grant=62,
    )
    return out.reshape(COLUMNS * SENT // 4, 4, 128)


def masks_of(counts, neighbours, me=None):
    return run(
        bind(mask_kernel, me),
        (counts, neighbours),
        [((4, ROWS, 128), F32), ((2, ROWS, 128), F32), ((6, TABLE), I32)],
        [pltpu.VMEM((128, 128), F32), pltpu.VMEM((8 * ROWS, 128), F32)],
        me,
        [pltpu.SMEM, pltpu.VMEM],
        [pltpu.VMEM, pltpu.VMEM, pltpu.SMEM],
        cost=(1 << 22, 1 << 17),
    )


def unpack(table, received):
    (out,) = run(
        unpack_kernel,
        (pltpu.with_memory_space_constraint(table, pltpu.SMEM), received.reshape(COLUMNS * SENT // PAIRS, PAIRS, 128)),
        [((3 * PAIRS * ROWS, 128), F32)],
        [pltpu.VMEM((2 * PAIRS * ROWS, 128), F32)],
        None,
        [pltpu.SMEM, pltpu.VMEM],
    )
    return out


def joined(packed):
    return run(join_pairs, (packed,), [((TILE, ROWS, 128), F32)], [], cost=(1 << 20, 1 << 18))[0]


def start_march(outer, own, far, near, faces, me=None):
    return run(
        bind(early_kernel, me),
        (outer, own, far, near, faces),
        [((2 * EARLY_PLANES, ROWS, 128), F32)] * 4,
        [pltpu.VMEM((TILE, ROWS, 128), F32)],
        me,
        cost=(1 << 22, 1 << 20),
    )


def end_march(table, inner, own, near, faces, early, me=None):
    (out,) = run(
        bind(late_kernel, me),
        (
            pltpu.with_memory_space_constraint(table, pltpu.SMEM),
            inner,
            own,
            near,
            faces,
            *early,
        ),
        [((COLUMNS * BACK // PAIRS, PAIRS, 128), F32)],
        [pltpu.VMEM((2 * TILE, ROWS, 128), F32)] * 4
        + [pltpu.VMEM((2 * PAIRS * ROWS, 128), F32), pltpu.VMEM((TILE, ROWS, 128), F32)],
        me,
        [pltpu.SMEM] + [pltpu.VMEM] * 8,
    )
    return out.reshape(COLUMNS, BACK, 128)


def deliver(counts, returned, me=None):
    (out,) = run(
        bind(deliver_kernel, me),
        (counts, returned.reshape(COLUMNS * BACK, 128)),
        [((CELLS, SLOTS), F32)],
        [pltpu.VMEM((2 * PAIRS, SLOTS, 128), F32)],
        me,
    )
    return out.reshape(TILE, TILE, TILE, SLOTS)


def exchange(x):
    return lax.all_to_all(x, "mem", split_axis=0, concat_axis=0, tiled=True)


def on_device(phi_owned, band_counts, neighbours):
    groups, members = lax.axis_size("grp"), lax.axis_size("mem")
    mates = [(m, m ^ 1) for m in range(members)]
    across = []
    for g in range(groups - 1):
        for m in range(0, members, 2):
            low, high = g * members + m + 1, (g + 1) * members + m
            across += [(low, high), (high, low)]
    received = exchange(pack(band_counts, phi_owned))
    near, faces, table = masks_of(band_counts, neighbours)
    far = lax.ppermute(near, ("grp", "mem"), across)
    received, far = lax.optimization_barrier((received, far))
    packed = unpack(table, received)
    outer = lax.ppermute(packed, ("grp", "mem"), across)
    inner = lax.ppermute(packed, "mem", mates)
    own = joined(packed)
    early = start_march(outer, own, far, near, faces)
    returned = exchange(end_march(table, inner, own, near, faces, early))
    return deliver(band_counts, returned)


def solution(mesh):
    return jax.shard_map(
        on_device,
        mesh=mesh,
        in_specs=(P(None, None, None, ("grp", "mem")), P("grp", None), P("grp", None, None)),
        out_specs=P(None, None, None, ("grp", "mem")),
        check_vma=False,
    )
```

```python
import functools

import jax
import jax.numpy as jnp
from jax import lax
from jax.experimental import pallas as pl
from jax.experimental.pallas import tpu as pltpu
from jax.sharding import PartitionSpec as P

STEPS = 4
TIME_STEP = 0.5
EPSILON = 1e-06

TILE = 8
ROWS = 32
COLUMNS = 64
SLOTS = 128
CELLS = TILE**3
DEPTH = SLOTS // COLUMNS
WIDE = 16
TABLE = 40
HALF = TILE // 2
PAIRS = HALF // 2
SENT = 3 * DEPTH * PAIRS
BACK = 2 * DEPTH * PAIRS

F32 = jnp.float32
I32 = jnp.int32


def shift(x, amount, axis):
    return pltpu.roll(x, amount % x.shape[axis] if isinstance(amount, int) else amount, axis)


def iota(shape, axis):
    return lax.broadcasted_iota(I32, shape, axis)


def own_start(counts_ref, me):
    total = jnp.int32(0)
    for owner in range(COLUMNS - 1):
        total = total + jnp.where(owner < me, counts_ref[0, owner], 0)
    return total


def plane_of(core, pair, upper):
    w = pair + PAIRS * upper
    return TILE - 1 - w if core else w


def pack_kernel(where_am_i, *refs):
    counts_hbm, phi_hbm, out_ref, counts_ref, phi_ref, turned_ref, sems = refs[-7:]
    copies = [
        pltpu.make_async_copy(counts_hbm, counts_ref, sems.at[0]),
        pltpu.make_async_copy(phi_hbm, phi_ref, sems.at[1]),
    ]
    for copy in copies:
        copy.start()
    copies[0].wait()
    turn = own_start(counts_ref, where_am_i(refs)) & (COLUMNS - 1)
    copies[1].wait()
    chips = COLUMNS // 2
    upper_x = iota((chips, 128), 1) % TILE >= HALF
    for core in range(2):
        for pair in range(PAIRS):
            blocks = []
            for y in range(TILE):
                for upper in range(2):
                    z = plane_of(core, pair, upper)
                    tiles = phi_ref[pl.ds(y * TILE + z, TILE, stride=TILE * TILE), :]
                    blocks.append(pltpu.roll(tiles, turn, 1))
            turned = jnp.concatenate(blocks, axis=0).T
            held_ref = turned_ref.at[core * PAIRS + pair]
            held_ref[8 : 8 + SLOTS, :] = turned
            held_ref[7:8, :] = turned[SLOTS - 1 :]
            held_ref[8 + SLOTS : 9 + SLOTS, :] = turned[:1]
            for d in range(DEPTH):
                first = 8 + d * COLUMNS
                base = core * SENT + d * PAIRS + pair
                for column in range(2):
                    out_ref[
                        pl.ds(base + column * DEPTH * PAIRS, chips, stride=2 * SENT), :
                    ] = held_ref[pl.ds(first + column, chips, stride=2), :]
                left = held_ref[pl.ds(first - 1, chips, stride=2), :]
                right = held_ref[pl.ds(first + 2, chips, stride=2), :]
                out_ref[pl.ds(base + 2 * DEPTH * PAIRS, chips, stride=2 * SENT), :] = jnp.where(
                    upper_x, left, right
                )


def fill_table(counts_ref, table_ref, column):
    for entry in range(6):
        table_ref[entry, 1] = jnp.int32(0)
        table_ref[entry, ROWS] = jnp.int32(0)

    def body(owner, start):
        turn = start & (COLUMNS - 1)
        for entry, delta in enumerate((0, 1, -1, 2)):
            first = (column + delta - turn) & (COLUMNS - 1)
            row = (start + first - delta) >> 6
            slot = ((first + turn - delta) & (SLOTS - 1)) >> 6
            base = owner * (3 * DEPTH) + min(entry, 2) * DEPTH
            table_ref[entry, row + 1] = base + slot
            table_ref[entry, row + 2] = base + (1 - slot)
            if entry < 2:
                base = owner * (2 * DEPTH) + entry * DEPTH
                table_ref[4 + entry, row + 1] = base + slot
                table_ref[4 + entry, row + 2] = base + (1 - slot)
        return start + counts_ref[0, owner]

    lax.fori_loop(0, COLUMNS, body, jnp.int32(0), unroll=8)


def mask_kernel(where_am_i, *refs):
    counts_ref, links_ref, flat_ref, outer_ref, table_ref, lhs_ref, found_ref = refs[-7:]
    me = where_am_i(refs)
    chip, core = me >> 1, me & 1
    fill_table(counts_ref, table_ref, 2 * chip)
    blocks = ROWS // 2
    for v in range(blocks):
        lhs_ref[v * 8 : v * 8 + 6, :] = jnp.where(
            links_ref[0, :, v * 128 : (v + 1) * 128] >= 0, 1.0, 0.0
        )
        lhs_ref[v * 8 + 6 : v * 8 + 8, :] = jnp.zeros((2, 128), F32)
    source = iota((128, 256), 0)
    target = iota((128, 256), 1)
    x16 = target % WIDE
    lane = iota((ROWS, 128), 1)
    for column in range(2):
        wanted = 2 * chip + column + jnp.where(x16 < 4, -1, jnp.where(x16 >= 12, 1, 0))
        pick = (source % COLUMNS == wanted) & (source // COLUMNS == target // 128)
        found = jnp.dot(
            lhs_ref[...].astype(jnp.bfloat16),
            jnp.where(pick, 1.0, 0.0).astype(jnp.bfloat16),
            preferred_element_type=F32,
        )
        for v in range(blocks):
            for odd in range(2):
                found_ref[pl.ds(2 * v + odd, 8, stride=ROWS), :] = found[
                    v * 8 : v * 8 + 8, odd * 128 : (odd + 1) * 128
                ]
        edge = (lane % WIDE == 3) | (lane % WIDE == 11)
        flat_ref[column] = jnp.where(edge, found_ref[ROWS : 2 * ROWS, :], 1.0)
        flat_ref[2 + column] = jnp.where(lane >= 112, found_ref[3 * ROWS : 4 * ROWS, :], 1.0)
        outer_ref[column] = jnp.where(
            core == 0, found_ref[4 * ROWS : 5 * ROWS, :], found_ref[5 * ROWS : 6 * ROWS, :]
        )


def unpack_kernel(table_ref, received_ref, planes_ref, packed_ref):
    for r in range(ROWS):
        for entry in range(4):
            packed_ref[pl.ds(entry * PAIRS * ROWS + r, PAIRS, stride=ROWS), :] = received_ref[
                table_ref[entry, r + 1]
            ]
    lane = iota((ROWS, 128), 1)
    x16 = lane % WIDE
    for pair in range(PAIRS):
        first, second, left, right = (
            packed_ref[(entry * PAIRS + pair) * ROWS : (entry * PAIRS + pair + 1) * ROWS, :]
            for entry in range(4)
        )
        outside = jnp.where(lane % TILE >= HALF, left, right)

        def join(left, here, right):
            return jnp.where(x16 < 4, left, jnp.where(x16 >= 12, right, here))

        second_4 = shift(second, 4, 1)
        first_m4 = shift(first, -4, 1)
        planes_ref[pair] = join(shift(outside, -4, 1), shift(first, 4, 1), shift(second, 12, 1))
        planes_ref[PAIRS + pair] = join(shift(outside, -12, 1), first_m4, second_4)
        planes_ref[HALF + pair] = join(first_m4, second_4, shift(outside, 12, 1))
        planes_ref[HALF + PAIRS + pair] = join(
            shift(first, -12, 1), shift(second, -4, 1), shift(outside, 4, 1)
        )


EARLY_PLANES = TILE - 2


def stepper(load, keep, signs, links, faces_ref):
    lane = iota((ROWS, 128), 1)
    first_y = lane < WIDE
    last_y = lane >= 128 - WIDE

    def one_step(step, column, lo, hi):
        level = load(step, column, lo - 1)
        after = load(step, column, lo)
        ahead_z = after - level
        if lo == HALF:
            ahead_z = ahead_z * faces_ref[column]
        for p in range(lo, hi):
            back_z = ahead_z
            level = after
            after = load(step, column, p + 1)
            ahead_z = after - level
            if p == HALF - 1:
                ahead_z = ahead_z * faces_ref[column]
            pull_ref, side_ref, at = signs(column, p)
            if step == 0:
                sign_field = level * lax.rsqrt(level * level + 1.0)
                pull = TIME_STEP * sign_field
                up = jnp.where(sign_field > 0, 1.0, -1.0)
                pull_ref[at] = pull
                side_ref[at] = up
            else:
                pull = pull_ref[at]
                up = side_ref[at]
            down = -up
            ahead = (shift(level, -1, 1) - level) * links(p)[column]
            back = shift(ahead, 1, 1)
            squares = jnp.square(jnp.maximum(jnp.maximum(up * back, down * ahead), 0.0))
            beyond = jnp.where(first_y, shift(level, -1, 0), level)
            ahead = (shift(beyond, -WIDE, 1) - level) * links(p)[2 + column]
            back = shift(jnp.where(last_y, shift(ahead, 1, 0), ahead), WIDE, 1)
            squares = squares + jnp.square(
                jnp.maximum(jnp.maximum(up * back, down * ahead), 0.0)
            )
            squares = squares + jnp.square(
                jnp.maximum(jnp.maximum(up * back_z, down * ahead_z), 0.0)
            )
            length = squares + EPSILON
            keep(step, column, p, level - pull * (length * lax.rsqrt(length) - 1.0))

    return one_step


def in_blocks(here, one_step, plan):
    def several(step, columns, lo, hi):
        for column in columns:
            one_step(step, column, lo, hi)

    for block, entry in enumerate(plan):
        pl.when(here > -1 - block)(functools.partial(several, *entry))


def early_at(column, p):
    return column * EARLY_PLANES + p - 1


def early_kernel(where_am_i, *refs):
    outer_ref, own_ref, far_ref, near_ref, faces_ref, odd_ref, even_ref, pull_ref, side_ref = refs[-9:]

    def load(step, column, p):
        if step == 0:
            base = column * HALF
            return outer_ref[base + HALF - 1 - p] if p < HALF else own_ref[base + p - HALF]
        return (odd_ref if step % 2 else even_ref)[early_at(column, p)]

    def keep(step, column, p, value):
        (even_ref if step % 2 else odd_ref)[early_at(column, p)] = value

    def signs(column, p):
        return pull_ref, side_ref, early_at(column, p)

    one_step = stepper(load, keep, signs, lambda p: far_ref if p < HALF else near_ref, faces_ref)
    plan = ((0, (0,), 1, 7), (0, (1,), 1, 7), (1, (0, 1), 2, 6), (2, (0, 1), 3, 5))
    in_blocks(where_am_i(refs), one_step, plan)


def late_kernel(where_am_i, *refs):
    (
        table_ref,
        inner_ref,
        own_ref,
        near_ref,
        faces_ref,
        early_odd_ref,
        early_even_ref,
        early_pull_ref,
        early_side_ref,
        out_ref,
        even_ref,
        odd_ref,
        pull_ref,
        side_ref,
        done_ref,
    ) = refs[-15:]

    def at(column, p):
        return column * TILE + p - HALF

    def load(step, column, p):
        if step == 0:
            base = column * HALF
            return own_ref[base + p - HALF] if p < TILE else inner_ref[base + 3 * HALF - 1 - p]
        if p <= EARLY_PLANES + 1 - step:
            return (early_odd_ref if step % 2 else early_even_ref)[early_at(column, p)]
        return (odd_ref if step % 2 else even_ref)[at(column, p)]

    def keep(step, column, p, value):
        (even_ref if step % 2 else odd_ref)[at(column, p)] = value

    def signs(column, p):
        if p <= EARLY_PLANES:
            return early_pull_ref, early_side_ref, early_at(column, p)
        return pull_ref, side_ref, at(column, p)

    one_step = stepper(load, keep, signs, lambda p: near_ref, faces_ref)
    in_blocks(where_am_i(refs), one_step, [(s, (0, 1), 7 - s, 11 - s) for s in range(STEPS)])
    lower = iota((ROWS, 128), 1) % WIDE < TILE
    for column in range(2):
        for pair in range(PAIRS):
            p = at(column, HALF + pair)
            row = (column * PAIRS + pair) * ROWS
            done_ref[row : row + ROWS, :] = jnp.where(
                lower, shift(even_ref[p], -4, 1), shift(even_ref[p + PAIRS], 4, 1)
            )
    for r in range(ROWS):
        for column in range(2):
            out_ref[table_ref[4 + column, r + 1]] = done_ref[
                pl.ds(column * PAIRS * ROWS + r, PAIRS, stride=ROWS), :
            ]


def deliver_kernel(where_am_i, *refs):
    counts_ref, returned_ref, out_hbm, turned_ref, planes_ref, sems = refs[-6:]
    me = where_am_i(refs)
    counts = counts_ref[...]
    owner = iota((1, COLUMNS), 1)
    turn = jnp.sum(jnp.where(owner < me, counts, 0)) & (COLUMNS - 1)
    live = iota((SLOTS, SLOTS), 1) < jnp.sum(jnp.where(owner == me, counts, 0))
    chips = COLUMNS // 2
    sends = []
    for core in range(2):
        for pair in range(PAIRS):
            held_ref = turned_ref.at[core * PAIRS + pair]
            for d in range(DEPTH):
                for column in range(2):
                    row = core * BACK + (column * DEPTH + d) * PAIRS + pair
                    held_ref[pl.ds(d * COLUMNS + column, chips, stride=2), :] = returned_ref[
                        pl.ds(row, chips, stride=2 * BACK), :
                    ]
            turned = pltpu.roll(held_ref[...].T, (SLOTS - turn) & (SLOTS - 1), 1)
            turned = jnp.where(live, turned, 0.0)
            for y in range(TILE):
                for upper in range(2):
                    row = y * WIDE + upper * TILE
                    z = plane_of(core, pair, upper)
                    planes_ref[z, pl.ds(y, TILE, stride=TILE), :] = turned[row : row + TILE]
            for upper in range(2):
                z = plane_of(core, pair, upper)
                sends.append(pltpu.make_async_copy(planes_ref.at[z], out_hbm.at[:, z], sems.at[z]))
                sends[-1].start()
    for send in sends:
        send.wait()


def spec(space=pltpu.VMEM):
    return pl.BlockSpec(memory_space=space)


def run(
    kernel, operands, shapes, scratch, me=None, spaces=None, out_spaces=None, cost=(0, 0), grant=32
):
    spaces = spaces or [pltpu.VMEM] * len(operands)
    out_spaces = out_spaces or [pltpu.VMEM] * len(shapes)
    if me is not None:
        operands = (me, *operands)
        spaces = [pltpu.SMEM, *spaces]
    out = pl.pallas_call(
        kernel,
        out_shape=[
            (pltpu.SMEM if space == pltpu.SMEM else jax.ShapeDtypeStruct)(*shape)
            for shape, space in zip(shapes, out_spaces)
        ],
        in_specs=[spec(s) for s in spaces],
        out_specs=[spec(s) for s in out_spaces],
        scratch_shapes=scratch,
        compiler_params=pltpu.CompilerParams(vmem_limit_bytes=grant << 20),
        cost_estimate=pl.CostEstimate(flops=cost[0], bytes_accessed=cost[1], transcendentals=0),
        name=getattr(kernel, "func", kernel).__name__,
    )(*operands)
    return out


def position(refs):
    return lax.axis_index("mem")


def given(refs):
    return refs[0][0]


def bind(kernel, me):
    return functools.partial(kernel, position if me is None else given)


def pack(counts, phi, me=None):
    (out,) = run(
        bind(pack_kernel, me),
        (counts, phi.reshape(CELLS, SLOTS)),
        [((COLUMNS * SENT, 128), F32)],
        [
            pltpu.SMEM((1, COLUMNS), I32),
            pltpu.VMEM((CELLS, SLOTS), F32),
            pltpu.VMEM((2 * PAIRS, SLOTS + 16, 128), F32),
            pltpu.SemaphoreType.DMA((2,)),
        ],
        me,
        [pltpu.HBM, pltpu.HBM],
        grant=62,
    )
    return out.reshape(COLUMNS * SENT // 4, 4, 128)


def masks_of(counts, neighbours, me=None):
    return run(
        bind(mask_kernel, me),
        (counts, neighbours),
        [((4, ROWS, 128), F32), ((2, ROWS, 128), F32), ((6, TABLE), I32)],
        [pltpu.VMEM((128, 128), F32), pltpu.VMEM((8 * ROWS, 128), F32)],
        me,
        [pltpu.SMEM, pltpu.VMEM],
        [pltpu.VMEM, pltpu.VMEM, pltpu.SMEM],
        cost=(1 << 22, 1 << 17),
    )


def unpack(table, received):
    (out,) = run(
        unpack_kernel,
        (pltpu.with_memory_space_constraint(table, pltpu.SMEM), received.reshape(COLUMNS * SENT // PAIRS, PAIRS, 128)),
        [((TILE, ROWS, 128), F32)],
        [pltpu.VMEM((4 * PAIRS * ROWS, 128), F32)],
        None,
        [pltpu.SMEM, pltpu.VMEM],
    )
    return out


def start_march(outer, own, far, near, faces, me=None):
    return run(
        bind(early_kernel, me),
        (outer, own, far, near, faces),
        [((2 * EARLY_PLANES, ROWS, 128), F32)] * 4,
        [],
        me,
        cost=(1 << 22, 1 << 20),
    )


def end_march(table, inner, own, near, faces, early, me=None):
    (out,) = run(
        bind(late_kernel, me),
        (
            pltpu.with_memory_space_constraint(table, pltpu.SMEM),
            inner,
            own,
            near,
            faces,
            *early,
        ),
        [((COLUMNS * BACK // PAIRS, PAIRS, 128), F32)],
        [pltpu.VMEM((2 * TILE, ROWS, 128), F32)] * 4
        + [pltpu.VMEM((2 * PAIRS * ROWS, 128), F32)],
        me,
        [pltpu.SMEM] + [pltpu.VMEM] * 8,
    )
    return out.reshape(COLUMNS, BACK, 128)


def deliver(counts, returned, me=None):
    (out,) = run(
        bind(deliver_kernel, me),
        (counts, returned.reshape(COLUMNS * BACK, 128)),
        [((TILE * TILE, TILE, SLOTS), F32)],
        [
            pltpu.VMEM((2 * PAIRS, SLOTS, 128), F32),
            pltpu.VMEM((TILE, TILE * TILE, SLOTS), F32),
            pltpu.SemaphoreType.DMA((TILE,)),
        ],
        me,
        None,
        [pltpu.HBM],
    )
    return out.reshape(TILE, TILE, TILE, SLOTS)


def exchange(x):
    return lax.all_to_all(x, "mem", split_axis=0, concat_axis=0, tiled=True)


def on_device(phi_owned, band_counts, neighbours):
    groups, members = lax.axis_size("grp"), lax.axis_size("mem")
    mates = [(m, m ^ 1) for m in range(members)]
    across = []
    for g in range(groups - 1):
        for m in range(0, members, 2):
            low, high = g * members + m + 1, (g + 1) * members + m
            across += [(low, high), (high, low)]
    received = exchange(pack(band_counts, phi_owned))
    near, faces, table = masks_of(band_counts, neighbours)
    far = lax.ppermute(near, ("grp", "mem"), across)
    received, far = lax.optimization_barrier((received, far))
    own = unpack(table, received)
    outer = lax.ppermute(own, ("grp", "mem"), across)
    inner = lax.ppermute(own, "mem", mates)
    early = start_march(outer, own, far, near, faces)
    returned = exchange(end_march(table, inner, own, near, faces, early))
    return deliver(band_counts, returned)


def solution(mesh):
    return jax.shard_map(
        on_device,
        mesh=mesh,
        in_specs=(P(None, None, None, ("grp", "mem")), P("grp", None), P("grp", None, None)),
        out_specs=P(None, None, None, ("grp", "mem")),
        check_vma=False,
    )
```
